32 devices in a mesh: rep: 16 (over z, x, core), shard: 2 (over y).
Axes of the slice: x: 2, y: 2, z: 4, core: 2. Of those that a mesh axis runs over, the one named last changes fastest.
Arguments:
- hidden_in: bfloat16 [4096, 1024], P(('rep', 'shard')), may hold values from -6 to 6
- cotangent: bfloat16 [4096, 1024], P(('rep', 'shard')), may hold values from -6 to 6
- norm_gain: float32 [1, 1024], P(None, 'shard'), may hold values from 0.5 to 1.5
- w_z: bfloat16 [1, 1024, 2048], P(None, None, 'shard'), may hold values from -0.1875 to 0.1875
- w_x: bfloat16 [1, 1024, 2048], P(None, None, 'shard'), may hold values from -0.1875 to 0.1875
- w_bc: bfloat16 [1, 1024, 256], P(None, None, 'shard'), may hold values from -0.1875 to 0.1875
- w_dt: bfloat16 [1, 1024, 32], P(None, None, 'shard'), may hold values from -0.1875 to 0.1875
- conv_x: float32 [1, 4, 2048], P(None, None, 'shard'), may hold values from -3 to 3
- conv_bc: float32 [1, 4, 256], P(None, None, 'shard'), may hold values from -3 to 3
- bias_x: float32 [1, 2048], P(None, 'shard'), may hold values from -1.75 to 1.75
- bias_bc: float32 [1, 256], P(None, 'shard'), may hold values from -1.75 to 1.75
- dt_bias: float32 [1, 32], P(None, 'shard'), may hold values from -5 to -2
- a_log: float32 [1, 32], P(None, 'shard'), may hold values from 0 to 2.77
- d_skip: float32 [1, 32], P(None, 'shard'), may hold values from 0.5 to 1.5
- gate_gain: float32 [1, 2048], P(None, 'shard'), may hold values from 0.5 to 1.5
- w_out: bfloat16 [1, 2048, 1024], P(None, 'shard'), may hold values from -0.125 to 0.125
- seq_len: int32 [256], replicated, may hold values from 0 to 128, as said below
- seq_owner: int32 [256], replicated, may hold values from 0 to 31, as said below
- seq_start: int32 [256], replicated, may hold values from 0 to 128, as said below
Outputs:
- hidden_out: float32 [4096, 1024], P(('rep', 'shard'))
- grad_hidden: float32 [4096, 1024], P(('rep', 'shard'))
- grad_norm_gain: float32 [1, 1024], P(None, 'shard')
- grad_w_z: float32 [1, 1024, 2048], P(None, None, 'shard')
- grad_w_x: float32 [1, 1024, 2048], P(None, None, 'shard')
- grad_w_bc: float32 [1, 1024, 256], P(None, None, 'shard')
- grad_w_dt: float32 [1, 1024, 32], P(None, None, 'shard')
- grad_conv_x: float32 [1, 4, 2048], P(None, None, 'shard')
- grad_conv_bc: float32 [1, 4, 256], P(None, None, 'shard')
- grad_bias_x: float32 [1, 2048], P(None, 'shard')
- grad_bias_bc: float32 [1, 256], P(None, 'shard')
- grad_dt_bias: float32 [1, 32], P(None, 'shard')
- grad_a_log: float32 [1, 32], P(None, 'shard')
- grad_d_skip: float32 [1, 32], P(None, 'shard')
- grad_gate_gain: float32 [1, 2048], P(None, 'shard')
- grad_w_out: float32 [1, 2048, 1024], P(None, 'shard')
The draws below stay inside these ranges and needn't reach their ends.
Inputs may be any that keep to these rules, and one draw needn't show every extreme that they name: `seq_len`: the records come in groups of 8 in a row; each group belongs to exactly one device, and every device has one group. A group's sequences lie back to back from its device's first slot in record order, never past its last slot; some records are empty. `seq_owner`: all records of a group name the same device. `seq_start`: A record starts where the previous record of its group ends, the first at slot 0; an empty record may start at slot 128.
All inputs are finite; a program needn't handle non-finite values.
Results may differ from the reference program's by a relative error of at most 0.04.
Values may be sent and summed in bfloat16 or wider, within the bound.
No kernel may reach another device: no remote copies, remote signals or barrier semaphores. Data moves between devices by JAX's collectives and lax.ppermute only.
A program may use at most 128 MiB of HBM per device.

```python
from functools import partial
import jax
import jax.numpy as jnp
from jax import lax

D = 1024
HEADS = 32
STATE = 128
CONV = 4
BLOCK = 64
LAYERS = 1
REC_DEV = 8
TOK_DEV = 128
INNER = 2048
TOKENS = 4096
SEQS = 256


def record_layout(key):
    device_total = SEQS // REC_DEV
    base_key = jax.random.fold_in(key, 11)
    key_level, key_cut, key_order, key_full = jax.random.split(base_key, 4)
    levels = jax.random.randint(key_level, (device_total,), 0, 4)
    device_load = jnp.right_shift(jnp.full((device_total,), TOK_DEV, jnp.int32), levels)
    full_device = jax.random.randint(key_full, (), 0, device_total).astype(jnp.int32)
    device_ids = jnp.arange(device_total, dtype=jnp.int32)
    is_full = device_ids == full_device
    device_load = jnp.where(is_full, TOK_DEV, device_load).astype(jnp.int32)
    cut_points = jax.random.randint(key_cut, (device_total, REC_DEV - 1), 0, device_load[:, None] + 1)
    cut_points = jnp.sort(cut_points, axis=1)
    cut_points = jnp.where(is_full[:, None], TOK_DEV, cut_points).astype(jnp.int32)
    zero_cut = jnp.zeros((device_total, 1), jnp.int32)
    start_cut = jnp.concatenate([zero_cut, cut_points], axis=1)
    end_cut = jnp.concatenate([cut_points, device_load[:, None]], axis=1)
    chosen = jax.random.permutation(key_order, device_total).astype(jnp.int32)
    lengths = (end_cut - start_cut)[chosen].reshape(-1).astype(jnp.int32)
    offsets = start_cut[chosen].reshape(-1).astype(jnp.int32)
    owners = jnp.repeat(chosen, REC_DEV).astype(jnp.int32)
    return (lengths, owners, offsets)


def draw_seq_len(key, part):
    return record_layout(key)[0]


def draw_seq_owner(key, part):
    return record_layout(key)[1]


def draw_seq_start(key, part):
    return record_layout(key)[2]


def block_levels(stream_key, extent, shards, smallest, top_value):
    gain, own = 1.0, jax.random.fold_in(stream_key, 6)
    for axis_at, blocks in shards:
        draws = jnp.exp(jax.random.uniform(jax.random.fold_in(own, axis_at), (blocks,), jnp.float32, smallest / len(shards), top_value / len(shards)))
        gain = gain * jnp.repeat(draws, extent[axis_at] // blocks).reshape([-1 if axis == axis_at else 1 for axis in range(len(extent))])
    return gain


def noise(key, dims, spread, most, cuts=(), kind=jnp.bfloat16):
    values = jax.random.normal(key, dims, jnp.float32) * spread
    if len(cuts) > 0:
        values = block_levels(key, dims, cuts, -0.22, 0.18) * values
    return jnp.clip(values, min=-most, max=most).astype(kind)


def setup_inputs(seed: int = 0) -> dict:
    keys = jax.random.split(jax.random.key(seed), 20)
    return {
        "hidden_in": noise(keys[0], (TOKENS, D), 1.0, 6.0, ((0, 32),)),
        "cotangent": noise(keys[1], (TOKENS, D), 1.0, 6.0, ((0, 32),)),
        "norm_gain": jnp.clip(1.0 + 0.1 * jax.random.normal(keys[2], (LAYERS, D), jnp.float32), 0.5, 1.5),
        "w_z": noise(keys[3], (LAYERS, D, INNER), D ** -0.5, 0.1875, ((2, 2),)),
        "w_x": noise(keys[4], (LAYERS, D, INNER), D ** -0.5, 0.1875, ((2, 2),)),
        "w_bc": noise(keys[5], (LAYERS, D, 2 * STATE), D ** -0.5, 0.1875, ((2, 2),)),
        "w_dt": noise(keys[6], (LAYERS, D, HEADS), D ** -0.5, 0.1875, ((2, 2),)),
        "conv_x": noise(keys[7], (LAYERS, CONV, INNER), CONV ** -0.5, 3.0, ((2, 2),), jnp.float32),
        "conv_bc": noise(keys[8], (LAYERS, CONV, 2 * STATE), CONV ** -0.5, 3.0, ((2, 2),), jnp.float32),
        "bias_x": noise(keys[9], (LAYERS, INNER), 0.3, 1.75, ((1, 2),), jnp.float32),
        "bias_bc": noise(keys[10], (LAYERS, 2 * STATE), 0.3, 1.75, ((1, 2),), jnp.float32),
        "dt_bias": jnp.clip(-5.0 + 3.0 * jax.random.uniform(keys[11], (LAYERS, HEADS), jnp.float32) ** block_levels(keys[11], (LAYERS, HEADS), ((1, 2),), -0.2, 0.2), -5.0, -2.0),
        "a_log": jnp.clip(2.77 * jax.random.uniform(keys[12], (LAYERS, HEADS), jnp.float32) ** block_levels(keys[12], (LAYERS, HEADS), ((1, 2),), -0.2, 0.2), 0.0, 2.77),
        "d_skip": jnp.clip(0.5 + 1.0 * jax.random.uniform(keys[13], (LAYERS, HEADS), jnp.float32) ** block_levels(keys[13], (LAYERS, HEADS), ((1, 2),), -0.2, 0.2), 0.5, 1.5),
        "gate_gain": jnp.clip(1.0 + 0.1 * jax.random.normal(keys[14], (LAYERS, INNER), jnp.float32), 0.5, 1.5),
        "w_out": noise(keys[15], (LAYERS, INNER, D), INNER ** -0.5, 0.125, ((1, 2),)),
        "seq_len": draw_seq_len(jax.random.fold_in(keys[19], 71), 0),
        "seq_owner": draw_seq_owner(jax.random.fold_in(keys[19], 71), 0),
        "seq_start": draw_seq_start(jax.random.fold_in(keys[19], 71), 0),
    }


epsilon = 1e-05
HIGHEST = lax.Precision.HIGHEST

def slot_segments(seq_len, seq_owner, seq_start, device, row_count):
    slot_ids = jnp.arange(row_count, dtype=jnp.int32)
    record_ids = jnp.arange(seq_len.shape[0], dtype=jnp.int32)
    covers = (seq_owner[:, None] == device) & (slot_ids[None, :] >= seq_start[:, None]) & (slot_ids[None, :] < seq_start[:, None] + seq_len[:, None])
    in_use = lax.optimization_barrier(jnp.sum(covers.astype(jnp.int32), axis=0)).astype(jnp.int32)
    covering = lax.optimization_barrier(jnp.sum(jnp.where(covers, record_ids[:, None], 0), axis=0)).astype(jnp.int32)
    lone_ids = (seq_len.shape[0] + device * row_count + slot_ids).astype(jnp.int32)
    segment = jnp.where(in_use > 0, covering, lone_ids).astype(jnp.int32)
    return (segment, in_use)

def causal_conv(inputs, kernel, bias_row, segment):
    kernel_len = kernel.shape[0]
    row_count = inputs.shape[0]
    result = bias_row[None, :] + kernel[kernel_len - 1][None, :] * inputs
    for offset in range(1, kernel_len):
        shifted = jnp.pad(inputs, ((offset, 0), (0, 0)))[:row_count]
        earlier = jnp.pad(segment, (offset, 0), constant_values=-1)[:row_count]
        same_seq = (earlier == segment).astype(inputs.dtype)
        result = result + kernel[kernel_len - 1 - offset][None, :] * shifted * same_seq[:, None]
    return result

def carry_state(state, inputs):
    local_part, span_total, keep_flag = inputs
    updated = local_part + keep_flag * jnp.exp(span_total)[:, None, None] * state
    return (updated, state)

def mixer_core(inner_x, inner_bc, dt_raw, conv_x, conv_bc, bias_x, bias_bc, dt_bias, a_log, d_skip, segment):
    row_count = inner_x.shape[0]
    head_count = dt_raw.shape[1]
    head_size = inner_x.shape[1] // head_count
    state_size = inner_bc.shape[1] // 2
    bin_count = row_count // BLOCK
    values = jax.nn.silu(causal_conv(inner_x, conv_x, bias_x, segment))
    maps_both = jax.nn.silu(causal_conv(inner_bc, conv_bc, bias_bc, segment))
    step_size = jax.nn.softplus(dt_raw + dt_bias[None, :])
    log_decay = -step_size * jnp.exp(a_log)[None, :]
    cumulative = jnp.transpose(jnp.cumsum(log_decay.reshape(bin_count, BLOCK, head_count), axis=1), (0, 2, 1))
    step_rows = jnp.transpose(step_size.reshape(bin_count, BLOCK, head_count), (0, 2, 1))
    bin_segment = segment.reshape(bin_count, BLOCK)
    positions = jnp.arange(BLOCK, dtype=jnp.int32)
    causal = (positions[:, None] >= positions[None, :])[None, :, :] & (bin_segment[:, :, None] == bin_segment[:, None, :])
    causal = causal[:, None, :, :]
    log_gaps = cumulative[:, :, :, None] - cumulative[:, :, None, :]
    decay_rows = jnp.where(causal, jnp.exp(jnp.where(causal, log_gaps, 0.0)), 0.0)
    key_rows = maps_both[:, :state_size].reshape(bin_count, BLOCK, state_size)
    query_rows = maps_both[:, state_size:].reshape(bin_count, BLOCK, state_size)
    scores = jnp.einsum('btn,bsn->bts', query_rows, key_rows, precision=HIGHEST)
    mixing = scores[:, None, :, :] * decay_rows * step_rows[:, :, None, :]
    head_values = values.reshape(bin_count, BLOCK, head_count, head_size)
    result = jnp.einsum('bhts,bshp->bthp', mixing, head_values, precision=HIGHEST)
    span_total = cumulative[:, :, BLOCK - 1]
    last_segment = bin_segment[:, BLOCK - 1]
    prior_segment = jnp.concatenate([jnp.full((1,), -1, jnp.int32), last_segment[:-1]]).astype(jnp.int32)
    in_last = (bin_segment == last_segment[:, None]).astype(jnp.float32)
    tail_weights = jnp.exp(span_total[:, :, None] - cumulative) * step_rows * in_last[:, None, :]
    weighted_values = head_values * jnp.transpose(tail_weights, (0, 2, 1))[:, :, :, None]
    local_states = jnp.einsum('bshp,bsn->bhpn', weighted_values, key_rows, precision=HIGHEST)
    keep_flags = (prior_segment == last_segment).astype(jnp.float32)
    start_state = jnp.zeros((head_count, head_size, state_size), jnp.float32)
    unused, incoming = lax.scan(carry_state, start_state, (local_states, span_total, keep_flags))
    reads = (bin_segment == prior_segment[:, None]).astype(jnp.float32)
    entry_decay = jnp.exp(cumulative) * reads[:, None, :]
    carried = jnp.einsum('btn,bhpn->bthp', query_rows, incoming, precision=HIGHEST)
    result = result + carried * jnp.transpose(entry_decay, (0, 2, 1))[:, :, :, None]
    result = result + d_skip[None, None, :, None] * head_values
    return result.reshape(row_count, head_count * head_size)

def pre_norm(residual, gain_row):
    scale_rows = lax.rsqrt(lax.optimization_barrier(jnp.mean(residual * residual, axis=1, keepdims=True)) + epsilon)
    return residual * scale_rows * gain_row[None, :]

def unchanged(row_sums):
    return row_sums

def rows_product(left, right):
    return lax.dot_general(left, right, (((0,), (0,)), ((), ())), preferred_element_type=jnp.float32)

def back_product(left, right):
    return lax.dot_general(left, right, (((1,), (1,)), ((), ())), preferred_element_type=jnp.float32)

def branch_forward(normed, matrices, smalls, segment, square_total):
    proj_z = jnp.dot(normed, matrices[0], preferred_element_type=jnp.float32)
    proj_x = jnp.dot(normed, matrices[1], preferred_element_type=jnp.float32)
    proj_bc = jnp.dot(normed, matrices[2], preferred_element_type=jnp.float32)
    proj_dt = jnp.dot(normed, matrices[3], preferred_element_type=jnp.float32)
    core_fn = partial(mixer_core, segment=segment)
    core_out, core_back = jax.vjp(core_fn, proj_x, proj_bc, proj_dt, smalls[0], smalls[1], smalls[2], smalls[3], smalls[4], smalls[5], smalls[6])
    gated_rows = core_out * jax.nn.silu(proj_z)
    inverse = lax.rsqrt(square_total(lax.optimization_barrier(jnp.sum(gated_rows * gated_rows, axis=1))) / INNER + epsilon)
    mixed_rows = (gated_rows * inverse[:, None] * smalls[7][None, :]).astype(jnp.bfloat16)
    return (mixed_rows, (proj_z, core_out, core_back, gated_rows, inverse))

def branch_backward(d_mixed, kept_state, gain_row, dot_total):
    proj_z, core_out, core_back, gated_rows, inverse = kept_state
    grad_gate = lax.optimization_barrier(jnp.sum(d_mixed * gated_rows * inverse[:, None], axis=0))
    d_hat = d_mixed * gain_row[None, :]
    dot_sum = dot_total(lax.optimization_barrier(jnp.sum(d_hat * gated_rows, axis=1)))
    d_gated = inverse[:, None] * d_hat - gated_rows * (inverse * inverse * inverse * dot_sum / INNER)[:, None]
    sigmoid_z = jax.nn.sigmoid(proj_z)
    d_core = d_gated * proj_z * sigmoid_z
    d_proj_z = d_gated * core_out * sigmoid_z * (1.0 + proj_z * (1.0 - sigmoid_z))
    core_grads = core_back(d_core)
    return (grad_gate, d_proj_z, core_grads)

def device_pass(block_in, block_cot, segment, in_use, weights):
    use_rows = in_use.astype(jnp.float32)[:, None]
    residual = block_in.astype(jnp.float32)
    saved_layers = []
    for layer_index in range(LAYERS):
        layer_weights = tuple((weight[layer_index] for weight in weights))
        normed = pre_norm(residual, layer_weights[0]).astype(jnp.bfloat16)
        mixed_rows, kept_state = branch_forward(normed, layer_weights[1:5], layer_weights[5:13], segment, unchanged)
        saved_layers.append((residual, normed, mixed_rows, kept_state, layer_weights))
        residual = residual + jnp.dot(mixed_rows, layer_weights[13], preferred_element_type=jnp.float32)
    d_residual = block_cot.astype(jnp.float32) * use_rows
    collected = []
    for layer_index in range(LAYERS - 1, -1, -1):
        residual_in, normed, mixed_rows, kept_state, layer_weights = saved_layers[layer_index]
        out_cot = d_residual.astype(jnp.bfloat16)
        grad_out = rows_product(mixed_rows, out_cot)
        d_mixed = back_product(out_cot, layer_weights[13])
        grad_gate, d_proj_z, core_grads = branch_backward(d_mixed, kept_state, layer_weights[12], unchanged)
        cot_z = d_proj_z.astype(jnp.bfloat16)
        cot_x = core_grads[0].astype(jnp.bfloat16)
        cot_bc = core_grads[1].astype(jnp.bfloat16)
        cot_dt = core_grads[2].astype(jnp.bfloat16)
        d_normed = back_product(cot_z, layer_weights[1]) + back_product(cot_x, layer_weights[2]) + back_product(cot_bc, layer_weights[3]) + back_product(cot_dt, layer_weights[4])
        norm_back = jax.vjp(pre_norm, residual_in, layer_weights[0])[1]
        d_previous, grad_norm = norm_back(d_normed)
        d_residual = d_residual + d_previous
        layer_grads = (grad_norm, rows_product(normed, cot_z), rows_product(normed, cot_x), rows_product(normed, cot_bc), rows_product(normed, cot_dt)) + tuple(core_grads[3:10]) + (grad_gate, grad_out)
        collected.append(layer_grads)
    ordered = collected[::-1]
    stacked = tuple((jnp.stack([layer_grads[grad_slot] for layer_grads in ordered]) for grad_slot in range(14)))
    return (residual * use_rows, d_residual, stacked)

def reference(hidden_in, cotangent, norm_gain, w_z, w_x, w_bc, w_dt, conv_x, conv_bc, bias_x, bias_bc, dt_bias, a_log, d_skip, gate_gain, w_out, seq_len, seq_owner, seq_start):
    weights = (norm_gain, w_z, w_x, w_bc, w_dt, conv_x, conv_bc, bias_x, bias_bc, dt_bias, a_log, d_skip, gate_gain, w_out)
    device_count = hidden_in.shape[0] // TOK_DEV

    def one_device(running, inputs):
        device, block_in, block_cot = inputs
        segment, in_use = slot_segments(seq_len, seq_owner, seq_start, device, TOK_DEV)
        block_out, block_grad, stacked = device_pass(block_in, block_cot, segment, in_use, weights)
        return (tuple((running[grad_slot] + stacked[grad_slot] for grad_slot in range(14))), (block_out, block_grad))
    start_totals = tuple((jnp.zeros(weight.shape, jnp.float32) for weight in weights))
    device_ids = jnp.arange(device_count, dtype=jnp.int32)
    totals, out_blocks = lax.scan(one_device, start_totals, (device_ids, hidden_in.reshape(device_count, TOK_DEV, D), cotangent.reshape(device_count, TOK_DEV, D)))
    hidden_out = out_blocks[0].reshape(hidden_in.shape)
    grad_hidden = out_blocks[1].reshape(hidden_in.shape)
    return (hidden_out, grad_hidden, totals[0], totals[1], totals[2], totals[3], totals[4], totals[5], totals[6], totals[7], totals[8], totals[9], totals[10], totals[11], totals[12], totals[13])
```

```python
from functools import partial

import jax
import jax.numpy as jnp
from jax import lax
from jax.experimental import pallas as pl
from jax.experimental.pallas import tpu as pltpu
from jax.sharding import PartitionSpec as P

epsilon = 1e-05
PARTS = 4
F32 = jnp.float32
BF16 = jnp.bfloat16
HEADS = 32
STATE = 128


def exchange(array, axis, bit):
    count = lax.axis_size(axis)
    return lax.ppermute(array, axis, [(i, i ^ bit) for i in range(count)])


def mm(left, right):
    return lax.dot_general(left, right, (((1,), (0,)), ((), ())), preferred_element_type=F32)


def mm_rt(left, right):
    return lax.dot_general(left, right, (((1,), (1,)), ((), ())), preferred_element_type=F32)


def mm_lt(left, right):
    return lax.dot_general(left, right, (((0,), (0,)), ((), ())), preferred_element_type=F32)


def whole(array):
    zeros = (0,) * array.ndim
    return (array, pl.BlockSpec(array.shape, lambda *_: zeros))


def chunked(array):
    tail = (0,) * (array.ndim - 1)
    return (array, pl.BlockSpec((1,) + array.shape[1:], lambda c, dev: (c,) + tail))


def columns(array, width):
    if width % 128 == 0:
        return (array, pl.BlockSpec((array.shape[0], width), lambda c, dev: (0, c)))
    pieces = array.reshape(array.shape[0], -1, width).transpose(1, 0, 2)
    return (pieces, pl.BlockSpec((None, array.shape[0], width), lambda c, dev: (c, 0, 0)))


def rows(array, height):
    return (array, pl.BlockSpec((height, array.shape[1]), lambda c, dev: (c, 0)))


def out_whole(shape, dtype):
    zeros = (0,) * len(shape)
    return (jax.ShapeDtypeStruct(shape, dtype), pl.BlockSpec(shape, lambda *_: zeros))


def out_chunked(shape, dtype):
    tail = (0,) * (len(shape) - 1)
    spec = pl.BlockSpec((1,) + shape[1:], lambda c, dev: (c,) + tail)
    return (jax.ShapeDtypeStruct(shape, dtype), spec)


def run(body, name, device, ins, outs, steps, scratch=(), flops=0):
    total = sum(a.size * a.dtype.itemsize for a, _ in ins)
    total += sum(s.size * s.dtype.itemsize for s, _ in outs)
    return pl.pallas_call(
        body,
        name=name,
        out_shape=[shape for shape, _ in outs],
        grid_spec=pltpu.PrefetchScalarGridSpec(
            num_scalar_prefetch=1,
            grid=(steps,),
            in_specs=[spec for _, spec in ins],
            out_specs=[spec for _, spec in outs],
            scratch_shapes=list(scratch),
        ),
        compiler_params=pltpu.CompilerParams(dimension_semantics=("arbitrary",)),
        cost_estimate=pl.CostEstimate(flops=flops, bytes_accessed=total, transcendentals=0),
    )(device, *[a for a, _ in ins])


def iota(shape, dim):
    return lax.broadcasted_iota(jnp.int32, shape, dim)


def roll_rows(array, shift):
    if array.shape[1] % 128 == 0:
        return pltpu.roll(array, shift % array.shape[0], 0)
    return jnp.roll(array, shift, 0)


def conv_rows(inputs, taps, bias, marks):
    result = bias + taps[3:4] * inputs
    for offset in range(1, 4):
        shifted = roll_rows(inputs, offset) * marks[:, offset : offset + 1]
        result = result + taps[3 - offset : 4 - offset] * shifted
    return result


def conv_back(d_out, inputs, taps, marks):
    d_in = taps[3:4] * d_out
    grads = [None] * 4
    grads[3] = jnp.sum(d_out * inputs, axis=0, keepdims=True)
    for offset in range(1, 4):
        kept = d_out * marks[:, offset : offset + 1]
        d_in = d_in + taps[3 - offset : 4 - offset] * roll_rows(kept, -offset)
        grads[3 - offset] = jnp.sum(kept * roll_rows(inputs, offset), axis=0, keepdims=True)
    return d_in, grads, jnp.sum(d_out, axis=0, keepdims=True)


def softplus(value):
    return jnp.maximum(value, 0.0) + jnp.log1p(jnp.exp(-jnp.abs(value)))


def solution(mesh):
    members = mesh.shape["shard"]
    replicas = mesh.shape["rep"]
    assert replicas % PARTS == 0 and replicas // PARTS >= 2
    assert replicas & (replicas - 1) == 0 and members & (members - 1) == 0
    return jax.shard_map(
        partial(on_device, members, replicas),
        mesh=mesh,
        in_specs=(
            P(("rep", "shard"), None),
            P(("rep", "shard"), None),
            P(None, "shard"),
            P(None, None, "shard"),
            P(None, None, "shard"),
            P(None, None, "shard"),
            P(None, None, "shard"),
            P(None, None, "shard"),
            P(None, None, "shard"),
            P(None, "shard"),
            P(None, "shard"),
            P(None, "shard"),
            P(None, "shard"),
            P(None, "shard"),
            P(None, "shard"),
            P(None, "shard", None),
            P(),
            P(),
            P(),
        ),
        out_specs=(
            P(("rep", "shard"), None),
            P(("rep", "shard"), None),
            P(None, "shard"),
            P(None, None, "shard"),
            P(None, None, "shard"),
            P(None, None, "shard"),
            P(None, None, "shard"),
            P(None, None, "shard"),
            P(None, None, "shard"),
            P(None, "shard"),
            P(None, "shard"),
            P(None, "shard"),
            P(None, "shard"),
            P(None, "shard"),
            P(None, "shard"),
            P(None, "shard", None),
        ),
        check_vma=False,
    )


def on_device(
    members,
    replicas,
    hidden_in,
    cotangent,
    norm_gain,
    w_z,
    w_x,
    w_bc,
    w_dt,
    conv_x,
    conv_bc,
    bias_x,
    bias_bc,
    dt_bias,
    a_log,
    d_skip,
    gate_gain,
    w_out,
    seq_len,
    seq_owner,
    seq_start,
):
    S = members
    T, D = hidden_in.shape
    R = S * T
    C = w_z.shape[2]
    H = w_dt.shape[2]
    NB = w_bc.shape[2]
    CH = C // PARTS
    HC = H // PARTS
    HS = C // H
    inner = C * S
    spans = replicas // PARTS
    DCH = D // spans
    w_z, w_x, w_bc, w_dt, w_out = w_z[0], w_x[0], w_bc[0], w_dt[0], w_out[0]

    shard_at = lax.axis_index("shard")
    device = (lax.axis_index("rep") * S + shard_at).astype(jnp.int32).reshape(1)

    def me_of(dev):
        return lax.rem(dev[0], S)

    def part_of(dev):
        return lax.rem(lax.div(dev[0], S), PARTS)

    def span_of(dev):
        return lax.div(dev[0], S * PARTS)

    blocks = [slice(b * T, (b + 1) * T) for b in range(S)]

    if S == 2:
        gain_other = exchange(norm_gain, "shard", 1)
        first = shard_at == 0
        gain = jnp.concatenate(
            [
                jnp.where(first, norm_gain, gain_other),
                jnp.where(first, gain_other, norm_gain),
            ],
            axis=1,
        )
    else:
        gain = lax.all_gather(norm_gain, "shard", axis=1, tiled=True)
    hidden = [hidden_in] + [exchange(hidden_in, "shard", j) for j in range(1, S)]
    cots = [cotangent] + [exchange(cotangent, "shard", j) for j in range(1, S)]

    lens = seq_len.reshape(1, -1)
    owners = seq_owner.reshape(1, -1)
    starts = seq_start.reshape(1, -1)
    records = lens.shape[1]
    taps_bc = jnp.concatenate([conv_bc[0], bias_bc, jnp.zeros((3, NB), F32)], axis=0)
    taps_x = jnp.concatenate(
        [
            conv_x[0],
            bias_x,
            gate_gain,
            jnp.repeat(d_skip, HS, axis=1),
            jnp.zeros((1, C), F32),
        ],
        axis=0,
    )
    wdt_parts = jnp.pad(
        w_dt.reshape(D, PARTS, HC).transpose(1, 0, 2), ((0, 0), (0, 0), (0, 128 - HC))
    )
    head_rows = jnp.concatenate([dt_bias, a_log], axis=0).reshape(2, PARTS, HC)
    head_rows = jnp.pad(head_rows.transpose(1, 0, 2), ((0, 0), (0, 6), (0, 128 - HC)))

    def prepare(dev, ln, ow, st, gain_r, wbc, tbc, *refs):
        hid, refs = refs[:S], refs[S:]
        normed_r, mask_r, cols_r, pbc_r, pre_r, map_r = refs[:6]
        sends = refs[6:]
        me = me_of(dev)
        base = dev[0] - me
        lane = iota((T, 128), 1)
        row = iota((T, 128), 0)
        for b in range(S):
            x = hid[b][...].astype(F32)
            scale = lax.rsqrt(jnp.mean(x * x, axis=1, keepdims=True) + epsilon)
            normed_r[blocks[b], :] = (x * scale * gain_r[...]).astype(BF16)
            slot = iota((T, records), 0)
            covers = (
                (ow[...] == base + (me ^ b)) & (slot >= st[...]) & (slot < st[...] + ln[...])
            )
            ids = iota((T, records), 1).astype(F32)
            used = jnp.sum(jnp.where(covers, 1.0, 0.0), axis=1, keepdims=True)
            found = jnp.sum(jnp.where(covers, ids, 0.0), axis=1, keepdims=True)
            lone = (records + row).astype(F32)
            seg = jnp.where(used > 0.5, found, lone)
            seg_t = seg.T
            same = (seg == seg_t) & (row >= lane)
            mask_r[blocks[b], :] = jnp.where(same, 1.0, 0.0)
            cols = jnp.where(lane == 0, used, 0.0)
            for offset in range(1, 4):
                mark = (pltpu.roll(seg, offset, 0) == seg) & (row >= offset)
                cols = jnp.where(lane == offset, jnp.where(mark, 1.0, 0.0), cols)
            cols_r[blocks[b], :] = cols
        pbc_r[...] = mm(normed_r[...], wbc[...])
        for b in range(S):
            marks = cols_r[blocks[b], :]
            pre = conv_rows(pbc_r[blocks[b], :], tbc[...], tbc[4:5], marks)
            pre_r[blocks[b], :] = pre
            out = (pre * jax.nn.sigmoid(pre)).astype(BF16)
            map_r[blocks[b], :] = out
            for j in range(1, S):
                sends[j - 1][blocks[b ^ j], :] = out

    outs = run(
        prepare,
        "norm_and_maps",
        device,
        [whole(a) for a in (lens, owners, starts, gain, w_bc, taps_bc, *hidden)],
        [
            out_whole((R, D), BF16),
            out_whole((R, 128), F32),
            out_whole((R, 128), F32),
            out_whole((R, NB), F32),
            out_whole((R, NB), F32),
            out_whole((R, NB), BF16),
        ]
        + [out_whole((R, NB), BF16) for _ in range(1, S)],
        1,
        flops=2 * R * D * NB,
    )
    normed, mask, cols, proj_bc, pre_bc, map_own = outs[:6]
    maps = [map_own] + [exchange(outs[5 + j], "shard", j) for j in range(1, S)]
    if S == 2:
        map_a, map_b = maps
    else:
        map_a = jnp.concatenate(maps[: S // 2], axis=1)
        map_b = jnp.concatenate(maps[S // 2 :], axis=1)

    normed_far = exchange(normed, "rep", 2)
    normed_all = [normed, exchange(normed, "rep", 1), normed_far, exchange(normed_far, "rep", 1)]
    cots_far = [exchange(c, "rep", 2) for c in cots]
    cots_all = [
        cots,
        [exchange(c, "rep", 1) for c in cots],
        cots_far,
        [exchange(c, "rep", 1) for c in cots_far],
    ]

    def project(dev, n_r, wz, wx, wdt, hp, tx, cols_r, wo, *refs):
        cot, refs = refs[:S], refs[S:]
        z_r, x_r, pre_r, y_r, cum_r, cumt_r, dm_r = refs
        n = n_r[...]
        z_r[0] = mm(n, wz[...])
        x_r[0] = mm(n, wx[...])
        y_r[0] = mm(n, wdt[0]) + hp[0, 0:1, :]
        row = iota((T, 128), 0)
        for b in range(S):
            marks = cols_r[blocks[b], :]
            pre_r[0, blocks[b], :] = conv_rows(x_r[0, blocks[b], :], tx[...], tx[4:5], marks)
            total = -softplus(y_r[0, blocks[b], :]) * jnp.exp(hp[0, 1:2, :])
            shift = 1
            while shift < T:
                total = total + jnp.where(row >= shift, pltpu.roll(total, shift, 0), 0.0)
                shift *= 2
            cum_r[0, blocks[b], :] = total
            cumt_r[0, b] = total.T[0:8]
            dm_r[0, blocks[b], :] = mm_rt(cot[b][...], wo[...]) * marks[:, 0:1]

    z, px, pre, y, cum, cum_t, d_mixed = run(
        project,
        "projections",
        device,
        [
            whole(normed),
            columns(w_z, CH),
            columns(w_x, CH),
            chunked(wdt_parts),
            chunked(head_rows),
            columns(taps_x, CH),
            whole(cols),
            rows(w_out, CH),
        ]
        + [whole(c) for c in cots],
        [
            out_chunked((PARTS, R, CH), F32),
            out_chunked((PARTS, R, CH), F32),
            out_chunked((PARTS, R, CH), F32),
            out_chunked((PARTS, R, 128), F32),
            out_chunked((PARTS, R, 128), F32),
            out_chunked((PARTS, S, 8, 128), F32),
            out_chunked((PARTS, R, CH), F32),
        ],
        PARTS,
        flops=6 * R * D * C,
    )

    def fill_scores(dev, a_r, b_r, mask_r, scores):
        a_is_key = me_of(dev) < S // 2
        for b in range(S):

            @pl.when(a_is_key)
            def _():
                scores[b] = mm_rt(b_r[blocks[b], :], a_r[blocks[b], :]) * mask_r[blocks[b], :]

            @pl.when(jnp.logical_not(a_is_key))
            def _():
                scores[b] = mm_rt(a_r[blocks[b], :], b_r[blocks[b], :]) * mask_r[blocks[b], :]

    def scan_forward(dev, a_r, b_r, mask_r, pre_r, y_r, cum_r, cumt_r, tx, z_r, dm_r, wo, *refs):
        core_r, sums_r, own_r = refs[0], refs[1], refs[2]
        sum_sends = refs[3 : 2 + S]
        sends = refs[2 + S : 1 + 2 * S]
        scores, acc, sums, gated_s = refs[1 + 2 * S :]
        c = pl.program_id(0)

        @pl.when(c == 0)
        def _():
            fill_scores(dev, a_r, b_r, mask_r, scores)
            acc[...] = jnp.zeros_like(acc)
            sums[...] = jnp.zeros_like(sums)

        lane = iota((T, 128), 1)
        for b in range(S):
            before = pre_r[0, blocks[b], :]
            values = before * jax.nn.sigmoid(before)
            step = softplus(y_r[0, blocks[b], :])
            parts = []
            for h in range(HC):
                at = slice(h * HS, (h + 1) * HS)
                gap = cum_r[0, blocks[b], h : h + 1] - cumt_r[0, b, h : h + 1, :]
                weights = (scores[b] * jnp.exp(jnp.minimum(gap, 0.0))).astype(BF16)
                scaled = (values[:, at] * step[:, h : h + 1]).astype(BF16)
                parts.append(mm(weights, scaled))
            core = jnp.concatenate(parts, axis=1) + values * tx[6:7]
            core_r[0, blocks[b], :] = core
            zed = z_r[0, blocks[b], :]
            gated = core * (zed * jax.nn.sigmoid(zed))
            gained = gated * tx[5:6]
            gated_s[blocks[b], :] = gained.astype(BF16)
            squares = jnp.sum(gated * gated, axis=1, keepdims=True)
            dots = jnp.sum(dm_r[0, blocks[b], :] * gained, axis=1, keepdims=True)
            sums[blocks[b], :] += jnp.where(lane == 0, squares, jnp.where(lane == 1, dots, 0.0))
        acc[...] += mm(gated_s[...], wo[...])

        @pl.when(c == PARTS - 1)
        def _():
            own_r[...] = acc[blocks[0], :]
            for j in range(1, S):
                sends[j - 1][...] = acc[blocks[j], :].astype(BF16)
            for b in range(S):
                turned = sums[blocks[b], :].T[0:8]
                sums_r[:, blocks[b]] = turned
                for j in range(1, S):
                    sum_sends[j - 1][:, blocks[b ^ j]] = turned

    outs = run(
        scan_forward,
        "scan_forward",
        device,
        [
            whole(map_a),
            whole(map_b),
            whole(mask),
            chunked(pre),
            chunked(y),
            chunked(cum),
            chunked(cum_t),
            columns(taps_x, CH),
            chunked(z),
            chunked(d_mixed),
            rows(w_out, CH),
        ],
        [
            out_chunked((PARTS, R, CH), F32),
            out_whole((8, R), F32),
            out_whole((T, D), F32),
        ]
        + [out_whole((8, R), F32) for _ in range(1, S)]
        + [out_whole((T, D), BF16) for _ in range(1, S)],
        PARTS,
        scratch=[
            pltpu.VMEM((S, T, T), F32),
            pltpu.VMEM((R, D), F32),
            pltpu.VMEM((R, 128), F32),
            pltpu.VMEM((R, CH), BF16),
        ],
        flops=2 * R * D * C + 4 * R * T * C,
    )
    core, sums_own, out_own = outs[:3]
    sums_all = [sums_own] + [exchange(outs[2 + j], "shard", j) for j in range(1, S)]
    out_other = [exchange(outs[1 + S + j], "shard", j) for j in range(1, S)]

    def gate_backward(dev, core_r, z_r, dm_r, tx, cols_r, *refs):
        parts, refs = refs[:S], refs[S:]
        mixed_r, cotz_r = refs[:PARTS], refs[PARTS : 2 * PARTS]
        cotz_c, dcore_r, gg_r, rows_r = refs[2 * PARTS :]
        c = pl.program_id(0)
        lane = iota((T, 128), 1)

        @pl.when(c == 0)
        def _():
            for b in range(S):
                total = parts[0][:, blocks[b]]
                for j in range(1, S):
                    total = total + parts[j][:, blocks[b]]
                turned = jnp.concatenate([total, jnp.zeros((T - 8, 128), F32)], axis=0).T
                inverse = lax.rsqrt(turned[:, 0:1] / inner + epsilon)
                factor = inverse * inverse * inverse * turned[:, 1:2] / inner
                rows_r[blocks[b], :] = jnp.where(
                    lane == 0, inverse, jnp.where(lane == 1, factor, 0.0)
                )

        gate_sum = jnp.zeros((1, CH), F32)
        mixed_parts, cot_parts = [], []
        for b in range(S):
            inverse = rows_r[blocks[b], 0:1]
            factor = rows_r[blocks[b], 1:2]
            used = cols_r[blocks[b], 0:1]
            core = core_r[0, blocks[b], :]
            zed = z_r[0, blocks[b], :]
            sig = jax.nn.sigmoid(zed)
            gated = core * (zed * sig)
            d_mixed = dm_r[0, blocks[b], :]
            scaled = gated * inverse
            gate_sum = gate_sum + jnp.sum(d_mixed * scaled, axis=0, keepdims=True)
            d_gated = inverse * (d_mixed * tx[5:6]) - gated * factor
            dcore_r[0, blocks[b], :] = (d_gated * (zed * sig)).astype(BF16)
            d_z = d_gated * core * sig * (1.0 + zed * (1.0 - sig))
            mixed_parts.append((scaled * tx[5:6] * used).astype(BF16))
            cot_parts.append(d_z.astype(BF16))
            cotz_c[0, blocks[b], :] = cot_parts[b]
        gg_r[0] = jnp.broadcast_to(gate_sum, (8, CH))
        mine = part_of(dev)
        for r in range(PARTS):

            @pl.when((c ^ mine) == r)
            def _():
                for b in range(S):
                    mixed_r[r][blocks[b], :] = mixed_parts[b]
                    cotz_r[r][blocks[b], :] = cot_parts[b]

    outs = run(
        gate_backward,
        "gate_backward",
        device,
        [chunked(core), chunked(z), chunked(d_mixed), columns(taps_x, CH), whole(cols)]
        + [whole(s) for s in sums_all],
        [out_whole((R, CH), BF16) for _ in range(2 * PARTS)]
        + [
            out_chunked((PARTS, R, CH), BF16),
            out_chunked((PARTS, R, CH), BF16),
            out_chunked((PARTS, 8, CH), F32),
            out_whole((R, 128), F32),
        ],
        PARTS,
        flops=40 * R * C,
    )
    mixed_parts, cotz_parts = outs[:PARTS], outs[PARTS : 2 * PARTS]
    cotz, d_core, gate_grads, row_scale = outs[2 * PARTS :]

    def quarter(parts):
        return [parts[0]] + [exchange(parts[r], "rep", r) for r in range(1, PARTS)]

    mixed_q = quarter(mixed_parts)
    cotz_q = quarter(cotz_parts)

    def scan_backward(
        dev, a_r, b_r, mask_r, pre_r, px_r, y_r, cum_r, cumt_r, hp, tx, core_r, dcore_r, cols_r, *refs
    ):
        cotx_r, refs = refs[:PARTS], refs[PARTS:]
        cotx_c, cdt_r, cg_r, hg_r, own_r = refs[:5]
        sends = refs[5 : 4 + S]
        scores, d_scores = refs[4 + S :]
        c = pl.program_id(0)

        @pl.when(c == 0)
        def _():
            fill_scores(dev, a_r, b_r, mask_r, scores)
            d_scores[...] = jnp.zeros_like(d_scores)

        lane = iota((T, 128), 1)
        row = iota((T, 128), 0)
        lane1 = iota((1, 128), 1)
        tap_grads = [jnp.zeros((1, CH), F32) for _ in range(5)]
        bias_grad = jnp.zeros((1, 128), F32)
        rate_grad = jnp.zeros((1, 128), F32)
        skip_grad = jnp.zeros((1, 128), F32)
        cot_parts = []
        rate = jnp.exp(hp[0, 1:2, :])
        for b in range(S):
            before = pre_r[0, blocks[b], :]
            sig = jax.nn.sigmoid(before)
            values = before * sig
            raw = y_r[0, blocks[b], :]
            step = softplus(raw)
            d_core_b = dcore_r[0, blocks[b], :]
            d_core_f = d_core_b.astype(F32)
            skip = values * tx[6:7]
            plain = core_r[0, blocks[b], :] - skip
            d_cum = jnp.zeros((T, 128), F32)
            d_step = jnp.zeros((T, 128), F32)
            d_values = []
            for h in range(HC):
                at = slice(h * HS, (h + 1) * HS)
                gap = cum_r[0, blocks[b], h : h + 1] - cumt_r[0, b, h : h + 1, :]
                decay = jnp.exp(jnp.minimum(gap, 0.0))
                weights = (scores[b] * decay).astype(BF16)
                v = values[:, at]
                scaled = (v * step[:, h : h + 1]).astype(BF16)
                d_out = d_core_b[:, at]
                d_out_f = d_core_f[:, at]
                d_scores[b] += mm_rt(d_out, scaled) * decay
                d_scaled = mm_lt(weights, d_out)
                change = jnp.sum(
                    d_out_f * plain[:, at] - d_scaled * scaled.astype(F32), axis=1, keepdims=True
                )
                d_cum = jnp.where(lane == h, change, d_cum)
                d_step = jnp.where(
                    lane == h, jnp.sum(d_scaled * v, axis=1, keepdims=True), d_step
                )
                d_values.append(d_scaled * step[:, h : h + 1])
                skip_grad = skip_grad + jnp.where(lane1 == h, jnp.sum(d_out_f * v), 0.0)
            shift = 1
            while shift < T:
                d_cum = d_cum + jnp.where(row < T - shift, pltpu.roll(d_cum, T - shift, 0), 0.0)
                shift *= 2
            rate_grad = rate_grad - jnp.sum(d_cum * step, axis=0, keepdims=True) * rate
            d_raw = (d_step - d_cum * rate) * jax.nn.sigmoid(raw)
            d_raw = jnp.where(lane < HC, d_raw, 0.0)
            bias_grad = bias_grad + jnp.sum(d_raw, axis=0, keepdims=True)
            cdt_r[0, blocks[b], :] = d_raw
            d_val = jnp.concatenate(d_values, axis=1) + d_core_f * tx[6:7]
            d_pre = d_val * sig * (1.0 + before * (1.0 - sig))
            d_in, grads, total = conv_back(
                d_pre, px_r[0, blocks[b], :], tx[...], cols_r[blocks[b], :]
            )
            for i, grad in enumerate(grads + [total]):
                tap_grads[i] = tap_grads[i] + grad
            cot_parts.append(d_in.astype(BF16))
            cotx_c[0, blocks[b], :] = cot_parts[b]
        cg_r[0] = jnp.concatenate(tap_grads + [jnp.zeros((3, CH), F32)], axis=0)
        hg_r[0] = jnp.concatenate(
            [bias_grad, rate_grad, skip_grad, jnp.zeros((5, 128), F32)], axis=0
        )
        mine = part_of(dev)
        for r in range(PARTS):

            @pl.when((c ^ mine) == r)
            def _():
                for b in range(S):
                    cotx_r[r][blocks[b], :] = cot_parts[b]

        @pl.when(c == PARTS - 1)
        def _():
            a_is_key = me_of(dev) < S // 2

            def finish(key_first):
                for b in range(S):
                    d_s = (d_scores[b] * mask_r[blocks[b], :]).astype(BF16)
                    a, bb = a_r[blocks[b], :], b_r[blocks[b], :]
                    if key_first:
                        both = (mm_lt(d_s, bb), mm(d_s, a))
                    else:
                        both = (mm(d_s, bb), mm_lt(d_s, a))
                    for j in range(S):
                        half = both[0] if j < S // 2 else both[1]
                        at = (j % (S // 2)) * NB
                        piece = half[:, at : at + NB]
                        if j == 0:
                            own_r[blocks[b], :] = piece
                        else:
                            sends[j - 1][blocks[b ^ j], :] = piece.astype(BF16)

            @pl.when(a_is_key)
            def _():
                finish(True)

            @pl.when(jnp.logical_not(a_is_key))
            def _():
                finish(False)

    outs = run(
        scan_backward,
        "scan_backward",
        device,
        [
            whole(map_a),
            whole(map_b),
            whole(mask),
            chunked(pre),
            chunked(px),
            chunked(y),
            chunked(cum),
            chunked(cum_t),
            chunked(head_rows),
            columns(taps_x, CH),
            chunked(core),
            chunked(d_core),
            whole(cols),
        ],
        [out_whole((R, CH), BF16) for _ in range(PARTS)]
        + [
            out_chunked((PARTS, R, CH), BF16),
            out_chunked((PARTS, R, 128), F32),
            out_chunked((PARTS, 8, CH), F32),
            out_chunked((PARTS, 8, 128), F32),
            out_whole((R, NB), F32),
        ]
        + [out_whole((R, NB), BF16) for _ in range(1, S)],
        PARTS,
        scratch=[pltpu.VMEM((S, T, T), F32), pltpu.VMEM((S, T, T), F32)],
        flops=8 * R * T * C,
    )
    cotx_parts = outs[:PARTS]
    cotx, cot_dt, tap_grads, head_grads, d_map_own = outs[PARTS : PARTS + 5]
    d_map_other = [exchange(outs[PARTS + 4 + j], "shard", j) for j in range(1, S)]
    cotx_q = quarter(cotx_parts)

    def input_backward(dev, cz, cx, cdt, wz, wx, wdt, dn_r, dt_r):
        c = pl.program_id(0)

        @pl.when(c == 0)
        def _():
            joined = cdt[0]
            for i in range(1, PARTS):
                joined = joined + pltpu.roll(cdt[i], i * HC, 1)
            joined = joined.astype(BF16)
            dt_r[...] = joined
            dn_r[...] = mm_rt(joined[:, 0:H], wdt[...])

        dn_r[...] += mm_rt(cz[0], wz[...]) + mm_rt(cx[0], wx[...])

    d_normed, cot_dt_all = run(
        input_backward,
        "input_backward",
        device,
        [
            chunked(cotz),
            chunked(cotx),
            whole(cot_dt),
            columns(w_z, CH),
            columns(w_x, CH),
            whole(w_dt),
        ],
        [out_whole((R, D), F32), out_whole((R, 128), BF16)],
        PARTS,
        flops=4 * R * D * C,
    )

    small_rows = -(-(NB + H + 16) // 16) * 16

    def maps_backward(
        dev, own, pre_r, pbc_r, cols_r, tbc, n_r, wbc, dn_r, cdt, cg, hg, gg, *refs
    ):
        others, hid, refs = refs[: S - 1], refs[S - 1 : 2 * S - 1], refs[2 * S - 1 :]
        dn_own, pack_r = refs[0], refs[1]
        sends = refs[2 : 1 + S]
        cot_s, dn_s = refs[1 + S :]
        pack_r[...] = jnp.zeros_like(pack_r)
        grads = [jnp.zeros((1, NB), F32) for _ in range(5)]
        for b in range(S):
            d_map = own[blocks[b], :]
            for other in others:
                d_map = d_map + other[blocks[b], :].astype(F32)
            before = pre_r[blocks[b], :]
            sig = jax.nn.sigmoid(before)
            d_pre = d_map * sig * (1.0 + before * (1.0 - sig))
            d_in, taps, total = conv_back(d_pre, pbc_r[blocks[b], :], tbc[...], cols_r[blocks[b], :])
            for i, grad in enumerate(taps + [total]):
                grads[i] = grads[i] + grad
            cot_s[blocks[b], :] = d_in.astype(BF16)
        dn_s[...] = dn_r[...] + mm_rt(cot_s[...], wbc[...])
        dn_own[...] = dn_s[blocks[0], :]
        gain_sum = jnp.zeros((1, D), F32)
        for b in range(S):
            x = hid[b][...].astype(F32)
            scale = lax.rsqrt(jnp.mean(x * x, axis=1, keepdims=True) + epsilon)
            part = dn_s[blocks[b], :]
            gain_sum = gain_sum + jnp.sum(part * (x * scale), axis=0, keepdims=True)
            if b > 0:
                sends[b - 1][...] = part.astype(BF16)
        pack_r[0:NB, :] = mm_lt(cot_s[...], n_r[...])
        pack_r[NB : NB + H, :] = mm_lt(cdt[...], n_r[...])[0:H]
        at = NB + H
        for i in range(PARTS):
            pack_r[at : at + 5, i * CH : (i + 1) * CH] = cg[i, 0:5]
            pack_r[at + 5 : at + 6, i * CH : (i + 1) * CH] = gg[i, 0:1]
            pack_r[at + 6 : at + 9, i * 128 : (i + 1) * 128] = hg[i, 0:3]
        for i in range(5):
            pack_r[at + 9 + i : at + 10 + i, 0:NB] = grads[i]
        pack_r[at + 14 : at + 15, :] = gain_sum

    outs = run(
        maps_backward,
        "maps_backward",
        device,
        [
            whole(a)
            for a in (
                d_map_own,
                pre_bc,
                proj_bc,
                cols,
                taps_bc,
                normed,
                w_bc,
                d_normed,
                cot_dt_all,
                tap_grads,
                head_grads,
                gate_grads,
                *d_map_other,
                *hidden,
            )
        ],
        [out_whole((T, D), F32), out_whole((small_rows, D), F32)]
        + [out_whole((T, D), BF16) for _ in range(1, S)],
        1,
        scratch=[pltpu.VMEM((R, NB), BF16), pltpu.VMEM((R, D), F32)],
        flops=2 * R * D * (2 * NB + 128),
    )
    dn_own, pack = outs[:2]
    dn_other = [exchange(outs[1 + j], "shard", j) for j in range(1, S)]

    def own_rows(dev, hid, cot, cols_r, rows_r, gain_r, dn_r, out_r, *refs):
        dns, outs_o, refs = refs[: S - 1], refs[S - 1 : 2 * S - 2], refs[2 * S - 2 :]
        hidden_r, grad_r = refs
        used = cols_r[:, 0:1]
        x = hid[...].astype(F32)
        added = out_r[...]
        for other in outs_o:
            added = added + other[...].astype(F32)
        hidden_r[...] = used * (x + rows_r[:, 0:1] * added)
        d_n = dn_r[...]
        for other in dns:
            d_n = d_n + other[...].astype(F32)
        scale = lax.rsqrt(jnp.mean(x * x, axis=1, keepdims=True) + epsilon)
        u = d_n * gain_r[...]
        dot = jnp.mean(u * x, axis=1, keepdims=True)
        grad_r[...] = used * cot[...].astype(F32) + scale * u - x * (scale * scale * scale * dot)

    hidden_out, grad_hidden = run(
        own_rows,
        "own_rows",
        device,
        [
            whole(hidden_in),
            whole(cotangent),
            (cols, pl.BlockSpec((T, 128), lambda *_: (0, 0))),
            (row_scale, pl.BlockSpec((T, 128), lambda *_: (0, 0))),
        ]
        + [whole(a) for a in (gain, dn_own, out_own, *dn_other, *out_other)],
        [out_whole((T, D), F32), out_whole((T, D), F32)],
        1,
    )

    def split_specs(shape):
        half = spans // 2
        send = pl.BlockSpec((1,) + shape, lambda i, dev: (jnp.minimum(i, half - 1), 0, 0))
        keep = pl.BlockSpec((1,) + shape, lambda i, dev: (jnp.maximum(i - half, 0), 0, 0))
        return [
            (jax.ShapeDtypeStruct((half,) + shape, BF16), send),
            (jax.ShapeDtypeStruct((half,) + shape, F32), keep),
        ]

    def relative(i):
        half = spans // 2
        return jnp.where(i < half, 2 * i + 1, 2 * (i - half))

    def by_span(array):
        height = array.shape[0]
        return (array, pl.BlockSpec((height, DCH), lambda i, dev: (0, span_of(dev) ^ relative(i))))

    def store_split(value, send_r, keep_r):
        i = pl.program_id(0)

        @pl.when(i < spans // 2)
        def _():
            send_r[0] = value.astype(BF16)

        @pl.when(i >= spans // 2)
        def _():
            keep_r[0] = value

    def in_weight_grad(dev, *refs):
        value = mm_lt(refs[0][...], refs[PARTS][...])
        for r in range(1, PARTS):
            value = value + mm_lt(refs[r][...], refs[PARTS + r][...])
        store_split(value, *refs[2 * PARTS :])

    def out_weight_grad(dev, *refs):
        value = jnp.zeros((CH, DCH), F32)
        for r in range(PARTS):
            for b in range(S):
                value = value + mm_lt(refs[r][blocks[b], :], refs[PARTS + r * S + b][...])
        store_split(value, *refs[PARTS + PARTS * S :])

    def sum_spans(send, keep):
        bit = PARTS
        total = keep + exchange(send, "rep", bit).astype(F32)
        while total.shape[0] > 1:
            bit *= 2
            send = total[1::2].astype(BF16)
            total = total[0::2] + exchange(send, "rep", bit).astype(F32)
        held = total.astype(BF16)
        while bit >= PARTS:
            held = jnp.concatenate([held, exchange(held, "rep", bit)], axis=0)
            bit //= 2
        far = exchange(held, "rep", 2)
        return [held, exchange(held, "rep", 1), far, exchange(far, "rep", 1)]

    def reversed_bits(i):
        result = jnp.int32(0) * i
        width = spans.bit_length() - 1
        for b in range(width):
            result = result | (((i >> b) & 1) << (width - 1 - b))
        return result

    def join_in(dev, *refs):
        mine = part_of(dev)
        for m in range(PARTS):

            @pl.when(mine == m)
            def _():
                for r in range(PARTS):
                    refs[PARTS][:, (m ^ r) * CH : ((m ^ r) + 1) * CH] = refs[r][0].astype(F32)

    def join_out(dev, *refs):
        mine = part_of(dev)
        for m in range(PARTS):

            @pl.when(mine == m)
            def _():
                for r in range(PARTS):
                    refs[PARTS][(m ^ r) * CH : ((m ^ r) + 1) * CH, :] = refs[r][0].astype(F32)

    def joined_in(pieces, name):
        return run(
            join_in,
            name,
            device,
            [chunked(p) for p in pieces],
            [
                (
                    jax.ShapeDtypeStruct((D, C), F32),
                    pl.BlockSpec((DCH, C), lambda i, dev: (span_of(dev) ^ reversed_bits(i), 0)),
                )
            ],
            spans,
        )[0]

    def joined_out(pieces, name):
        return run(
            join_out,
            name,
            device,
            [chunked(p) for p in pieces],
            [
                (
                    jax.ShapeDtypeStruct((C, D), F32),
                    pl.BlockSpec((C, DCH), lambda i, dev: (0, span_of(dev) ^ reversed_bits(i))),
                )
            ],
            spans,
        )[0]

    grad_flops = 2 * PARTS * R * D * CH
    send, keep = run(
        out_weight_grad,
        "out_weight_grad",
        device,
        [whole(m) for m in mixed_q] + [by_span(c) for group in cots_all for c in group],
        split_specs((CH, DCH)),
        spans,
        flops=grad_flops,
    )
    grad_out = joined_out(sum_spans(send, keep), "join_out")
    send, keep = run(
        in_weight_grad,
        "z_weight_grad",
        device,
        [by_span(n) for n in normed_all] + [whole(c) for c in cotz_q],
        split_specs((DCH, CH)),
        spans,
        flops=grad_flops,
    )
    grad_z = joined_in(sum_spans(send, keep), "join_z")
    send, keep = run(
        in_weight_grad,
        "x_weight_grad",
        device,
        [by_span(n) for n in normed_all] + [whole(c) for c in cotx_q],
        split_specs((DCH, CH)),
        spans,
        flops=grad_flops,
    )
    grad_x = joined_in(sum_spans(send, keep), "join_x")

    bit = 1
    while bit < replicas:
        rounded = pack.astype(BF16)
        pack = rounded.astype(F32) + exchange(rounded, "rep", bit).astype(F32)
        bit *= 2
    at = NB + H
    grad_bc = pack[0:NB].T
    grad_dt = pack[NB:at].T
    grad_conv_x = pack[at : at + 4, 0:C]
    grad_bias_x = pack[at + 4 : at + 5, 0:C]
    grad_gate = pack[at + 5 : at + 6, 0:C]
    heads = pack[at + 6 : at + 9, 0 : PARTS * 128].reshape(3, PARTS, 128)[:, :, 0:HC].reshape(3, H)
    grad_conv_bc = pack[at + 9 : at + 13, 0:NB]
    grad_bias_bc = pack[at + 13 : at + 14, 0:NB]
    gain_row = pack[at + 14].reshape(S, D // S)
    grad_gain = lax.dynamic_index_in_dim(gain_row, shard_at, 0, keepdims=True)
    for j in range(1, S):
        theirs = lax.dynamic_index_in_dim(gain_row, shard_at ^ j, 0, keepdims=True)
        grad_gain = grad_gain + exchange(theirs, "shard", j)
    return (
        hidden_out,
        grad_hidden,
        grad_gain,
        grad_z[None],
        grad_x[None],
        grad_bc[None],
        grad_dt[None],
        grad_conv_x[None],
        grad_conv_bc[None],
        grad_bias_x,
        grad_bias_bc,
        heads[0:1],
        heads[1:2],
        heads[2:3],
        grad_gate,
        grad_out[None],
    )
```

```python
from functools import partial

import jax
import jax.numpy as jnp
import numpy as np
from jax import lax
from jax.experimental import pallas as pl
from jax.experimental.pallas import tpu as pltpu
from jax.sharding import PartitionSpec as P

epsilon = 1e-05
PARTS = 4
F32 = jnp.float32
BF16 = jnp.bfloat16
VM = 1.5
UNIT = 1.1e9


def exchange(array, axis, bit):
    count = lax.axis_size(axis)
    return lax.ppermute(array, axis, [(i, i ^ bit) for i in range(count)])


def mm(left, right):
    return lax.dot_general(left, right, (((1,), (0,)), ((), ())), preferred_element_type=F32)


def mm_rt(left, right):
    return lax.dot_general(left, right, (((1,), (1,)), ((), ())), preferred_element_type=F32)


def mm_lt(left, right):
    return lax.dot_general(left, right, (((0,), (0,)), ((), ())), preferred_element_type=F32)


def whole(array):
    zeros = (0,) * array.ndim
    return (array, pl.BlockSpec(array.shape, lambda *_: zeros))


def chunked(array, start=0):
    tail = (0,) * (array.ndim - 1)
    return (array, pl.BlockSpec((1,) + array.shape[1:], lambda c, dev: (c + start,) + tail))


def columns(array, width, at):
    if width % 128 == 0:
        return (array, pl.BlockSpec((array.shape[0], width), lambda c, dev: (0, at(c, dev))))
    pieces = array.reshape(array.shape[0], -1, width).transpose(1, 0, 2)
    spec = pl.BlockSpec((None, array.shape[0], width), lambda c, dev: (at(c, dev), 0, 0))
    return (pieces, spec)


def rows(array, height, at):
    return (array, pl.BlockSpec((height, array.shape[1]), lambda c, dev: (at(c, dev), 0)))


def split(value):
    high = value.astype(BF16)
    return high, (value - high.astype(F32)).astype(BF16)


def spread(value, pattern):
    high, low = split(value)
    return mm(high, pattern) + mm(low, pattern)


def out_whole(shape, dtype):
    zeros = (0,) * len(shape)
    return (jax.ShapeDtypeStruct(shape, dtype), pl.BlockSpec(shape, lambda *_: zeros))


def out_chunked(shape, dtype):
    tail = (0,) * (len(shape) - 1)
    spec = pl.BlockSpec((1,) + shape[1:], lambda c, dev: (c,) + tail)
    return (jax.ShapeDtypeStruct(shape, dtype), spec)


def run(body, name, device, ins, outs, steps, scratch=(), us=1.0):
    total = sum(a.size * a.dtype.itemsize for a, _ in ins)
    total += sum(s.size * s.dtype.itemsize for s, _ in outs)
    held = 0
    for array, spec in list(ins) + list(outs):
        size = array.dtype.itemsize
        for extent in spec.block_shape:
            size *= extent or 1
        held += size * (1 if size == array.size * array.dtype.itemsize else 2)
    for buffer in scratch:
        held += buffer.dtype.itemsize * int(np.prod(buffer.shape))
    return pl.pallas_call(
        body,
        name=name,
        out_shape=[shape for shape, _ in outs],
        grid_spec=pltpu.PrefetchScalarGridSpec(
            num_scalar_prefetch=1,
            grid=(steps,),
            in_specs=[spec for _, spec in ins],
            out_specs=[spec for _, spec in outs],
            scratch_shapes=list(scratch),
        ),
        compiler_params=pltpu.CompilerParams(
            dimension_semantics=("arbitrary",),
            vmem_limit_bytes=int(held * VM) + (3 << 20),
        ),
        cost_estimate=pl.CostEstimate(
            flops=int(us * UNIT), bytes_accessed=total, transcendentals=0
        ),
    )(device, *[a for a, _ in ins])


def iota(shape, dim):
    return lax.broadcasted_iota(jnp.int32, shape, dim)


def roll_rows(array, shift):
    if array.shape[1] % 128 == 0:
        return pltpu.roll(array, shift % array.shape[0], 0)
    return jnp.roll(array, shift, 0)


def conv_rows(inputs, taps, bias, marks):
    result = bias + taps[3:4] * inputs
    for offset in range(1, 4):
        shifted = roll_rows(inputs, offset) * marks[:, offset : offset + 1]
        result = result + taps[3 - offset : 4 - offset] * shifted
    return result


def conv_back(d_out, inputs, taps, marks):
    d_in = taps[3:4] * d_out
    grads = [None] * 4
    grads[3] = jnp.sum(d_out * inputs, axis=0, keepdims=True)
    for offset in range(1, 4):
        kept = d_out * marks[:, offset : offset + 1]
        d_in = d_in + taps[3 - offset : 4 - offset] * roll_rows(kept, -offset)
        grads[3 - offset] = jnp.sum(kept * roll_rows(inputs, offset), axis=0, keepdims=True)
    return d_in, grads, jnp.sum(d_out, axis=0, keepdims=True)


def softplus(value):
    return jnp.maximum(value, 0.0) + jnp.log1p(jnp.exp(-jnp.abs(value)))


def solution(mesh):
    members = mesh.shape["shard"]
    replicas = mesh.shape["rep"]
    assert replicas % PARTS == 0 and replicas // PARTS >= 2
    assert replicas & (replicas - 1) == 0 and members & (members - 1) == 0
    return jax.shard_map(
        partial(on_device, members, replicas),
        mesh=mesh,
        in_specs=(
            P(("rep", "shard"), None),
            P(("rep", "shard"), None),
            P(None, "shard"),
            P(None, None, "shard"),
            P(None, None, "shard"),
            P(None, None, "shard"),
            P(None, None, "shard"),
            P(None, None, "shard"),
            P(None, None, "shard"),
            P(None, "shard"),
            P(None, "shard"),
            P(None, "shard"),
            P(None, "shard"),
            P(None, "shard"),
            P(None, "shard"),
            P(None, "shard", None),
            P(),
            P(),
            P(),
        ),
        out_specs=(
            P(("rep", "shard"), None),
            P(("rep", "shard"), None),
            P(None, "shard"),
            P(None, None, "shard"),
            P(None, None, "shard"),
            P(None, None, "shard"),
            P(None, None, "shard"),
            P(None, None, "shard"),
            P(None, None, "shard"),
            P(None, "shard"),
            P(None, "shard"),
            P(None, "shard"),
            P(None, "shard"),
            P(None, "shard"),
            P(None, "shard"),
            P(None, "shard", None),
        ),
        check_vma=False,
    )


def on_device(
    members,
    replicas,
    hidden_in,
    cotangent,
    norm_gain,
    w_z,
    w_x,
    w_bc,
    w_dt,
    conv_x,
    conv_bc,
    bias_x,
    bias_bc,
    dt_bias,
    a_log,
    d_skip,
    gate_gain,
    w_out,
    seq_len,
    seq_owner,
    seq_start,
):
    S = members
    T, D = hidden_in.shape
    R = S * T
    C = w_z.shape[2]
    H = w_dt.shape[2]
    NB = w_bc.shape[2]
    CH = C // PARTS
    HC = H // PARTS
    HS = C // H
    inner = C * S
    spans = replicas // PARTS
    DCH = D // spans
    w_z, w_x, w_bc, w_dt, w_out = w_z[0], w_x[0], w_bc[0], w_dt[0], w_out[0]

    shard_at = lax.axis_index("shard")
    device = (lax.axis_index("rep") * S + shard_at).astype(jnp.int32).reshape(1)

    def me_of(dev):
        return lax.rem(dev[0], S)

    def part_of(dev):
        return lax.rem(lax.div(dev[0], S), PARTS)

    def span_of(dev):
        return lax.div(dev[0], S * PARTS)

    blocks = [slice(b * T, (b + 1) * T) for b in range(S)]

    if S == 2:
        gains = [norm_gain, exchange(norm_gain, "shard", 1)]
    else:
        gains = [lax.all_gather(norm_gain, "shard", axis=1, tiled=True)]
    hidden = [hidden_in] + [exchange(hidden_in, "shard", j) for j in range(1, S)]
    cots = [cotangent] + [exchange(cotangent, "shard", j) for j in range(1, S)]

    lens = seq_len.reshape(1, -1)
    owners = seq_owner.reshape(1, -1)
    starts = seq_start.reshape(1, -1)
    records = lens.shape[1]
    wdt_t = w_dt.T
    conv_x, conv_bc = conv_x[0], conv_bc[0]

    def chunk(c, dev):
        return part_of(dev) ^ c

    def to_part(value, c, dev):
        return pltpu.roll(value, lax.rem(128 - chunk(c, dev) * HC, 128), 1)

    def from_part(value, c, dev):
        return pltpu.roll(value, chunk(c, dev) * HC, 1)

    def head_pattern():
        return jnp.where(iota((128, CH), 0) == iota((128, CH), 1) // HS, 1.0, 0.0).astype(BF16)

    def head_pattern_t():
        return jnp.where(iota((CH, 128), 0) // HS == iota((CH, 128), 1), 1.0, 0.0).astype(BF16)

    def pad_lanes(value):
        gap = jnp.zeros((value.shape[0], 128 - value.shape[1]), F32)
        return jnp.concatenate([value, gap], axis=1)

    group = min(2, HC)
    width = group * HS

    def head_masks():
        lane = iota((1, width), 1) // HS
        return [jnp.where(lane == g, 1.0, 0.0) for g in range(group)]

    def prepare(dev, ln, ow, st, wbc, tbc, bbc, *refs):
        parts, refs = refs[: len(gains)], refs[len(gains) :]
        hid, refs = refs[:S], refs[S:]
        gain_r, normed_r, mask_r, cols_r, pbc_r, pre_r, map_r = refs[:7]
        sends = refs[7:]
        me = me_of(dev)
        base = dev[0] - me
        if S == 2:
            low, high = parts[0][...], parts[1][...]
            first = me == 0
            gain_r[...] = jnp.concatenate(
                [jnp.where(first, low, high), jnp.where(first, high, low)], axis=1
            )
        else:
            gain_r[...] = parts[0][...]
        lane = iota((T, 128), 1)
        row = iota((T, 128), 0)
        for b in range(S):
            x = hid[b][...].astype(F32)
            scale = lax.rsqrt(jnp.mean(x * x, axis=1, keepdims=True) + epsilon)
            normed_r[blocks[b], :] = (x * scale * gain_r[...]).astype(BF16)
            slot = iota((T, records), 0)
            covers = (
                (ow[...] == base + (me ^ b)) & (slot >= st[...]) & (slot < st[...] + ln[...])
            )
            ids = iota((T, records), 1).astype(F32)
            used = jnp.sum(jnp.where(covers, 1.0, 0.0), axis=1, keepdims=True)
            found = jnp.sum(jnp.where(covers, ids, 0.0), axis=1, keepdims=True)
            lone = (records + row).astype(F32)
            seg = jnp.where(used > 0.5, found, lone)
            seg_t = seg.T
            same = (seg == seg_t) & (row >= lane)
            mask_r[blocks[b], :] = jnp.where(same, 1.0, 0.0)
            cols = jnp.where(lane == 0, used, 0.0)
            for offset in range(1, 4):
                mark = (pltpu.roll(seg, offset, 0) == seg) & (row >= offset)
                cols = jnp.where(lane == offset, jnp.where(mark, 1.0, 0.0), cols)
            cols_r[blocks[b], :] = cols
        pbc_r[...] = mm(normed_r[...], wbc[...])
        for b in range(S):
            marks = cols_r[blocks[b], :]
            pre = conv_rows(pbc_r[blocks[b], :], tbc[...], bbc[...], marks)
            pre_r[blocks[b], :] = pre
            out = (pre * jax.nn.sigmoid(pre)).astype(BF16)
            map_r[blocks[b], :] = out
            for j in range(1, S):
                sends[j - 1][blocks[b ^ j], :] = out

    outs = run(
        prepare,
        "norm_and_maps",
        device,
        [whole(a) for a in (lens, owners, starts, w_bc, conv_bc, bias_bc, *gains, *hidden)],
        [
            out_whole((1, D), F32),
            out_whole((R, D), BF16),
            out_whole((R, 128), F32),
            out_whole((R, 128), F32),
            out_whole((R, NB), F32),
            out_whole((R, NB), F32),
            out_whole((R, NB), BF16),
        ]
        + [out_whole((R, NB), BF16) for _ in range(1, S)],
        1,
        us=2.5,
    )
    gain, normed, mask, cols, proj_bc, pre_bc, map_own = outs[:7]
    maps = [map_own] + [exchange(outs[6 + j], "shard", j) for j in range(1, S)]
    if S == 2:
        map_a, map_b = maps
    else:
        map_a = jnp.concatenate(maps[: S // 2], axis=1)
        map_b = jnp.concatenate(maps[S // 2 :], axis=1)

    normed_far = exchange(normed, "rep", 2)
    normed_all = [normed, exchange(normed, "rep", 1), normed_far, exchange(normed_far, "rep", 1)]

    def project(dev, n_r, wz, wx, wdt, dtb, alog, dsk, tx, bx, cols_r, wo, *refs):
        cot, refs = refs[:S], refs[S:]
        z_r, x_r, pre_r, y_r, cum_r, cumt_r, hp_r, sk_r, dm_r, cg_r = refs[:10]
        y_s, cum_s = refs[10:]
        c = pl.program_id(0)
        n = n_r[...]

        @pl.when(c == 0)
        def _():
            y_s[...] = pad_lanes(mm_rt(n, wdt[...]) + dtb[...])
            row = iota((T, 128), 0)
            rate = jnp.exp(pad_lanes(alog[...]))
            for b in range(S):
                total = -softplus(y_s[blocks[b], :]) * rate
                shift = 1
                while shift < T:
                    total = total + jnp.where(row >= shift, pltpu.roll(total, shift, 0), 0.0)
                    shift *= 2
                cum_s[blocks[b], :] = total
                cg_r[blocks[b], :] = cot[b][...]

        z_r[0] = mm(n, wz[...])
        x_r[0] = mm(n, wx[...])
        y_r[0] = to_part(y_s[...], c, dev)
        turned = to_part(cum_s[...], c, dev)
        cum_r[0] = turned
        pair = jnp.concatenate(
            [pad_lanes(alog[...]), pad_lanes(dsk[...]), jnp.zeros((6, 128), F32)], axis=0
        )
        pair = to_part(pair, c, dev)
        hp_r[0] = jnp.exp(pair)
        skips = [jnp.broadcast_to(pair[1:2, h : h + 1], (1, HS)) for h in range(HC)]
        sk_r[0] = jnp.broadcast_to(jnp.concatenate(skips, axis=1), (8, CH))
        dm_r[0] = mm_rt(cg_r[...], wo[...]) * cols_r[:, 0:1]
        for b in range(S):
            marks = cols_r[blocks[b], :]
            pre_r[0, blocks[b], :] = conv_rows(x_r[0, blocks[b], :], tx[...], bx[...], marks)
            cumt_r[0, b] = turned[blocks[b]].T[0:8]

    z, px, pre, y, cum, cum_t, head_rows, skip_rows, d_mixed, cot_group = run(
        project,
        "projections",
        device,
        [
            whole(normed),
            columns(w_z, CH, chunk),
            columns(w_x, CH, chunk),
            whole(wdt_t),
            whole(dt_bias),
            whole(a_log),
            whole(d_skip),
            columns(conv_x, CH, chunk),
            columns(bias_x, CH, chunk),
            whole(cols),
            rows(w_out, CH, chunk),
        ]
        + [whole(c) for c in cots],
        [
            out_chunked((PARTS, R, CH), F32),
            out_chunked((PARTS, R, CH), F32),
            out_chunked((PARTS, R, CH), F32),
            out_chunked((PARTS, R, 128), F32),
            out_chunked((PARTS, R, 128), F32),
            out_chunked((PARTS, S, 8, 128), F32),
            out_chunked((PARTS, 8, 128), F32),
            out_chunked((PARTS, 8, CH), F32),
            out_chunked((PARTS, R, CH), F32),
            out_whole((R, D), BF16),
        ],
        PARTS,
        scratch=[pltpu.VMEM((R, 128), F32), pltpu.VMEM((R, 128), F32)],
        us=4.0,
    )
    cots_far = exchange(cot_group, "rep", 2)
    cots_all = [
        cot_group,
        exchange(cot_group, "rep", 1),
        cots_far,
        exchange(cots_far, "rep", 1),
    ]

    def decays(cum_r, cumt_r, b, h):
        gap = cum_r[0, blocks[b], h : h + 1] - cumt_r[0, b, h : h + 1, :]
        return gap

    def fill_scores(dev, a_r, b_r, mask_r, scores):
        a_is_key = me_of(dev) < S // 2
        for b in range(S):

            @pl.when(a_is_key)
            def _():
                scores[b] = mm_rt(b_r[blocks[b], :], a_r[blocks[b], :]) * mask_r[blocks[b], :]

            @pl.when(jnp.logical_not(a_is_key))
            def _():
                scores[b] = mm_rt(a_r[blocks[b], :], b_r[blocks[b], :]) * mask_r[blocks[b], :]

    def scan_forward(
        dev, a_r, b_r, mask_r, pre_r, y_r, cum_r, cumt_r, sk, gg, z_r, dm_r, wo, *refs
    ):
        core_r, sums_r, own_r = refs[0], refs[1], refs[2]
        sum_sends = refs[3 : 2 + S]
        sends = refs[2 + S : 1 + 2 * S]
        scores, acc, sums, gated_s = refs[1 + 2 * S :]
        c = pl.program_id(0)

        @pl.when(c == 0)
        def _():
            fill_scores(dev, a_r, b_r, mask_r, scores)
            acc[...] = jnp.zeros_like(acc)
            sums[...] = jnp.zeros_like(sums)

        lane = iota((T, 128), 1)
        pattern = head_pattern()
        masks = head_masks()
        for b in range(S):
            before = pre_r[0, blocks[b], :]
            values = before * jax.nn.sigmoid(before)
            step = spread(softplus(y_r[0, blocks[b], :]), pattern)
            scaled = (values * step).astype(BF16)
            parts = []
            for first in range(0, HC, group):
                at = slice(first * HS, first * HS + width)
                weights = []
                for h in range(first, first + group):
                    gap = cum_r[0, blocks[b], h : h + 1] - cumt_r[0, b, h : h + 1, :]
                    weights.append(
                        (scores[b] * jnp.exp(jnp.minimum(gap, 0.0))).astype(BF16)
                    )
                stacked = [scaled[:, at] * m.astype(BF16) for m in masks]
                parts.append(
                    mm(jnp.concatenate(weights, axis=1), jnp.concatenate(stacked, axis=0))
                )
            core = jnp.concatenate(parts, axis=1) + values * sk[0, 0:1]
            core_r[0, blocks[b], :] = core
            zed = z_r[0, blocks[b], :]
            gated = core * (zed * jax.nn.sigmoid(zed))
            gained = gated * gg[...]
            gated_s[blocks[b], :] = gained.astype(BF16)
            squares = jnp.sum(gated * gated, axis=1, keepdims=True)
            dots = jnp.sum(dm_r[0, blocks[b], :] * gained, axis=1, keepdims=True)
            sums[blocks[b], :] += jnp.where(lane == 0, squares, jnp.where(lane == 1, dots, 0.0))
        acc[...] += mm(gated_s[...], wo[...])

        @pl.when(c == PARTS - 1)
        def _():
            own_r[...] = acc[blocks[0], :]
            for j in range(1, S):
                sends[j - 1][...] = acc[blocks[j], :].astype(BF16)
            for b in range(S):
                turned = sums[blocks[b], :].T[0:8]
                sums_r[:, blocks[b]] = turned
                for j in range(1, S):
                    sum_sends[j - 1][:, blocks[b ^ j]] = turned

    outs = run(
        scan_forward,
        "scan_forward",
        device,
        [
            whole(map_a),
            whole(map_b),
            whole(mask),
            chunked(pre),
            chunked(y),
            chunked(cum),
            chunked(cum_t),
            chunked(skip_rows),
            columns(gate_gain, CH, chunk),
            chunked(z),
            chunked(d_mixed),
            rows(w_out, CH, chunk),
        ],
        [
            out_chunked((PARTS, R, CH), F32),
            out_whole((8, R), F32),
            out_whole((T, D), F32),
        ]
        + [out_whole((8, R), F32) for _ in range(1, S)]
        + [out_whole((T, D), BF16) for _ in range(1, S)],
        PARTS,
        scratch=[
            pltpu.VMEM((S, T, T), F32),
            pltpu.VMEM((R, D), F32),
            pltpu.VMEM((R, 128), F32),
            pltpu.VMEM((R, CH), BF16),
        ],
        us=4.0,
    )
    core, sums_own, out_own = outs[:3]
    sums_all = [sums_own] + [exchange(outs[2 + j], "shard", j) for j in range(1, S)]
    out_sends = [outs[1 + S + j] for j in range(1, S)]

    def gate_backward(dev, core_r, z_r, dm_r, gg, cols_r, *refs):
        parts, refs = refs[:S], refs[S:]
        both_r = refs[:PARTS]
        cotz_c, dcore_r, gg_r, rows_r = refs[PARTS:]
        c = pl.program_id(0)
        lane = iota((T, 128), 1)

        @pl.when(c == 0)
        def _():
            for b in range(S):
                total = parts[0][:, blocks[b]]
                for j in range(1, S):
                    total = total + parts[j][:, blocks[b]]
                turned = jnp.concatenate([total, jnp.zeros((T - 8, 128), F32)], axis=0).T
                inverse = lax.rsqrt(turned[:, 0:1] / inner + epsilon)
                factor = inverse * inverse * inverse * turned[:, 1:2] / inner
                rows_r[blocks[b], :] = jnp.where(
                    lane == 0, inverse, jnp.where(lane == 1, factor, 0.0)
                )

        gate_sum = jnp.zeros((1, CH), F32)
        mixed_parts, cot_parts = [], []
        for b in range(S):
            inverse = rows_r[blocks[b], 0:1]
            factor = rows_r[blocks[b], 1:2]
            used = cols_r[blocks[b], 0:1]
            core = core_r[0, blocks[b], :]
            zed = z_r[0, blocks[b], :]
            sig = jax.nn.sigmoid(zed)
            gated = core * (zed * sig)
            d_mixed = dm_r[0, blocks[b], :]
            scaled = gated * inverse
            gate_sum = gate_sum + jnp.sum(d_mixed * scaled, axis=0, keepdims=True)
            d_gated = inverse * (d_mixed * gg[...]) - gated * factor
            dcore_r[0, blocks[b], :] = (d_gated * (zed * sig)).astype(BF16)
            d_z = d_gated * core * sig * (1.0 + zed * (1.0 - sig))
            mixed_parts.append((scaled * gg[...] * used).astype(BF16))
            cot_parts.append(d_z.astype(BF16))
            cotz_c[0, blocks[b], :] = cot_parts[b]
        gg_r[0] = jnp.broadcast_to(gate_sum, (8, CH))
        for r in range(PARTS):

            @pl.when(c == r)
            def _():
                for b in range(S):
                    both_r[r][blocks[b], 0:CH] = mixed_parts[b]
                    both_r[r][blocks[b], CH : 2 * CH] = cot_parts[b]

    outs = run(
        gate_backward,
        "gate_backward",
        device,
        [chunked(core), chunked(z), chunked(d_mixed), columns(gate_gain, CH, chunk), whole(cols)]
        + [whole(s) for s in sums_all],
        [out_whole((R, 2 * CH), BF16) for _ in range(PARTS)]
        + [
            out_chunked((PARTS, R, CH), BF16),
            out_chunked((PARTS, R, CH), BF16),
            out_chunked((PARTS, 8, CH), F32),
            out_whole((R, 128), F32),
        ],
        PARTS,
        us=2.2,
    )
    cotz, d_core, gate_grads, row_scale = outs[PARTS:]
    both_q = [outs[0]] + [exchange(outs[r], "rep", r) for r in range(1, PARTS)]

    half_parts = PARTS // 2

    def scan_backward(
        last, dev, a_r, b_r, mask_r, pre_r, px_r, y_r, cum_r, cumt_r, hp, sk, tx, core_r, dcore_r,
        cols_r, *refs
    ):
        if last:
            d_before, refs = refs[0], refs[1:]
        cotx_r, refs = refs[:half_parts], refs[half_parts:]
        cotx_c, cdt_r, cg_r, hg_r = refs[:4]
        if last:
            own_r, sends = refs[4], refs[5 : 4 + S]
            scores, scores_t, d_scores = refs[4 + S :]
        else:
            d_scores, scores, scores_t = refs[4:]
        c = pl.program_id(0)

        @pl.when(c == 0)
        def _():
            fill_scores(dev, a_r, b_r, mask_r, scores)
            for b in range(S):
                scores_t[b] = scores[b].T
            d_scores[...] = d_before[...] if last else jnp.zeros_like(d_scores)

        row = iota((T, 128), 0)
        lane = iota((T, 128), 1)
        pattern = head_pattern()
        pattern_t = head_pattern_t()
        masks = [m.astype(BF16) for m in head_masks()]
        tap_grads = [jnp.zeros((1, CH), F32) for _ in range(6)]
        bias_grad = jnp.zeros((1, 128), F32)
        rate_grad = jnp.zeros((1, 128), F32)
        cot_parts = []
        rate = hp[0, 0:1, :]
        for b in range(S):
            before = pre_r[0, blocks[b], :]
            sig = jax.nn.sigmoid(before)
            values = before * sig
            raw = y_r[0, blocks[b], :]
            step = softplus(raw)
            step_full = spread(step, pattern)
            scaled = (values * step_full).astype(BF16)
            d_out = dcore_r[0, blocks[b], :]
            d_scaled = []
            for first in range(0, HC, group):
                at = slice(first * HS, first * HS + width)
                stacked = jnp.concatenate([d_out[:, at] * m for m in masks], axis=0)
                d_weights = mm_rt(stacked, scaled[:, at])
                turned, change = [], None
                for g in range(group):
                    h = first + g
                    gap = cum_r[0, blocks[b], h : h + 1] - cumt_r[0, b, h : h + 1, :]
                    turned.append((scores_t[b] * jnp.exp(jnp.minimum(-gap, 0.0))).astype(BF16))
                    term = d_weights[g * T : (g + 1) * T] * jnp.exp(jnp.minimum(gap, 0.0))
                    change = term if change is None else change + term
                d_scores[b] += change
                d_scaled.append(mm(jnp.concatenate(turned, axis=1), stacked))
            d_scaled = jnp.concatenate(d_scaled, axis=1)
            d_out = d_out.astype(F32)
            plain = core_r[0, blocks[b], :] - values * sk[0, 0:1]
            d_cum = spread(d_out * plain - d_scaled * scaled.astype(F32), pattern_t)
            d_step = spread(d_scaled * values, pattern_t)
            shift = 1
            while shift < T:
                d_cum = d_cum + jnp.where(row < T - shift, pltpu.roll(d_cum, T - shift, 0), 0.0)
                shift *= 2
            rate_grad = rate_grad - jnp.sum(d_cum * step, axis=0, keepdims=True) * rate
            d_raw = (d_step - d_cum * rate) * jax.nn.sigmoid(raw)
            d_raw = jnp.where(lane < HC, d_raw, 0.0)
            bias_grad = bias_grad + jnp.sum(d_raw, axis=0, keepdims=True)
            cdt_r[0, blocks[b], :] = d_raw
            d_val = d_scaled * step_full + d_out * sk[0, 0:1]
            d_pre = d_val * sig * (1.0 + before * (1.0 - sig))
            d_in, grads, total = conv_back(
                d_pre, px_r[0, blocks[b], :], tx[...], cols_r[blocks[b], :]
            )
            skip = jnp.sum(d_out * values, axis=0, keepdims=True)
            for i, grad in enumerate(grads + [total, skip]):
                tap_grads[i] = tap_grads[i] + grad
            cot_parts.append(d_in.astype(BF16))
            cotx_c[0, blocks[b], :] = cot_parts[b]
        cg_r[0] = jnp.concatenate(tap_grads + [jnp.zeros((2, CH), F32)], axis=0)
        high, low = split(jnp.broadcast_to(tap_grads[5], (8, CH)))
        skip_grad = mm(high, pattern_t) + mm(low, pattern_t)
        hg_r[0] = jnp.concatenate(
            [bias_grad, rate_grad, skip_grad[0:1], jnp.zeros((5, 128), F32)], axis=0
        )
        for r in range(half_parts):

            @pl.when(c == r)
            def _():
                for b in range(S):
                    cotx_r[r][blocks[b], :] = cot_parts[b]

        if last:

            @pl.when(c == half_parts - 1)
            def _():
                a_is_key = me_of(dev) < S // 2

                def finish(key_first):
                    for b in range(S):
                        d_s = (d_scores[b] * mask_r[blocks[b], :]).astype(BF16)
                        a, bb = a_r[blocks[b], :], b_r[blocks[b], :]
                        if key_first:
                            both = (mm_lt(d_s, bb), mm(d_s, a))
                        else:
                            both = (mm(d_s, bb), mm_lt(d_s, a))
                        for j in range(S):
                            half = both[0] if j < S // 2 else both[1]
                            at = (j % (S // 2)) * NB
                            piece = half[:, at : at + NB]
                            if j == 0:
                                own_r[blocks[b], :] = piece
                            else:
                                sends[j - 1][blocks[b ^ j], :] = piece.astype(BF16)

                @pl.when(a_is_key)
                def _():
                    finish(True)

                @pl.when(jnp.logical_not(a_is_key))
                def _():
                    finish(False)

    def half_backward(last, carried):
        start = 0 if last else half_parts
        ins = [whole(map_a), whole(map_b), whole(mask)]
        for array in (pre, px, y, cum, cum_t, head_rows, skip_rows):
            ins.append(chunked(array, start))
        ins.append(columns(conv_x, CH, lambda c, dev: chunk(c + start, dev)))
        ins += [chunked(core, start), chunked(d_core, start), whole(cols)]
        outs = [out_whole((R, CH), BF16) for _ in range(half_parts)] + [
            out_chunked((half_parts, R, CH), BF16),
            out_chunked((half_parts, R, 128), F32),
            out_chunked((half_parts, 8, CH), F32),
            out_chunked((half_parts, 8, 128), F32),
        ]
        square = pltpu.VMEM((S, T, T), F32)
        if last:
            ins.append(whole(carried))
            outs += [out_whole((R, NB), F32)]
            outs += [out_whole((R, NB), BF16) for _ in range(1, S)]
            scratch = [square, square, square]
        else:
            outs += [out_whole((S, T, T), F32)]
            scratch = [square, square]
        return run(
            partial(scan_backward, last),
            "scan_backward_near" if last else "scan_backward_far",
            device,
            ins,
            outs,
            half_parts,
            scratch=scratch,
            us=5.0,
        )

    far = half_backward(False, None)
    cotx_far = [exchange(far[r], "rep", half_parts + r) for r in range(half_parts)]
    near = half_backward(True, far[half_parts + 4])
    cotx_q = [near[0], exchange(near[1], "rep", 1)] + cotx_far
    halves = [near[half_parts : half_parts + 4], far[half_parts : half_parts + 4]]
    d_map_own = near[half_parts + 4]
    d_map_other = [exchange(near[half_parts + 4 + j], "shard", j) for j in range(1, S)]

    def input_backward(dev, cz, near_x, far_x, near_dt, far_dt, wz, wx, wdt, dn_r, dt_r):
        c = pl.program_id(0)

        @pl.when(c == 0)
        def _():
            joined = jnp.zeros((R, 128), F32)
            for i in range(PARTS):
                held = (near_dt, far_dt)[i // half_parts]
                joined = joined + from_part(held[i % half_parts], i, dev)
            joined = joined.astype(BF16)
            dt_r[...] = joined
            dn_r[...] = mm(joined[:, 0:H], wdt[...])

        @pl.when(c < half_parts)
        def _():
            dn_r[...] += mm_rt(cz[0], wz[...]) + mm_rt(near_x[0], wx[...])

        @pl.when(c >= half_parts)
        def _():
            dn_r[...] += mm_rt(cz[0], wz[...]) + mm_rt(far_x[0], wx[...])

    def half_spec(array, first):
        def at(c, dev):
            if first:
                return (jnp.minimum(c, half_parts - 1), 0, 0)
            return (jnp.maximum(c - half_parts, 0), 0, 0)

        return (array, pl.BlockSpec((1,) + array.shape[1:], at))

    d_normed, cot_dt_all = run(
        input_backward,
        "input_backward",
        device,
        [
            chunked(cotz),
            half_spec(halves[0][0], True),
            half_spec(halves[1][0], False),
            whole(halves[0][1]),
            whole(halves[1][1]),
            columns(w_z, CH, chunk),
            columns(w_x, CH, chunk),
            whole(wdt_t),
        ],
        [out_whole((R, D), F32), out_whole((R, 128), BF16)],
        PARTS,
        us=3.0,
    )

    small_rows = -(-(NB + H + 16) // 16) * 16

    def maps_backward(
        dev, own, pre_r, pbc_r, cols_r, tbc, n_r, wbc, dn_r, cdt, cg0, cg1, hg0, hg1, gg, *refs
    ):
        others, hid, refs = refs[: S - 1], refs[S - 1 : 2 * S - 1], refs[2 * S - 1 :]
        kept, refs = refs[: S - 1], refs[S - 1 :]
        dn_own, pack_r = refs[0], refs[1]
        sends = refs[2 : 1 + S]
        cot_s, dn_s = refs[1 + S :]
        pack_r[...] = jnp.zeros_like(pack_r)
        grads = [jnp.zeros((1, NB), F32) for _ in range(5)]
        for b in range(S):
            d_map = own[blocks[b], :]
            for other in others:
                d_map = d_map + other[blocks[b], :].astype(F32)
            before = pre_r[blocks[b], :]
            sig = jax.nn.sigmoid(before)
            d_pre = d_map * sig * (1.0 + before * (1.0 - sig))
            d_in, taps, total = conv_back(d_pre, pbc_r[blocks[b], :], tbc[...], cols_r[blocks[b], :])
            for i, grad in enumerate(taps + [total]):
                grads[i] = grads[i] + grad
            cot_s[blocks[b], :] = d_in.astype(BF16)
        dn_s[...] = dn_r[...] + mm_rt(cot_s[...], wbc[...])
        dn_own[...] = dn_s[blocks[0], :]
        gain_sum = jnp.zeros((1, D), F32)
        for b in range(S):
            x = hid[b][...].astype(F32)
            scale = lax.rsqrt(jnp.mean(x * x, axis=1, keepdims=True) + epsilon)
            part = dn_s[blocks[b], :]
            gain_sum = gain_sum + jnp.sum(part * (x * scale), axis=0, keepdims=True)
            if b > 0:
                sends[b - 1][:, 0:D] = part.astype(BF16)
                sends[b - 1][:, D : 2 * D] = kept[b - 1][...]
        pack_r[0:NB, :] = mm_lt(cot_s[...], n_r[...])
        pack_r[NB : NB + H, :] = mm_lt(cdt[...], n_r[...])[0:H]
        at = NB + H
        heads = jnp.zeros((8, 128), F32)
        for i in range(PARTS):
            heads = heads + from_part((hg0, hg1)[i // half_parts][i % half_parts], i, dev)
        pack_r[at + 6 : at + 9, 0:128] = heads[0:3]
        mine = part_of(dev)
        for m in range(PARTS):

            @pl.when(mine == m)
            def _():
                for i in range(PARTS):
                    cg = (cg0, cg1)[i // half_parts]
                    lanes = slice((m ^ i) * CH, ((m ^ i) + 1) * CH)
                    pack_r[at : at + 5, lanes] = cg[i % half_parts, 0:5]
                    pack_r[at + 5 : at + 6, lanes] = gg[i, 0:1]

        for i in range(5):
            pack_r[at + 9 + i : at + 10 + i, 0:NB] = grads[i]
        pack_r[at + 14 : at + 15, :] = gain_sum

    outs = run(
        maps_backward,
        "maps_backward",
        device,
        [
            whole(a)
            for a in (
                d_map_own,
                pre_bc,
                proj_bc,
                cols,
                conv_bc,
                normed,
                w_bc,
                d_normed,
                cot_dt_all,
                halves[0][2],
                halves[1][2],
                halves[0][3],
                halves[1][3],
                gate_grads,
                *d_map_other,
                *hidden,
                *out_sends,
            )
        ],
        [out_whole((T, D), F32), out_whole((small_rows, D), F32)]
        + [out_whole((T, 2 * D), BF16) for _ in range(1, S)],
        1,
        scratch=[pltpu.VMEM((R, NB), BF16), pltpu.VMEM((R, D), F32)],
        us=3.0,
    )
    dn_own, pack = outs[:2]
    dn_other = [exchange(outs[1 + j], "shard", j) for j in range(1, S)]

    def own_rows(dev, hid, cot, cols_r, rows_r, gain_r, dn_r, out_r, *refs):
        others, refs = refs[: S - 1], refs[S - 1 :]
        hidden_r, grad_r = refs
        used = cols_r[:, 0:1]
        x = hid[...].astype(F32)
        added = out_r[...]
        for other in others:
            added = added + other[:, D : 2 * D].astype(F32)
        hidden_r[...] = used * (x + rows_r[:, 0:1] * added)
        d_n = dn_r[...]
        for other in others:
            d_n = d_n + other[:, 0:D].astype(F32)
        scale = lax.rsqrt(jnp.mean(x * x, axis=1, keepdims=True) + epsilon)
        u = d_n * gain_r[...]
        dot = jnp.mean(u * x, axis=1, keepdims=True)
        grad_r[...] = used * cot[...].astype(F32) + scale * u - x * (scale * scale * scale * dot)

    hidden_out, grad_hidden = run(
        own_rows,
        "own_rows",
        device,
        [
            whole(hidden_in),
            whole(cotangent),
            (cols, pl.BlockSpec((T, 128), lambda *_: (0, 0))),
            (row_scale, pl.BlockSpec((T, 128), lambda *_: (0, 0))),
        ]
        + [whole(a) for a in (gain, dn_own, out_own, *dn_other)],
        [out_whole((T, D), F32), out_whole((T, D), F32)],
        1,
    )

    def split_specs(shape):
        half = spans // 2
        send = pl.BlockSpec((1,) + shape, lambda i, dev: (jnp.minimum(i, half - 1), 0, 0, 0))
        keep = pl.BlockSpec((1,) + shape, lambda i, dev: (jnp.maximum(i - half, 0), 0, 0, 0))
        return [
            (jax.ShapeDtypeStruct((half,) + shape, BF16), send),
            (jax.ShapeDtypeStruct((half,) + shape, F32), keep),
        ]

    def relative(i):
        half = spans // 2
        return jnp.where(i < half, 2 * i + 1, 2 * (i - half))

    def by_span(array):
        height = array.shape[0]
        return (array, pl.BlockSpec((height, DCH), lambda i, dev: (0, span_of(dev) ^ relative(i))))

    def store_split(value, slot, send_r, keep_r):
        i = pl.program_id(0)

        @pl.when(i < spans // 2)
        def _():
            send_r[0, slot] = value.astype(BF16)

        @pl.when(i >= spans // 2)
        def _():
            keep_r[0, slot] = value

    def pair_weight_grad(dev, *refs):
        both, cot, norm = refs[:PARTS], refs[PARTS : 2 * PARTS], refs[2 * PARTS : 3 * PARTS]
        value = jnp.zeros((CH, DCH), F32)
        other = jnp.zeros((CH, DCH), F32)
        for r in range(PARTS):
            value = value + mm_lt(both[r][:, 0:CH], cot[r][...])
            other = other + mm_lt(both[r][:, CH : 2 * CH], norm[r][...])
        store_split(value, 0, *refs[3 * PARTS :])
        store_split(other, 1, *refs[3 * PARTS :])

    def x_weight_grad(dev, *refs):
        value = jnp.zeros((CH, DCH), F32)
        for r in range(PARTS):
            value = value + mm_lt(refs[r][...], refs[PARTS + r][...])
        store_split(value, 0, *refs[2 * PARTS :])

    def sum_spans(send, keep):
        bit = PARTS
        total = keep + exchange(send, "rep", bit).astype(F32)
        while total.shape[0] > 1:
            bit *= 2
            send = total[1::2].astype(BF16)
            total = total[0::2] + exchange(send, "rep", bit).astype(F32)
        held = total.astype(BF16)
        while bit >= PARTS:
            held = jnp.concatenate([held, exchange(held, "rep", bit)], axis=0)
            bit //= 2
        far = exchange(held, "rep", 2)
        return [held, exchange(held, "rep", 1), far, exchange(far, "rep", 1)]

    def reversed_bits(i):
        result = jnp.int32(0) * i
        count = spans.bit_length() - 1
        for b in range(count):
            result = result | (((i >> b) & 1) << (count - 1 - b))
        return result

    def in_spec(name=None):
        def at(i, dev):
            return (span_of(dev) ^ reversed_bits(i), 0)

        return (jax.ShapeDtypeStruct((D, C), F32), pl.BlockSpec((DCH, C), at))

    def out_spec():
        def at(i, dev):
            return (0, span_of(dev) ^ reversed_bits(i))

        return (jax.ShapeDtypeStruct((C, D), F32), pl.BlockSpec((C, DCH), at))

    def join_pair(dev, *refs):
        mine = part_of(dev)
        for m in range(PARTS):

            @pl.when(mine == m)
            def _():
                for r in range(PARTS):
                    at = slice((m ^ r) * CH, ((m ^ r) + 1) * CH)
                    refs[PARTS][at, :] = refs[r][0, 0].astype(F32)
                    refs[PARTS + 1][:, at] = refs[r][0, 1].astype(F32).T

    def join_x(dev, *refs):
        mine = part_of(dev)
        for m in range(PARTS):

            @pl.when(mine == m)
            def _():
                for r in range(PARTS):
                    at = slice((m ^ r) * CH, ((m ^ r) + 1) * CH)
                    refs[PARTS][:, at] = refs[r][0, 0].astype(F32).T

    send, keep = run(
        pair_weight_grad,
        "pair_weight_grad",
        device,
        [whole(b) for b in both_q]
        + [by_span(c) for c in cots_all]
        + [by_span(n) for n in normed_all],
        split_specs((2, CH, DCH)),
        spans,
        us=5.0,
    )
    pieces = sum_spans(send, keep)
    grad_out, grad_z = run(
        join_pair,
        "join_pair",
        device,
        [chunked(p) for p in pieces],
        [out_spec(), in_spec()],
        spans,
        us=6.0,
    )
    send, keep = run(
        x_weight_grad,
        "x_weight_grad",
        device,
        [whole(c) for c in cotx_q] + [by_span(n) for n in normed_all],
        split_specs((1, CH, DCH)),
        spans,
        us=2.5,
    )
    pieces = sum_spans(send, keep)
    (grad_x,) = run(
        join_x,
        "join_x",
        device,
        [chunked(p) for p in pieces],
        [in_spec()],
        spans,
        us=4.0,
    )

    bit = 1
    while bit < replicas:
        rounded = pack.astype(BF16)
        pack = rounded.astype(F32) + exchange(rounded, "rep", bit).astype(F32)
        bit *= 2

    def unpack(dev, pack_r, *refs):
        at = NB + H
        refs[0][...] = pack_r[0:NB, :].T
        refs[1][...] = pack_r[NB:at, :]
        refs[2][...] = pack_r[at : at + 4, 0:C]
        refs[3][...] = pack_r[at + 9 : at + 13, 0:NB]
        refs[4][...] = pack_r[at + 4 : at + 5, 0:C]
        refs[5][...] = pack_r[at + 13 : at + 14, 0:NB]
        for i in range(3):
            refs[6 + i][...] = pack_r[at + 6 + i : at + 7 + i, 0:H]
        refs[9][...] = pack_r[at + 5 : at + 6, 0:C]
        me = me_of(dev)
        for m in range(S):

            @pl.when(me == m)
            def _():
                for j in range(S):
                    lanes = slice((m ^ j) * (D // S), ((m ^ j) + 1) * (D // S))
                    refs[10 + j][...] = pack_r[at + 14 : at + 15, lanes]

    outs = run(
        unpack,
        "unpack",
        device,
        [whole(pack)],
        [
            out_whole(shape, F32)
            for shape in [(D, NB), (H, D), (4, C), (4, NB), (1, C), (1, NB)]
            + [(1, H)] * 3
            + [(1, C)]
            + [(1, D // S)] * S
        ],
        1,
        us=1.5,
    )
    grad_bc, grad_dt, grad_conv_x, grad_conv_bc, grad_bias_x, grad_bias_bc = outs[:6]
    heads, grad_gate = outs[6:9], outs[9]
    grad_gain = outs[10]
    for j in range(1, S):
        grad_gain = grad_gain + exchange(outs[10 + j], "shard", j)
    return (
        hidden_out,
        grad_hidden,
        grad_gain,
        grad_z[None],
        grad_x[None],
        grad_bc[None],
        grad_dt.T[None],
        grad_conv_x[None],
        grad_conv_bc[None],
        grad_bias_x,
        grad_bias_bc,
        *heads,
        grad_gate,
        grad_out[None],
    )
```

```python
from functools import partial

import jax
import jax.numpy as jnp
import numpy as np
from jax import lax
from jax.experimental import pallas as pl
from jax.experimental.pallas import tpu as pltpu
from jax.sharding import PartitionSpec as P

epsilon = 1e-05
PARTS = 4
F32 = jnp.float32
BF16 = jnp.bfloat16
VM = 1.5
UNIT = 3e9


def exchange(array, axis, bit):
    count = lax.axis_size(axis)
    return lax.ppermute(array, axis, [(i, i ^ bit) for i in range(count)])


def mm(left, right):
    return lax.dot_general(left, right, (((1,), (0,)), ((), ())), preferred_element_type=F32)


def mm_rt(left, right):
    return lax.dot_general(left, right, (((1,), (1,)), ((), ())), preferred_element_type=F32)


def mm_lt(left, right):
    return lax.dot_general(left, right, (((0,), (0,)), ((), ())), preferred_element_type=F32)


def whole(array):
    zeros = (0,) * array.ndim
    return (array, pl.BlockSpec(array.shape, lambda *_: zeros))


def chunked(array, start=0):
    tail = (0,) * (array.ndim - 1)
    return (array, pl.BlockSpec((1,) + array.shape[1:], lambda c, dev: (c + start,) + tail))


def columns(array, width, at):
    if width % 128 == 0:
        return (array, pl.BlockSpec((array.shape[0], width), lambda c, dev: (0, at(c, dev))))
    pieces = array.reshape(array.shape[0], -1, width).transpose(1, 0, 2)
    spec = pl.BlockSpec((None, array.shape[0], width), lambda c, dev: (at(c, dev), 0, 0))
    return (pieces, spec)


def rows(array, height, at):
    return (array, pl.BlockSpec((height, array.shape[1]), lambda c, dev: (at(c, dev), 0)))


def split(value):
    high = value.astype(BF16)
    return high, (value - high.astype(F32)).astype(BF16)


def spread(value, pattern):
    high, low = split(value)
    return mm(high, pattern) + mm(low, pattern)


def out_whole(shape, dtype):
    zeros = (0,) * len(shape)
    return (jax.ShapeDtypeStruct(shape, dtype), pl.BlockSpec(shape, lambda *_: zeros))


def out_chunked(shape, dtype):
    tail = (0,) * (len(shape) - 1)
    spec = pl.BlockSpec((1,) + shape[1:], lambda c, dev: (c,) + tail)
    return (jax.ShapeDtypeStruct(shape, dtype), spec)


def run(body, name, device, ins, outs, steps, scratch=(), us=1.0, pull=False):
    total = sum(a.size * a.dtype.itemsize for a, _ in ins)
    total += sum(s.size * s.dtype.itemsize for s, _ in outs)
    held = 0
    for array, spec in list(ins) + list(outs):
        size = array.dtype.itemsize
        for extent in spec.block_shape:
            size *= extent or 1
        held += size * (1 if size == array.size * array.dtype.itemsize else 2)
    for buffer in scratch:
        held += buffer.dtype.itemsize * int(np.prod(buffer.shape))
    if pull:
        count, inner = len(ins), body
        scratch = (
            [pltpu.VMEM(a.shape, a.dtype) for a, _ in ins]
            + [pltpu.SemaphoreType.DMA((count,))]
            + list(scratch)
        )
        ins = [(a, pl.BlockSpec(memory_space=pltpu.HBM)) for a, _ in ins]

        def body(dev, *refs):
            held = refs[count + len(outs) :]
            copies = [
                pltpu.make_async_copy(refs[i], held[i], held[count].at[i]) for i in range(count)
            ]
            for copy in copies:
                copy.start()
            for copy in copies:
                copy.wait()
            inner(dev, *held[:count], *refs[count : count + len(outs)], *held[count + 1 :])

    return pl.pallas_call(
        body,
        name=name,
        out_shape=[shape for shape, _ in outs],
        grid_spec=pltpu.PrefetchScalarGridSpec(
            num_scalar_prefetch=1,
            grid=(steps,),
            in_specs=[spec for _, spec in ins],
            out_specs=[spec for _, spec in outs],
            scratch_shapes=list(scratch),
        ),
        compiler_params=pltpu.CompilerParams(
            dimension_semantics=("arbitrary",),
            vmem_limit_bytes=int(held * VM) + (3 << 20),
        ),
        cost_estimate=pl.CostEstimate(
            flops=int(us * UNIT), bytes_accessed=total, transcendentals=0
        ),
    )(device, *[a for a, _ in ins])


def iota(shape, dim):
    return lax.broadcasted_iota(jnp.int32, shape, dim)


def roll_rows(array, shift):
    if array.shape[1] % 128 == 0:
        return pltpu.roll(array, shift % array.shape[0], 0)
    return jnp.roll(array, shift, 0)


def conv_rows(inputs, taps, bias, marks):
    result = bias + taps[3:4] * inputs
    for offset in range(1, 4):
        shifted = roll_rows(inputs, offset) * marks[:, offset : offset + 1]
        result = result + taps[3 - offset : 4 - offset] * shifted
    return result


def conv_back(d_out, inputs, taps, marks):
    d_in = taps[3:4] * d_out
    grads = [None] * 4
    grads[3] = jnp.sum(d_out * inputs, axis=0, keepdims=True)
    for offset in range(1, 4):
        kept = d_out * marks[:, offset : offset + 1]
        d_in = d_in + taps[3 - offset : 4 - offset] * roll_rows(kept, -offset)
        grads[3 - offset] = jnp.sum(kept * roll_rows(inputs, offset), axis=0, keepdims=True)
    return d_in, grads, jnp.sum(d_out, axis=0, keepdims=True)


def softplus(value):
    return jnp.maximum(value, 0.0) + jnp.log1p(jnp.exp(-jnp.abs(value)))


def solution(mesh):
    members = mesh.shape["shard"]
    replicas = mesh.shape["rep"]
    assert replicas % PARTS == 0 and replicas // PARTS >= 2
    assert replicas & (replicas - 1) == 0 and members & (members - 1) == 0
    return jax.shard_map(
        partial(on_device, members, replicas),
        mesh=mesh,
        in_specs=(
            P(("rep", "shard"), None),
            P(("rep", "shard"), None),
            P(None, "shard"),
            P(None, None, "shard"),
            P(None, None, "shard"),
            P(None, None, "shard"),
            P(None, None, "shard"),
            P(None, None, "shard"),
            P(None, None, "shard"),
            P(None, "shard"),
            P(None, "shard"),
            P(None, "shard"),
            P(None, "shard"),
            P(None, "shard"),
            P(None, "shard"),
            P(None, "shard", None),
            P(),
            P(),
            P(),
        ),
        out_specs=(
            P(("rep", "shard"), None),
            P(("rep", "shard"), None),
            P(None, "shard"),
            P(None, None, "shard"),
            P(None, None, "shard"),
            P(None, None, "shard"),
            P(None, None, "shard"),
            P(None, None, "shard"),
            P(None, None, "shard"),
            P(None, "shard"),
            P(None, "shard"),
            P(None, "shard"),
            P(None, "shard"),
            P(None, "shard"),
            P(None, "shard"),
            P(None, "shard", None),
        ),
        check_vma=False,
    )


def on_device(
    members,
    replicas,
    hidden_in,
    cotangent,
    norm_gain,
    w_z,
    w_x,
    w_bc,
    w_dt,
    conv_x,
    conv_bc,
    bias_x,
    bias_bc,
    dt_bias,
    a_log,
    d_skip,
    gate_gain,
    w_out,
    seq_len,
    seq_owner,
    seq_start,
):
    S = members
    T, D = hidden_in.shape
    R = S * T
    C = w_z.shape[2]
    H = w_dt.shape[2]
    NB = w_bc.shape[2]
    CH = C // PARTS
    HC = H // PARTS
    HS = C // H
    inner = C * S
    spans = replicas // PARTS
    DCH = D // spans
    w_z, w_x, w_bc, w_dt, w_out = w_z[0], w_x[0], w_bc[0], w_dt[0], w_out[0]

    shard_at = lax.axis_index("shard")
    device = (lax.axis_index("rep") * S + shard_at).astype(jnp.int32).reshape(1)

    def me_of(dev):
        return lax.rem(dev[0], S)

    def part_of(dev):
        return lax.rem(lax.div(dev[0], S), PARTS)

    def span_of(dev):
        return lax.div(dev[0], S * PARTS)

    blocks = [slice(b * T, (b + 1) * T) for b in range(S)]

    hidden = [hidden_in] + [exchange(hidden_in, "shard", j) for j in range(1, S)]

    lens = seq_len.reshape(1, -1)
    owners = seq_owner.reshape(1, -1)
    starts = seq_start.reshape(1, -1)
    records = lens.shape[1]
    wdt_t = w_dt.T
    conv_x, conv_bc = conv_x[0], conv_bc[0]

    def chunk(c, dev):
        return part_of(dev) ^ c

    def to_part(value, c, dev):
        return pltpu.roll(value, lax.rem(128 - chunk(c, dev) * HC, 128), 1)

    def from_part(value, c, dev):
        return pltpu.roll(value, chunk(c, dev) * HC, 1)

    def head_pattern():
        return jnp.where(iota((128, CH), 0) == iota((128, CH), 1) // HS, 1.0, 0.0).astype(BF16)

    def head_pattern_t():
        return jnp.where(iota((CH, 128), 0) // HS == iota((CH, 128), 1), 1.0, 0.0).astype(BF16)

    def pad_lanes(value):
        gap = jnp.zeros((value.shape[0], 128 - value.shape[1]), F32)
        return jnp.concatenate([value, gap], axis=1)

    group = min(2, HC)
    width = group * HS

    def head_masks():
        lane = iota((1, width), 1) // HS
        return [jnp.where(lane == g, 1.0, 0.0) for g in range(group)]

    def segments(dev, ln, ow, st, hid, cot, *refs):
        given, refs = refs[:4], refs[4:]
        mask_r, cols_r, mine_r, cot_r = refs[:4]
        for source, target in zip(given, refs[4:]):
            target[...] = source[...]
        mine_r[:, 0:D] = hid[...]
        mine_r[:, D : 2 * D] = cot[...]
        cot_r[...] = cot[...]
        me = me_of(dev)
        base = dev[0] - me
        lane = iota((T, 128), 1)
        row = iota((T, 128), 0)
        slot = iota((T, records), 0)
        ids = iota((T, records), 1).astype(F32)
        for b in range(S):
            covers = (
                (ow[...] == base + (me ^ b)) & (slot >= st[...]) & (slot < st[...] + ln[...])
            )
            used = jnp.sum(jnp.where(covers, 1.0, 0.0), axis=1, keepdims=True)
            found = jnp.sum(jnp.where(covers, ids, 0.0), axis=1, keepdims=True)
            lone = (records + row).astype(F32)
            seg = jnp.where(used > 0.5, found, lone)
            same = (seg == seg.T) & (row >= lane)
            mask_r[blocks[b], :] = jnp.where(same, 1.0, 0.0)
            cols = jnp.where(lane == 0, used, 0.0)
            for offset in range(1, 4):
                mark = (pltpu.roll(seg, offset, 0) == seg) & (row >= offset)
                cols = jnp.where(lane == offset, jnp.where(mark, 1.0, 0.0), cols)
            cols_r[blocks[b], :] = cols

    mask, cols, mine_rows, cot_own, own_gain, bc_weight, bc_taps, bc_bias = run(
        segments,
        "segments",
        device,
        [
            whole(a)
            for a in (
                lens,
                owners,
                starts,
                hidden_in,
                cotangent,
                norm_gain,
                w_bc,
                conv_bc,
                bias_bc,
            )
        ],
        [
            out_whole((R, 128), F32),
            out_whole((R, 128), F32),
            out_whole((T, 2 * D), BF16),
            out_whole((T, D), BF16),
            out_whole(norm_gain.shape, F32),
            out_whole(w_bc.shape, BF16),
            out_whole(conv_bc.shape, F32),
            out_whole(bias_bc.shape, F32),
        ],
        1,
        us=1.5,
        pull=True,
    )
    if S == 2:
        gains = [own_gain, exchange(own_gain, "shard", 1)]
    else:
        gains = [lax.all_gather(own_gain, "shard", axis=1, tiled=True)]
    far_rows = [exchange(mine_rows, "rep", 2)]

    def prepare(dev, wbc, tbc, bbc, cols_r, cot, *refs):
        parts, refs = refs[: len(gains)], refs[len(gains) :]
        hid, refs = refs[:S], refs[S:]
        gain_r, normed_r, pbc_r, pre_r, map_r, cot_r = refs[:6]
        sends = refs[6:]
        me = me_of(dev)
        if S == 2:
            low, high = parts[0][...], parts[1][...]
            first = me == 0
            gain_r[...] = jnp.concatenate(
                [jnp.where(first, low, high), jnp.where(first, high, low)], axis=1
            )
        else:
            gain_r[...] = parts[0][...]
        for b in range(S):
            x = hid[b][...].astype(F32)
            scale = lax.rsqrt(jnp.mean(x * x, axis=1, keepdims=True) + epsilon)
            normed_r[blocks[b], :] = (x * scale * gain_r[...]).astype(BF16)
        pbc_r[...] = mm(normed_r[...], wbc[...])
        for b in range(S):
            marks = cols_r[blocks[b], :]
            pre = conv_rows(pbc_r[blocks[b], :], tbc[...], bbc[...], marks)
            pre_r[blocks[b], :] = pre
            out = (pre * jax.nn.sigmoid(pre)).astype(BF16)
            map_r[blocks[b], :] = out
            for j in range(1, S):
                sends[j - 1][blocks[b ^ j], :] = out
        cot_r[...] = cot[...]

    outs = run(
        prepare,
        "norm_and_maps",
        device,
        [whole(a) for a in (bc_weight, bc_taps, bc_bias, cols, cot_own, *gains, *hidden)],
        [
            out_whole((1, D), F32),
            out_whole((R, D), BF16),
            out_whole((R, NB), F32),
            out_whole((R, NB), F32),
            out_whole((R, NB), BF16),
            out_whole((T, D), BF16),
        ]
        + [out_whole((R, NB), BF16) for _ in range(1, S)],
        1,
        us=1.0,
    )
    gain, normed, proj_bc, pre_bc, map_own, cot_own = outs[:6]
    maps = [map_own] + [exchange(outs[5 + j], "shard", j) for j in range(1, S)]
    if S == 2:
        map_a, map_b = maps
    else:
        map_a = jnp.concatenate(maps[: S // 2], axis=1)
        map_b = jnp.concatenate(maps[S // 2 :], axis=1)
    cots = [cot_own] + [exchange(cot_own, "shard", j) for j in range(1, S)]

    def project(dev, n_r, wz, wx, wdt, dtb, alog, dsk, tx, bx, cols_r, *refs):
        z_r, x_r, pre_r, y_r, cum_r, cumt_r, hp_r, sk_r = refs[:8]
        y_s, cum_s = refs[8:]
        c = pl.program_id(0)
        n = n_r[...]

        @pl.when(c == 0)
        def _():
            y_s[...] = pad_lanes(mm_rt(n, wdt[...]) + dtb[...])
            row = iota((T, 128), 0)
            rate = jnp.exp(pad_lanes(alog[...]))
            for b in range(S):
                total = -softplus(y_s[blocks[b], :]) * rate
                shift = 1
                while shift < T:
                    total = total + jnp.where(row >= shift, pltpu.roll(total, shift, 0), 0.0)
                    shift *= 2
                cum_s[blocks[b], :] = total

        z_r[0] = mm(n, wz[...])
        x_r[0] = mm(n, wx[...])
        y_r[0] = to_part(y_s[...], c, dev)
        turned = to_part(cum_s[...], c, dev)
        cum_r[0] = turned
        pair = jnp.concatenate(
            [pad_lanes(alog[...]), pad_lanes(dsk[...]), jnp.zeros((6, 128), F32)], axis=0
        )
        pair = to_part(pair, c, dev)
        hp_r[0] = jnp.exp(pair)
        skips = [jnp.broadcast_to(pair[1:2, h : h + 1], (1, HS)) for h in range(HC)]
        sk_r[0] = jnp.broadcast_to(jnp.concatenate(skips, axis=1), (8, CH))
        for b in range(S):
            marks = cols_r[blocks[b], :]
            pre_r[0, blocks[b], :] = conv_rows(x_r[0, blocks[b], :], tx[...], bx[...], marks)
            cumt_r[0, b] = turned[blocks[b]].T[0:8]

    z, px, pre, y, cum, cum_t, head_rows, skip_rows = run(
        project,
        "projections",
        device,
        [
            whole(normed),
            columns(w_z, CH, chunk),
            columns(w_x, CH, chunk),
            whole(wdt_t),
            whole(dt_bias),
            whole(a_log),
            whole(d_skip),
            columns(conv_x, CH, chunk),
            columns(bias_x, CH, chunk),
            whole(cols),
        ],
        [
            out_chunked((PARTS, R, CH), F32),
            out_chunked((PARTS, R, CH), F32),
            out_chunked((PARTS, R, CH), F32),
            out_chunked((PARTS, R, 128), F32),
            out_chunked((PARTS, R, 128), F32),
            out_chunked((PARTS, S, 8, 128), F32),
            out_chunked((PARTS, 8, 128), F32),
            out_chunked((PARTS, 8, CH), F32),
        ],
        PARTS,
        scratch=[pltpu.VMEM((R, 128), F32), pltpu.VMEM((R, 128), F32)],
        us=4.0,
    )
    def fill_scores(dev, a_r, b_r, mask_r, scores):
        a_is_key = me_of(dev) < S // 2
        for b in range(S):

            @pl.when(a_is_key)
            def _():
                scores[b] = mm_rt(b_r[blocks[b], :], a_r[blocks[b], :]) * mask_r[blocks[b], :]

            @pl.when(jnp.logical_not(a_is_key))
            def _():
                scores[b] = mm_rt(a_r[blocks[b], :], b_r[blocks[b], :]) * mask_r[blocks[b], :]

    def scan_forward(
        dev, a_r, b_r, mask_r, pre_r, y_r, cum_r, cumt_r, sk, gg, z_r, wo, *refs
    ):
        core_r, sums, own_r = refs[0], refs[1], refs[2]
        sends = refs[3 : 2 + S]
        scores, acc, gated_s = refs[2 + S :]
        c = pl.program_id(0)

        @pl.when(c == 0)
        def _():
            fill_scores(dev, a_r, b_r, mask_r, scores)
            acc[...] = jnp.zeros_like(acc)
            sums[...] = jnp.zeros_like(sums)

        lane = iota((T, 128), 1)
        pattern = head_pattern()
        masks = head_masks()
        for b in range(S):
            before = pre_r[0, blocks[b], :]
            values = before * jax.nn.sigmoid(before)
            step = spread(softplus(y_r[0, blocks[b], :]), pattern)
            scaled = (values * step).astype(BF16)
            parts = []
            for first in range(0, HC, group):
                at = slice(first * HS, first * HS + width)
                weights = []
                for h in range(first, first + group):
                    gap = cum_r[0, blocks[b], h : h + 1] - cumt_r[0, b, h : h + 1, :]
                    weights.append(
                        (scores[b] * jnp.exp(jnp.minimum(gap, 0.0))).astype(BF16)
                    )
                stacked = [scaled[:, at] * m.astype(BF16) for m in masks]
                parts.append(
                    mm(jnp.concatenate(weights, axis=1), jnp.concatenate(stacked, axis=0))
                )
            core = jnp.concatenate(parts, axis=1) + values * sk[0, 0:1]
            core_r[0, blocks[b], :] = core
            zed = z_r[0, blocks[b], :]
            gated = core * (zed * jax.nn.sigmoid(zed))
            gained = gated * gg[...]
            gated_s[blocks[b], :] = gained.astype(BF16)
            squares = jnp.sum(gated * gated, axis=1, keepdims=True)
            sums[blocks[b], :] += jnp.where(lane == 0, squares, 0.0)
        acc[...] += mm(gated_s[...], wo[...])

        @pl.when(c == PARTS - 1)
        def _():
            own_r[...] = acc[blocks[0], :]
            for j in range(1, S):
                sends[j - 1][...] = acc[blocks[j], :].astype(BF16)

    outs = run(
        scan_forward,
        "scan_forward",
        device,
        [
            whole(map_a),
            whole(map_b),
            whole(mask),
            chunked(pre),
            chunked(y),
            chunked(cum),
            chunked(cum_t),
            chunked(skip_rows),
            columns(gate_gain, CH, chunk),
            chunked(z),
            rows(w_out, CH, chunk),
        ],
        [
            out_chunked((PARTS, R, CH), F32),
            out_whole((R, 128), F32),
            out_whole((T, D), F32),
        ]
        + [out_whole((T, D), BF16) for _ in range(1, S)],
        PARTS,
        scratch=[
            pltpu.VMEM((S, T, T), F32),
            pltpu.VMEM((R, D), F32),
            pltpu.VMEM((R, CH), BF16),
        ],
        us=4.0,
    )
    core, squares, out_own = outs[:3]
    out_sends = outs[3:]

    def mixed_backward(dev, core_r, z_r, gg, cols_r, squares_r, wo, *refs):
        cot, refs = refs[:S], refs[S:]
        dm_r, sums_r = refs[0], refs[1]
        sends, sums = refs[2 : 1 + S], refs[1 + S]
        c = pl.program_id(0)
        lane = iota((T, 128), 1)

        @pl.when(c == 0)
        def _():
            sums[...] = squares_r[...]

        for b in range(S):
            d_mixed = mm_rt(cot[b][...], wo[...]) * cols_r[blocks[b], 0:1]
            dm_r[0, blocks[b], :] = d_mixed
            zed = z_r[0, blocks[b], :]
            gated = core_r[0, blocks[b], :] * (zed * jax.nn.sigmoid(zed))
            dots = jnp.sum(d_mixed * (gated * gg[...]), axis=1, keepdims=True)
            sums[blocks[b], :] += jnp.where(lane == 1, dots, 0.0)

        @pl.when(c == PARTS - 1)
        def _():
            for b in range(S):
                turned = sums[blocks[b], :].T[0:8]
                sums_r[:, blocks[b]] = turned
                for j in range(1, S):
                    sends[j - 1][:, blocks[b ^ j]] = turned

    outs = run(
        mixed_backward,
        "mixed_backward",
        device,
        [
            chunked(core),
            chunked(z),
            columns(gate_gain, CH, chunk),
            whole(cols),
            whole(squares),
            rows(w_out, CH, chunk),
        ]
        + [whole(c) for c in cots],
        [out_chunked((PARTS, R, CH), F32), out_whole((8, R), F32)]
        + [out_whole((8, R), F32) for _ in range(1, S)],
        PARTS,
        scratch=[pltpu.VMEM((R, 128), F32)],
        us=1.6,
    )
    d_mixed, sums_own = outs[:2]
    sums_all = [sums_own] + [exchange(outs[1 + j], "shard", j) for j in range(1, S)]

    def gate_backward(dev, core_r, z_r, dm_r, gg, cols_r, *refs):
        parts, refs = refs[:S], refs[S:]
        both_r = refs[:PARTS]
        cotz_c, dcore_r, gg_r, rows_r = refs[PARTS:]
        c = pl.program_id(0)
        lane = iota((T, 128), 1)

        @pl.when(c == 0)
        def _():
            for b in range(S):
                total = parts[0][:, blocks[b]]
                for j in range(1, S):
                    total = total + parts[j][:, blocks[b]]
                turned = jnp.concatenate([total, jnp.zeros((T - 8, 128), F32)], axis=0).T
                inverse = lax.rsqrt(turned[:, 0:1] / inner + epsilon)
                factor = inverse * inverse * inverse * turned[:, 1:2] / inner
                rows_r[blocks[b], :] = jnp.where(
                    lane == 0, inverse, jnp.where(lane == 1, factor, 0.0)
                )

        gate_sum = jnp.zeros((1, CH), F32)
        mixed_parts, cot_parts = [], []
        for b in range(S):
            inverse = rows_r[blocks[b], 0:1]
            factor = rows_r[blocks[b], 1:2]
            used = cols_r[blocks[b], 0:1]
            core = core_r[0, blocks[b], :]
            zed = z_r[0, blocks[b], :]
            sig = jax.nn.sigmoid(zed)
            gated = core * (zed * sig)
            d_mixed = dm_r[0, blocks[b], :]
            scaled = gated * inverse
            gate_sum = gate_sum + jnp.sum(d_mixed * scaled, axis=0, keepdims=True)
            d_gated = inverse * (d_mixed * gg[...]) - gated * factor
            dcore_r[0, blocks[b], :] = (d_gated * (zed * sig)).astype(BF16)
            d_z = d_gated * core * sig * (1.0 + zed * (1.0 - sig))
            mixed_parts.append((scaled * gg[...] * used).astype(BF16))
            cot_parts.append(d_z.astype(BF16))
            cotz_c[0, blocks[b], :] = cot_parts[b]
        gg_r[0] = jnp.broadcast_to(gate_sum, (8, CH))
        for r in range(PARTS):

            @pl.when(c == r)
            def _():
                for b in range(S):
                    both_r[r][blocks[b], 0:CH] = mixed_parts[b]
                    both_r[r][blocks[b], CH : 2 * CH] = cot_parts[b]

    outs = run(
        gate_backward,
        "gate_backward",
        device,
        [chunked(core), chunked(z), chunked(d_mixed), columns(gate_gain, CH, chunk), whole(cols)]
        + [whole(s) for s in sums_all],
        [out_whole((R, 2 * CH), BF16) for _ in range(PARTS)]
        + [
            out_chunked((PARTS, R, CH), BF16),
            out_chunked((PARTS, R, CH), BF16),
            out_chunked((PARTS, 8, CH), F32),
            out_whole((R, 128), F32),
        ],
        PARTS,
        us=2.2,
    )
    cotz, d_core, gate_grads, row_scale = outs[PARTS:]
    both_q = [outs[0]] + [exchange(outs[r], "rep", r) for r in range(1, PARTS)]

    far_rows = far_rows + [exchange(far_rows[0], "shard", j) for j in range(1, S)]

    def plane_rows(dev, gain_r, n_r, *refs):
        cot, far, out_r = refs[:S], refs[S : 2 * S], refs[2 * S]
        out_r[0:R, 0:D] = n_r[...]
        for b in range(S):
            out_r[blocks[b], D : 2 * D] = cot[b][...]
            x = far[b][:, 0:D].astype(F32)
            scale = lax.rsqrt(jnp.mean(x * x, axis=1, keepdims=True) + epsilon)
            at = slice(R + b * T, R + (b + 1) * T)
            out_r[at, 0:D] = (x * scale * gain_r[...]).astype(BF16)
            out_r[at, D : 2 * D] = far[b][:, D : 2 * D]

    (plane,) = run(
        plane_rows,
        "plane_rows",
        device,
        [whole(a) for a in (gain, normed, *cots, *far_rows)],
        [out_whole((2 * R, 2 * D), BF16)],
        1,
        us=1.0,
    )
    planes = [plane, exchange(plane, "rep", 1)]

    half_parts = PARTS // 2

    def scan_backward(
        last, dev, a_r, b_r, mask_r, pre_r, px_r, y_r, cum_r, cumt_r, hp, sk, tx, core_r, dcore_r,
        cols_r, *refs
    ):
        if last:
            d_before, refs = refs[0], refs[1:]
        cotx_r, refs = refs[:half_parts], refs[half_parts:]
        cotx_c, cdt_r, cg_r, hg_r = refs[:4]
        if last:
            own_r, sends = refs[4], refs[5 : 4 + S]
            scores, scores_t, d_scores = refs[4 + S :]
        else:
            d_scores, scores, scores_t = refs[4:]
        c = pl.program_id(0)

        @pl.when(c == 0)
        def _():
            fill_scores(dev, a_r, b_r, mask_r, scores)
            for b in range(S):
                scores_t[b] = scores[b].T
            d_scores[...] = d_before[...] if last else jnp.zeros_like(d_scores)

        row = iota((T, 128), 0)
        lane = iota((T, 128), 1)
        pattern = head_pattern()
        pattern_t = head_pattern_t()
        masks = [m.astype(BF16) for m in head_masks()]
        tap_grads = [jnp.zeros((1, CH), F32) for _ in range(6)]
        bias_grad = jnp.zeros((1, 128), F32)
        rate_grad = jnp.zeros((1, 128), F32)
        cot_parts = []
        rate = hp[0, 0:1, :]
        for b in range(S):
            before = pre_r[0, blocks[b], :]
            sig = jax.nn.sigmoid(before)
            values = before * sig
            raw = y_r[0, blocks[b], :]
            step = softplus(raw)
            step_full = spread(step, pattern)
            scaled = (values * step_full).astype(BF16)
            d_out = dcore_r[0, blocks[b], :]
            d_scaled = []
            for first in range(0, HC, group):
                at = slice(first * HS, first * HS + width)
                stacked = jnp.concatenate([d_out[:, at] * m for m in masks], axis=0)
                d_weights = mm_rt(stacked, scaled[:, at])
                turned, change = [], None
                for g in range(group):
                    h = first + g
                    gap = cum_r[0, blocks[b], h : h + 1] - cumt_r[0, b, h : h + 1, :]
                    turned.append((scores_t[b] * jnp.exp(jnp.minimum(-gap, 0.0))).astype(BF16))
                    term = d_weights[g * T : (g + 1) * T] * jnp.exp(jnp.minimum(gap, 0.0))
                    change = term if change is None else change + term
                d_scores[b] += change
                d_scaled.append(mm(jnp.concatenate(turned, axis=1), stacked))
            d_scaled = jnp.concatenate(d_scaled, axis=1)
            d_out = d_out.astype(F32)
            plain = core_r[0, blocks[b], :] - values * sk[0, 0:1]
            d_cum = spread(d_out * plain - d_scaled * scaled.astype(F32), pattern_t)
            d_step = spread(d_scaled * values, pattern_t)
            shift = 1
            while shift < T:
                d_cum = d_cum + jnp.where(row < T - shift, pltpu.roll(d_cum, T - shift, 0), 0.0)
                shift *= 2
            rate_grad = rate_grad - jnp.sum(d_cum * step, axis=0, keepdims=True) * rate
            d_raw = (d_step - d_cum * rate) * jax.nn.sigmoid(raw)
            d_raw = jnp.where(lane < HC, d_raw, 0.0)
            bias_grad = bias_grad + jnp.sum(d_raw, axis=0, keepdims=True)
            cdt_r[0, blocks[b], :] = d_raw
            d_val = d_scaled * step_full + d_out * sk[0, 0:1]
            d_pre = d_val * sig * (1.0 + before * (1.0 - sig))
            d_in, grads, total = conv_back(
                d_pre, px_r[0, blocks[b], :], tx[...], cols_r[blocks[b], :]
            )
            skip = jnp.sum(d_out * values, axis=0, keepdims=True)
            for i, grad in enumerate(grads + [total, skip]):
                tap_grads[i] = tap_grads[i] + grad
            cot_parts.append(d_in.astype(BF16))
            cotx_c[0, blocks[b], :] = cot_parts[b]
        cg_r[0] = jnp.concatenate(tap_grads + [jnp.zeros((2, CH), F32)], axis=0)
        high, low = split(jnp.broadcast_to(tap_grads[5], (8, CH)))
        skip_grad = mm(high, pattern_t) + mm(low, pattern_t)
        hg_r[0] = jnp.concatenate(
            [bias_grad, rate_grad, skip_grad[0:1], jnp.zeros((5, 128), F32)], axis=0
        )
        for r in range(half_parts):

            @pl.when(c == r)
            def _():
                for b in range(S):
                    cotx_r[r][blocks[b], :] = cot_parts[b]

        if last:

            @pl.when(c == half_parts - 1)
            def _():
                a_is_key = me_of(dev) < S // 2

                def finish(key_first):
                    for b in range(S):
                        d_s = (d_scores[b] * mask_r[blocks[b], :]).astype(BF16)
                        a, bb = a_r[blocks[b], :], b_r[blocks[b], :]
                        if key_first:
                            both = (mm_lt(d_s, bb), mm(d_s, a))
                        else:
                            both = (mm(d_s, bb), mm_lt(d_s, a))
                        for j in range(S):
                            half = both[0] if j < S // 2 else both[1]
                            at = (j % (S // 2)) * NB
                            piece = half[:, at : at + NB]
                            if j == 0:
                                own_r[blocks[b], :] = piece
                            else:
                                sends[j - 1][blocks[b ^ j], :] = piece.astype(BF16)

                @pl.when(a_is_key)
                def _():
                    finish(True)

                @pl.when(jnp.logical_not(a_is_key))
                def _():
                    finish(False)

    def half_backward(last, carried):
        start = 0 if last else half_parts
        ins = [whole(map_a), whole(map_b), whole(mask)]
        for array in (pre, px, y, cum, cum_t, head_rows, skip_rows):
            ins.append(chunked(array, start))
        ins.append(columns(conv_x, CH, lambda c, dev: chunk(c + start, dev)))
        ins += [chunked(core, start), chunked(d_core, start), whole(cols)]
        outs = [out_whole((R, CH), BF16) for _ in range(half_parts)] + [
            out_chunked((half_parts, R, CH), BF16),
            out_chunked((half_parts, R, 128), F32),
            out_chunked((half_parts, 8, CH), F32),
            out_chunked((half_parts, 8, 128), F32),
        ]
        square = pltpu.VMEM((S, T, T), F32)
        if last:
            ins.append(whole(carried))
            outs += [out_whole((R, NB), F32)]
            outs += [out_whole((R, NB), BF16) for _ in range(1, S)]
            scratch = [square, square, square]
        else:
            outs += [out_whole((S, T, T), F32)]
            scratch = [square, square]
        return run(
            partial(scan_backward, last),
            "scan_backward_near" if last else "scan_backward_far",
            device,
            ins,
            outs,
            half_parts,
            scratch=scratch,
            us=5.0,
        )

    far = half_backward(False, None)
    cotx_far = [exchange(far[r], "rep", half_parts + r) for r in range(half_parts)]
    near = half_backward(True, far[half_parts + 4])
    cotx_q = [near[0], exchange(near[1], "rep", 1)] + cotx_far
    halves = [near[half_parts : half_parts + 4], far[half_parts : half_parts + 4]]
    token = near[half_parts + 3]
    d_map_own = near[half_parts + 4]
    d_map_other = [exchange(near[half_parts + 4 + j], "shard", j) for j in range(1, S)]

    def input_backward(dev, cz, near_x, far_x, near_dt, far_dt, wz, wx, wdt, dn_r, dt_r):
        c = pl.program_id(0)

        @pl.when(c == 0)
        def _():
            joined = jnp.zeros((R, 128), F32)
            for i in range(PARTS):
                held = (near_dt, far_dt)[i // half_parts]
                joined = joined + from_part(held[i % half_parts], i, dev)
            joined = joined.astype(BF16)
            dt_r[...] = joined
            dn_r[...] = mm(joined[:, 0:H], wdt[...])

        @pl.when(c < half_parts)
        def _():
            dn_r[...] += mm_rt(cz[0], wz[...]) + mm_rt(near_x[0], wx[...])

        @pl.when(c >= half_parts)
        def _():
            dn_r[...] += mm_rt(cz[0], wz[...]) + mm_rt(far_x[0], wx[...])

    def half_spec(array, first):
        def at(c, dev):
            if first:
                return (jnp.minimum(c, half_parts - 1), 0, 0)
            return (jnp.maximum(c - half_parts, 0), 0, 0)

        return (array, pl.BlockSpec((1,) + array.shape[1:], at))

    d_normed, cot_dt_all = run(
        input_backward,
        "input_backward",
        device,
        [
            chunked(cotz),
            half_spec(halves[0][0], True),
            half_spec(halves[1][0], False),
            whole(halves[0][1]),
            whole(halves[1][1]),
            columns(w_z, CH, chunk),
            columns(w_x, CH, chunk),
            whole(wdt_t),
        ],
        [out_whole((R, D), F32), out_whole((R, 128), BF16)],
        PARTS,
        us=3.0,
    )

    small_half = -(-(NB + H + 15) // 32) * 16

    def maps_backward(
        dev, own, pre_r, pbc_r, cols_r, tbc, n_r, wbc, dn_r, cdt, cg0, cg1, hg0, hg1, gg, *refs
    ):
        others, hid, refs = refs[: S - 1], refs[S - 1 : 2 * S - 1], refs[2 * S - 1 :]
        kept, refs = refs[: S - 1], refs[S - 1 :]
        dn_own, pack_keep, pack_send = refs[0], refs[1], refs[2]
        sends = refs[3 : 2 + S]
        cot_s, dn_s, pack_r = refs[2 + S :]
        pack_r[...] = jnp.zeros_like(pack_r)
        grads = [jnp.zeros((1, NB), F32) for _ in range(5)]
        for b in range(S):
            d_map = own[blocks[b], :]
            for other in others:
                d_map = d_map + other[blocks[b], :].astype(F32)
            before = pre_r[blocks[b], :]
            sig = jax.nn.sigmoid(before)
            d_pre = d_map * sig * (1.0 + before * (1.0 - sig))
            d_in, taps, total = conv_back(d_pre, pbc_r[blocks[b], :], tbc[...], cols_r[blocks[b], :])
            for i, grad in enumerate(taps + [total]):
                grads[i] = grads[i] + grad
            cot_s[blocks[b], :] = d_in.astype(BF16)
        dn_s[...] = dn_r[...] + mm_rt(cot_s[...], wbc[...])
        dn_own[...] = dn_s[blocks[0], :]
        gain_sum = jnp.zeros((1, D), F32)
        for b in range(S):
            x = hid[b][...].astype(F32)
            scale = lax.rsqrt(jnp.mean(x * x, axis=1, keepdims=True) + epsilon)
            part = dn_s[blocks[b], :]
            gain_sum = gain_sum + jnp.sum(part * (x * scale), axis=0, keepdims=True)
            if b > 0:
                sends[b - 1][:, 0:D] = part.astype(BF16)
                sends[b - 1][:, D : 2 * D] = kept[b - 1][...]
        pack_r[0:NB, :] = mm_lt(cot_s[...], n_r[...])
        pack_r[NB : NB + H, :] = mm_lt(cdt[...], n_r[...])[0:H]
        at = NB + H
        heads = jnp.zeros((8, 128), F32)
        for i in range(PARTS):
            heads = heads + from_part((hg0, hg1)[i // half_parts][i % half_parts], i, dev)
        pack_r[at + 6 : at + 9, 0:128] = heads[0:3]
        mine = part_of(dev)
        for m in range(PARTS):

            @pl.when(mine == m)
            def _():
                for i in range(PARTS):
                    cg = (cg0, cg1)[i // half_parts]
                    lanes = slice((m ^ i) * CH, ((m ^ i) + 1) * CH)
                    pack_r[at : at + 5, lanes] = cg[i % half_parts, 0:5]
                    pack_r[at + 5 : at + 6, lanes] = gg[i, 0:1]

        for i in range(5):
            pack_r[at + 9 + i : at + 10 + i, 0:NB] = grads[i]
        pack_r[at + 14 : at + 15, :] = gain_sum
        core_at = lax.rem(mine, 2)
        keep_at = pl.multiple_of(core_at * small_half, 16)
        send_at = pl.multiple_of((1 - core_at) * small_half, 16)
        pack_keep[...] = pack_r[pl.ds(keep_at, small_half), :]
        pack_send[...] = pack_r[pl.ds(send_at, small_half), :].astype(BF16)

    outs = run(
        maps_backward,
        "maps_backward",
        device,
        [
            whole(a)
            for a in (
                d_map_own,
                pre_bc,
                proj_bc,
                cols,
                conv_bc,
                normed,
                w_bc,
                d_normed,
                cot_dt_all,
                halves[0][2],
                halves[1][2],
                halves[0][3],
                halves[1][3],
                gate_grads,
                *d_map_other,
                *hidden,
                *out_sends,
            )
        ],
        [
            out_whole((T, D), F32),
            out_whole((small_half, D), F32),
            out_whole((small_half, D), BF16),
        ]
        + [out_whole((T, 2 * D), BF16) for _ in range(1, S)],
        1,
        scratch=[
            pltpu.VMEM((R, NB), BF16),
            pltpu.VMEM((R, D), F32),
            pltpu.VMEM((2 * small_half, D), F32),
        ],
        us=3.0,
    )
    dn_own, pack, pack_send = outs[:3]
    dn_other = [exchange(outs[2 + j], "shard", j) for j in range(1, S)]

    def own_rows(dev, hid, cot, cols_r, rows_r, gain_r, dn_r, out_r, *refs):
        others, refs = refs[: S - 1], refs[S - 1 :]
        hidden_r, grad_r = refs
        used = cols_r[:, 0:1]
        x = hid[...].astype(F32)
        added = out_r[...]
        for other in others:
            added = added + other[:, D : 2 * D].astype(F32)
        hidden_r[...] = used * (x + rows_r[:, 0:1] * added)
        d_n = dn_r[...]
        for other in others:
            d_n = d_n + other[:, 0:D].astype(F32)
        scale = lax.rsqrt(jnp.mean(x * x, axis=1, keepdims=True) + epsilon)
        u = d_n * gain_r[...]
        dot = jnp.mean(u * x, axis=1, keepdims=True)
        grad_r[...] = used * cot[...].astype(F32) + scale * u - x * (scale * scale * scale * dot)

    hidden_out, grad_hidden = run(
        own_rows,
        "own_rows",
        device,
        [
            whole(hidden_in),
            whole(cotangent),
            (cols, pl.BlockSpec((T, 128), lambda *_: (0, 0))),
            (row_scale, pl.BlockSpec((T, 128), lambda *_: (0, 0))),
        ]
        + [whole(a) for a in (gain, dn_own, out_own, *dn_other)],
        [out_whole((T, D), F32), out_whole((T, D), F32)],
        1,
    )

    def split_specs(shape):
        half = spans // 2
        send = pl.BlockSpec((1,) + shape, lambda i, dev: (jnp.minimum(i, half - 1), 0, 0, 0))
        keep = pl.BlockSpec((1,) + shape, lambda i, dev: (jnp.maximum(i - half, 0), 0, 0, 0))
        return [
            (jax.ShapeDtypeStruct((half,) + shape, BF16), send),
            (jax.ShapeDtypeStruct((half,) + shape, F32), keep),
        ]

    def relative(i):
        half = spans // 2
        return jnp.where(i < half, 2 * i + 1, 2 * (i - half))

    def by_span(array, side):
        def at(i, dev):
            return (0, side * spans + (span_of(dev) ^ relative(i)))

        return (array, pl.BlockSpec((array.shape[0], DCH), at))

    def four(refs):
        ends = (slice(0, R), slice(R, 2 * R))
        return [refs[0][ends[0], :], refs[1][ends[0], :], refs[0][ends[1], :], refs[1][ends[1], :]]

    def store_split(value, slot, send_r, keep_r):
        i = pl.program_id(0)

        @pl.when(i < spans // 2)
        def _():
            send_r[0, slot] = value.astype(BF16)

        @pl.when(i >= spans // 2)
        def _():
            keep_r[0, slot] = value

    def pair_weight_grad(dev, *refs):
        both, norm, cot = refs[:PARTS], four(refs[PARTS:]), four(refs[PARTS + 2 :])
        value = jnp.zeros((CH, DCH), F32)
        other = jnp.zeros((CH, DCH), F32)
        for r in range(PARTS):
            value = value + mm_lt(both[r][:, 0:CH], cot[r])
            other = other + mm_lt(both[r][:, CH : 2 * CH], norm[r])
        store_split(value, 0, *refs[-2:])
        store_split(other, 1, *refs[-2:])

    def x_weight_grad(dev, *refs):
        value = jnp.zeros((CH, DCH), F32)
        norm = four(refs[PARTS:])
        for r in range(PARTS):
            value = value + mm_lt(refs[r][...], norm[r])
        store_split(value, 0, *refs[-2:])

    def sum_spans(send, keep):
        bit = PARTS
        total = keep + exchange(send, "rep", bit).astype(F32)
        while total.shape[0] > 1:
            bit *= 2
            send = total[1::2].astype(BF16)
            total = total[0::2] + exchange(send, "rep", bit).astype(F32)
        held = total.astype(BF16)
        while bit >= PARTS:
            held = jnp.concatenate([held, exchange(held, "rep", bit)], axis=0)
            bit //= 2
        far = exchange(held, "rep", 2)
        return [held, exchange(held, "rep", 1), far, exchange(far, "rep", 1)]

    def reversed_bits(i):
        result = jnp.int32(0) * i
        count = spans.bit_length() - 1
        for b in range(count):
            result = result | (((i >> b) & 1) << (count - 1 - b))
        return result

    def in_spec(name=None):
        def at(i, dev):
            return (span_of(dev) ^ reversed_bits(i), 0)

        return (jax.ShapeDtypeStruct((D, C), F32), pl.BlockSpec((DCH, C), at))

    def out_spec():
        def at(i, dev):
            return (0, span_of(dev) ^ reversed_bits(i))

        return (jax.ShapeDtypeStruct((C, D), F32), pl.BlockSpec((C, DCH), at))

    def join_pair(dev, *refs):
        mine = part_of(dev)
        for m in range(PARTS):

            @pl.when(mine == m)
            def _():
                for r in range(PARTS):
                    at = slice((m ^ r) * CH, ((m ^ r) + 1) * CH)
                    refs[PARTS][at, :] = refs[r][0, 0].astype(F32)
                    refs[PARTS + 1][:, at] = refs[r][0, 1].astype(F32).T
        refs[PARTS + 2][...] = jnp.zeros((8, 128), F32)

    def join_x(dev, *refs):
        mine = part_of(dev)
        for m in range(PARTS):

            @pl.when(mine == m)
            def _():
                for r in range(PARTS):
                    at = slice((m ^ r) * CH, ((m ^ r) + 1) * CH)
                    refs[PARTS + 1][:, at] = refs[r][0, 0].astype(F32).T

    send, keep = run(
        pair_weight_grad,
        "pair_weight_grad",
        device,
        [whole(b) for b in both_q]
        + [by_span(p, 0) for p in planes]
        + [by_span(p, 1) for p in planes]
        + [whole(token)],
        split_specs((2, CH, DCH)),
        spans,
        us=5.0,
    )
    pieces = sum_spans(send, keep)
    grad_out, grad_z, joined = run(
        join_pair,
        "join_pair",
        device,
        [chunked(p) for p in pieces],
        [out_spec(), in_spec(), out_whole((8, 128), F32)],
        spans,
        us=6.0,
    )
    send, keep = run(
        x_weight_grad,
        "x_weight_grad",
        device,
        [whole(c) for c in cotx_q] + [by_span(p, 0) for p in planes],
        split_specs((1, CH, DCH)),
        spans,
        us=2.5,
    )
    pieces = sum_spans(send, keep)
    (grad_x,) = run(
        join_x,
        "join_x",
        device,
        [chunked(p) for p in pieces] + [whole(joined)],
        [in_spec()],
        spans,
        us=4.0,
    )

    pack = pack + exchange(pack_send, "rep", 1).astype(F32)
    bit = 2
    while bit < replicas:
        rounded = pack.astype(BF16)
        pack = rounded.astype(F32) + exchange(rounded, "rep", bit).astype(F32)
        bit *= 2

    pack = pack.astype(BF16)
    pack_other = exchange(pack, "rep", 1)

    def unpack(dev, own, other, *refs):
        pack_r = refs[-1]
        core_at = lax.rem(part_of(dev), 2)
        own_at = pl.multiple_of(core_at * small_half, 16)
        other_at = pl.multiple_of((1 - core_at) * small_half, 16)
        pack_r[pl.ds(own_at, small_half), :] = own[...].astype(F32)
        pack_r[pl.ds(other_at, small_half), :] = other[...].astype(F32)
        at = NB + H
        refs[0][...] = pack_r[0:NB, :].T
        refs[1][...] = pack_r[NB:at, :]
        refs[2][...] = pack_r[at : at + 4, 0:C]
        refs[3][...] = pack_r[at + 9 : at + 13, 0:NB]
        refs[4][...] = pack_r[at + 4 : at + 5, 0:C]
        refs[5][...] = pack_r[at + 13 : at + 14, 0:NB]
        for i in range(3):
            refs[6 + i][...] = pack_r[at + 6 + i : at + 7 + i, 0:H]
        refs[9][...] = pack_r[at + 5 : at + 6, 0:C]
        me = me_of(dev)
        for m in range(S):

            @pl.when(me == m)
            def _():
                for j in range(S):
                    lanes = slice((m ^ j) * (D // S), ((m ^ j) + 1) * (D // S))
                    refs[10 + j][...] = pack_r[at + 14 : at + 15, lanes]

    outs = run(
        unpack,
        "unpack",
        device,
        [whole(pack), whole(pack_other)],
        [
            out_whole(shape, F32)
            for shape in [(D, NB), (H, D), (4, C), (4, NB), (1, C), (1, NB)]
            + [(1, H)] * 3
            + [(1, C)]
            + [(1, D // S)] * S
        ],
        1,
        scratch=[pltpu.VMEM((2 * small_half, D), F32)],
        us=1.5,
    )
    grad_bc, grad_dt, grad_conv_x, grad_conv_bc, grad_bias_x, grad_bias_bc = outs[:6]
    heads, grad_gate = outs[6:9], outs[9]
    grad_gain = outs[10]
    for j in range(1, S):
        grad_gain = grad_gain + exchange(outs[10 + j], "shard", j)
    return (
        hidden_out,
        grad_hidden,
        grad_gain,
        grad_z[None],
        grad_x[None],
        grad_bc[None],
        grad_dt.T[None],
        grad_conv_x[None],
        grad_conv_bc[None],
        grad_bias_x,
        grad_bias_bc,
        *heads,
        grad_gate,
        grad_out[None],
    )
```

```python
from functools import partial

import jax
import jax.numpy as jnp
import numpy as np
from jax import lax
from jax.experimental import pallas as pl
from jax.experimental.pallas import tpu as pltpu
from jax.sharding import PartitionSpec as P

epsilon = 1e-05
PARTS = 4
F32 = jnp.float32
BF16 = jnp.bfloat16
VM = 1.5
UNIT = 1.1e9


def exchange(array, axis, bit):
    count = lax.axis_size(axis)
    return lax.ppermute(array, axis, [(i, i ^ bit) for i in range(count)])


def mm(left, right):
    return lax.dot_general(left, right, (((1,), (0,)), ((), ())), preferred_element_type=F32)


def mm_rt(left, right):
    return lax.dot_general(left, right, (((1,), (1,)), ((), ())), preferred_element_type=F32)


def mm_lt(left, right):
    return lax.dot_general(left, right, (((0,), (0,)), ((), ())), preferred_element_type=F32)


def whole(array):
    zeros = (0,) * array.ndim
    return (array, pl.BlockSpec(array.shape, lambda *_: zeros))


def chunked(array, start=0):
    tail = (0,) * (array.ndim - 1)
    return (array, pl.BlockSpec((1,) + array.shape[1:], lambda c, dev: (c + start,) + tail))


def columns(array, width, at):
    if width % 128 == 0:
        return (array, pl.BlockSpec((array.shape[0], width), lambda c, dev: (0, at(c, dev))))
    pieces = array.reshape(array.shape[0], -1, width).transpose(1, 0, 2)
    spec = pl.BlockSpec((None, array.shape[0], width), lambda c, dev: (at(c, dev), 0, 0))
    return (pieces, spec)


def rows(array, height, at):
    return (array, pl.BlockSpec((height, array.shape[1]), lambda c, dev: (at(c, dev), 0)))


def split(value):
    high = value.astype(BF16)
    return high, (value - high.astype(F32)).astype(BF16)


def spread(value, pattern):
    high, low = split(value)
    return mm(high, pattern) + mm(low, pattern)


def out_whole(shape, dtype):
    zeros = (0,) * len(shape)
    return (jax.ShapeDtypeStruct(shape, dtype), pl.BlockSpec(shape, lambda *_: zeros))


def out_chunked(shape, dtype):
    tail = (0,) * (len(shape) - 1)
    spec = pl.BlockSpec((1,) + shape[1:], lambda c, dev: (c,) + tail)
    return (jax.ShapeDtypeStruct(shape, dtype), spec)


def run(body, name, device, ins, outs, steps, scratch=(), us=1.0, after=None):
    ins, outs = list(ins), list(outs)
    count, made = len(ins), len(outs)
    if after is not None:
        ins.append(whole(after))
    outs.append(out_whole((8, 128), F32))
    skip = len(ins)

    def ordered(dev, *refs):
        refs[skip + made][...] = jnp.zeros((8, 128), F32)
        body(dev, *refs[:count], *refs[skip : skip + made], *refs[skip + made + 1 :])

    total = sum(a.size * a.dtype.itemsize for a, _ in ins)
    total += sum(s.size * s.dtype.itemsize for s, _ in outs)
    held = 0
    for array, spec in list(ins) + list(outs):
        size = array.dtype.itemsize
        for extent in spec.block_shape:
            size *= extent or 1
        held += size * (1 if size == array.size * array.dtype.itemsize else 2)
    for buffer in scratch:
        held += buffer.dtype.itemsize * int(np.prod(buffer.shape))
    return pl.pallas_call(
        ordered,
        name=name,
        out_shape=[shape for shape, _ in outs],
        grid_spec=pltpu.PrefetchScalarGridSpec(
            num_scalar_prefetch=1,
            grid=(steps,),
            in_specs=[spec for _, spec in ins],
            out_specs=[spec for _, spec in outs],
            scratch_shapes=list(scratch),
        ),
        compiler_params=pltpu.CompilerParams(
            dimension_semantics=("arbitrary",),
            vmem_limit_bytes=int(held * VM) + (3 << 20),
        ),
        cost_estimate=pl.CostEstimate(
            flops=int(us * UNIT), bytes_accessed=total, transcendentals=0
        ),
    )(device, *[a for a, _ in ins])


def iota(shape, dim):
    return lax.broadcasted_iota(jnp.int32, shape, dim)


def roll_rows(array, shift):
    if array.shape[1] % 128 == 0:
        return pltpu.roll(array, shift % array.shape[0], 0)
    return jnp.roll(array, shift, 0)


def conv_rows(inputs, taps, bias, marks):
    result = bias + taps[3:4] * inputs
    for offset in range(1, 4):
        shifted = roll_rows(inputs, offset) * marks[:, offset : offset + 1]
        result = result + taps[3 - offset : 4 - offset] * shifted
    return result


def conv_back(d_out, inputs, taps, marks):
    d_in = taps[3:4] * d_out
    grads = [None] * 4
    grads[3] = jnp.sum(d_out * inputs, axis=0, keepdims=True)
    for offset in range(1, 4):
        kept = d_out * marks[:, offset : offset + 1]
        d_in = d_in + taps[3 - offset : 4 - offset] * roll_rows(kept, -offset)
        grads[3 - offset] = jnp.sum(kept * roll_rows(inputs, offset), axis=0, keepdims=True)
    return d_in, grads, jnp.sum(d_out, axis=0, keepdims=True)


def softplus(value):
    return jnp.maximum(value, 0.0) + jnp.log1p(jnp.exp(-jnp.abs(value)))


def solution(mesh):
    members = mesh.shape["shard"]
    replicas = mesh.shape["rep"]
    assert replicas % PARTS == 0 and replicas // PARTS >= 2
    assert replicas & (replicas - 1) == 0 and members & (members - 1) == 0
    return jax.shard_map(
        partial(on_device, members, replicas),
        mesh=mesh,
        in_specs=(
            P(("rep", "shard"), None),
            P(("rep", "shard"), None),
            P(None, "shard"),
            P(None, None, "shard"),
            P(None, None, "shard"),
            P(None, None, "shard"),
            P(None, None, "shard"),
            P(None, None, "shard"),
            P(None, None, "shard"),
            P(None, "shard"),
            P(None, "shard"),
            P(None, "shard"),
            P(None, "shard"),
            P(None, "shard"),
            P(None, "shard"),
            P(None, "shard", None),
            P(),
            P(),
            P(),
        ),
        out_specs=(
            P(("rep", "shard"), None),
            P(("rep", "shard"), None),
            P(None, "shard"),
            P(None, None, "shard"),
            P(None, None, "shard"),
            P(None, None, "shard"),
            P(None, None, "shard"),
            P(None, None, "shard"),
            P(None, None, "shard"),
            P(None, "shard"),
            P(None, "shard"),
            P(None, "shard"),
            P(None, "shard"),
            P(None, "shard"),
            P(None, "shard"),
            P(None, "shard", None),
        ),
        check_vma=False,
    )


def on_device(
    members,
    replicas,
    hidden_in,
    cotangent,
    norm_gain,
    w_z,
    w_x,
    w_bc,
    w_dt,
    conv_x,
    conv_bc,
    bias_x,
    bias_bc,
    dt_bias,
    a_log,
    d_skip,
    gate_gain,
    w_out,
    seq_len,
    seq_owner,
    seq_start,
):
    S = members
    T, D = hidden_in.shape
    R = S * T
    C = w_z.shape[2]
    H = w_dt.shape[2]
    NB = w_bc.shape[2]
    CH = C // PARTS
    HC = H // PARTS
    HS = C // H
    inner = C * S
    spans = replicas // PARTS
    DCH = D // spans
    w_z, w_x, w_bc, w_dt, w_out = w_z[0], w_x[0], w_bc[0], w_dt[0], w_out[0]

    shard_at = lax.axis_index("shard")
    device = (lax.axis_index("rep") * S + shard_at).astype(jnp.int32).reshape(1)

    def me_of(dev):
        return lax.rem(dev[0], S)

    def part_of(dev):
        return lax.rem(lax.div(dev[0], S), PARTS)

    def span_of(dev):
        return lax.div(dev[0], S * PARTS)

    tokens = {}

    def launch(body, name, *rest, after=None, **options):
        *results, tokens[name] = run(
            body, name, *rest, after=tokens.get(after), **options
        )
        return results

    blocks = [slice(b * T, (b + 1) * T) for b in range(S)]

    hidden = [hidden_in] + [exchange(hidden_in, "shard", j) for j in range(1, S)]

    lens = seq_len.reshape(1, -1)
    owners = seq_owner.reshape(1, -1)
    starts = seq_start.reshape(1, -1)
    records = lens.shape[1]
    wdt_t = w_dt.T
    conv_x, conv_bc = conv_x[0], conv_bc[0]

    def chunk(c, dev):
        return part_of(dev) ^ c

    def to_part(value, c, dev):
        return pltpu.roll(value, lax.rem(128 - chunk(c, dev) * HC, 128), 1)

    def from_part(value, c, dev):
        return pltpu.roll(value, chunk(c, dev) * HC, 1)

    def head_pattern():
        return jnp.where(iota((128, CH), 0) == iota((128, CH), 1) // HS, 1.0, 0.0).astype(BF16)

    def head_pattern_t():
        return jnp.where(iota((CH, 128), 0) // HS == iota((CH, 128), 1), 1.0, 0.0).astype(BF16)

    def pad_lanes(value):
        gap = jnp.zeros((value.shape[0], 128 - value.shape[1]), F32)
        return jnp.concatenate([value, gap], axis=1)

    group = min(2, HC)
    width = group * HS

    def head_masks():
        lane = iota((1, width), 1) // HS
        return [jnp.where(lane == g, 1.0, 0.0) for g in range(group)]

    def segments(dev, ln, ow, st, cot, *refs):
        given, refs = refs[:4], refs[4:]
        mask_r, cols_r, cot_r = refs[:3]
        for source, target in zip(given, refs[3:]):
            target[...] = source[...]
        cot_r[...] = cot[...]
        me = me_of(dev)
        base = dev[0] - me
        lane = iota((T, 128), 1)
        row = iota((T, 128), 0)
        slot = iota((T, records), 0)
        ids = iota((T, records), 1).astype(F32)
        for b in range(S):
            covers = (
                (ow[...] == base + (me ^ b)) & (slot >= st[...]) & (slot < st[...] + ln[...])
            )
            used = jnp.sum(jnp.where(covers, 1.0, 0.0), axis=1, keepdims=True)
            found = jnp.sum(jnp.where(covers, ids, 0.0), axis=1, keepdims=True)
            lone = (records + row).astype(F32)
            seg = jnp.where(used > 0.5, found, lone)
            same = (seg == seg.T) & (row >= lane)
            mask_r[blocks[b], :] = jnp.where(same, 1.0, 0.0)
            cols = jnp.where(lane == 0, used, 0.0)
            for offset in range(1, 4):
                mark = (pltpu.roll(seg, offset, 0) == seg) & (row >= offset)
                cols = jnp.where(lane == offset, jnp.where(mark, 1.0, 0.0), cols)
            cols_r[blocks[b], :] = cols

    mask, cols, cot_own, own_gain, bc_weight, bc_taps, bc_bias = launch(
        segments,
        "segments",
        device,
        [
            whole(a)
            for a in (
                lens,
                owners,
                starts,
                cotangent,
                norm_gain,
                w_bc,
                conv_bc,
                bias_bc,
            )
        ],
        [
            out_whole((R, 128), F32),
            out_whole((R, 128), F32),
            out_whole((T, D), BF16),
            out_whole(norm_gain.shape, F32),
            out_whole(w_bc.shape, BF16),
            out_whole(conv_bc.shape, F32),
            out_whole(bias_bc.shape, F32),
        ],
        1,
        us=1.5,
    )
    if S == 2:
        gains = [own_gain, exchange(norm_gain, "shard", 1)]
    else:
        gains = [lax.all_gather(own_gain, "shard", axis=1, tiled=True)]

    def prepare(dev, wbc, tbc, bbc, cols_r, cot, *refs):
        parts, refs = refs[: len(gains)], refs[len(gains) :]
        hid, refs = refs[:S], refs[S:]
        gain_r, normed_r, pbc_r, pre_r, map_r, cot_r, mine_r = refs[:7]
        sends = refs[7:]
        me = me_of(dev)
        if S == 2:
            low, high = parts[0][...], parts[1][...]
            first = me == 0
            gain_r[...] = jnp.concatenate(
                [jnp.where(first, low, high), jnp.where(first, high, low)], axis=1
            )
        else:
            gain_r[...] = parts[0][...]
        for b in range(S):
            x = hid[b][...].astype(F32)
            scale = lax.rsqrt(jnp.mean(x * x, axis=1, keepdims=True) + epsilon)
            normed_r[blocks[b], :] = (x * scale * gain_r[...]).astype(BF16)
        pbc_r[...] = mm(normed_r[...], wbc[...])
        for b in range(S):
            marks = cols_r[blocks[b], :]
            pre = conv_rows(pbc_r[blocks[b], :], tbc[...], bbc[...], marks)
            pre_r[blocks[b], :] = pre
            out = (pre * jax.nn.sigmoid(pre)).astype(BF16)
            map_r[blocks[b], :] = out
            for j in range(1, S):
                sends[j - 1][blocks[b ^ j], :] = out
        cot_r[...] = cot[...]
        mine_r[:, 0:D] = normed_r[blocks[0], :]
        mine_r[:, D : 2 * D] = cot[...]

    outs = launch(
        prepare,
        "norm_and_maps",
        device,
        [whole(a) for a in (bc_weight, bc_taps, bc_bias, cols, cot_own, *gains, *hidden)],
        [
            out_whole((1, D), F32),
            out_whole((R, D), BF16),
            out_whole((R, NB), F32),
            out_whole((R, NB), F32),
            out_whole((R, NB), BF16),
            out_whole((T, D), BF16),
            out_whole((T, 2 * D), BF16),
        ]
        + [out_whole((R, NB), BF16) for _ in range(1, S)],
        1,
        us=1.0,
    )
    gain, normed, proj_bc, pre_bc, map_own, cot_own, mine_rows = outs[:7]
    far_rows = [exchange(mine_rows, "rep", 2)]
    maps = [map_own] + [exchange(outs[6 + j], "shard", j) for j in range(1, S)]
    if S == 2:
        map_a, map_b = maps
    else:
        map_a = jnp.concatenate(maps[: S // 2], axis=1)
        map_b = jnp.concatenate(maps[S // 2 :], axis=1)
    cots = [cot_own] + [exchange(cot_own, "shard", j) for j in range(1, S)]

    def project(dev, n_r, wz, wx, wdt, dtb, alog, dsk, tx, bx, cols_r, *refs):
        z_r, x_r, pre_r, y_r, cum_r, cumt_r, hp_r, sk_r = refs[:8]
        y_s, cum_s = refs[8:]
        c = pl.program_id(0)
        n = n_r[...]

        @pl.when(c == 0)
        def _():
            y_s[...] = pad_lanes(mm_rt(n, wdt[...]) + dtb[...])
            row = iota((T, 128), 0)
            rate = jnp.exp(pad_lanes(alog[...]))
            for b in range(S):
                total = -softplus(y_s[blocks[b], :]) * rate
                shift = 1
                while shift < T:
                    total = total + jnp.where(row >= shift, pltpu.roll(total, shift, 0), 0.0)
                    shift *= 2
                cum_s[blocks[b], :] = total

        z_r[0] = mm(n, wz[...])
        x_r[0] = mm(n, wx[...])
        y_r[0] = to_part(y_s[...], c, dev)
        turned = to_part(cum_s[...], c, dev)
        cum_r[0] = turned
        pair = jnp.concatenate(
            [pad_lanes(alog[...]), pad_lanes(dsk[...]), jnp.zeros((6, 128), F32)], axis=0
        )
        pair = to_part(pair, c, dev)
        hp_r[0] = jnp.exp(pair)
        skips = [jnp.broadcast_to(pair[1:2, h : h + 1], (1, HS)) for h in range(HC)]
        sk_r[0] = jnp.broadcast_to(jnp.concatenate(skips, axis=1), (8, CH))
        for b in range(S):
            marks = cols_r[blocks[b], :]
            pre_r[0, blocks[b], :] = conv_rows(x_r[0, blocks[b], :], tx[...], bx[...], marks)
            cumt_r[0, b] = turned[blocks[b]].T[0:8]

    z, px, pre, y, cum, cum_t, head_rows, skip_rows = launch(
        project,
        "projections",
        device,
        [
            whole(normed),
            columns(w_z, CH, chunk),
            columns(w_x, CH, chunk),
            whole(wdt_t),
            whole(dt_bias),
            whole(a_log),
            whole(d_skip),
            columns(conv_x, CH, chunk),
            columns(bias_x, CH, chunk),
            whole(cols),
        ],
        [
            out_chunked((PARTS, R, CH), F32),
            out_chunked((PARTS, R, CH), F32),
            out_chunked((PARTS, R, CH), F32),
            out_chunked((PARTS, R, 128), F32),
            out_chunked((PARTS, R, 128), F32),
            out_chunked((PARTS, S, 8, 128), F32),
            out_chunked((PARTS, 8, 128), F32),
            out_chunked((PARTS, 8, CH), F32),
        ],
        PARTS,
        scratch=[pltpu.VMEM((R, 128), F32), pltpu.VMEM((R, 128), F32)],
        us=4.0,
    )
    def fill_scores(dev, a_r, b_r, mask_r, scores):
        a_is_key = me_of(dev) < S // 2
        for b in range(S):

            @pl.when(a_is_key)
            def _():
                scores[b] = mm_rt(b_r[blocks[b], :], a_r[blocks[b], :]) * mask_r[blocks[b], :]

            @pl.when(jnp.logical_not(a_is_key))
            def _():
                scores[b] = mm_rt(a_r[blocks[b], :], b_r[blocks[b], :]) * mask_r[blocks[b], :]

    def scan_forward(
        dev, a_r, b_r, mask_r, pre_r, y_r, cum_r, cumt_r, sk, gg, z_r, wo, *refs
    ):
        core_r, sums, own_r = refs[0], refs[1], refs[2]
        sends = refs[3 : 2 + S]
        scores, acc, gated_s = refs[2 + S :]
        c = pl.program_id(0)

        @pl.when(c == 0)
        def _():
            fill_scores(dev, a_r, b_r, mask_r, scores)
            acc[...] = jnp.zeros_like(acc)
            sums[...] = jnp.zeros_like(sums)

        lane = iota((T, 128), 1)
        pattern = head_pattern()
        masks = head_masks()
        for b in range(S):
            before = pre_r[0, blocks[b], :]
            values = before * jax.nn.sigmoid(before)
            step = spread(softplus(y_r[0, blocks[b], :]), pattern)
            scaled = (values * step).astype(BF16)
            parts = []
            for first in range(0, HC, group):
                at = slice(first * HS, first * HS + width)
                weights = []
                for h in range(first, first + group):
                    gap = cum_r[0, blocks[b], h : h + 1] - cumt_r[0, b, h : h + 1, :]
                    weights.append(
                        (scores[b] * jnp.exp(jnp.minimum(gap, 0.0))).astype(BF16)
                    )
                stacked = [scaled[:, at] * m.astype(BF16) for m in masks]
                parts.append(
                    mm(jnp.concatenate(weights, axis=1), jnp.concatenate(stacked, axis=0))
                )
            core = jnp.concatenate(parts, axis=1) + values * sk[0, 0:1]
            core_r[0, blocks[b], :] = core
            zed = z_r[0, blocks[b], :]
            gated = core * (zed * jax.nn.sigmoid(zed))
            gained = gated * gg[...]
            gated_s[blocks[b], :] = gained.astype(BF16)
            squares = jnp.sum(gated * gated, axis=1, keepdims=True)
            sums[blocks[b], :] += jnp.where(lane == 0, squares, 0.0)
        acc[...] += mm(gated_s[...], wo[...])

        @pl.when(c == PARTS - 1)
        def _():
            own_r[...] = acc[blocks[0], :]
            for j in range(1, S):
                sends[j - 1][...] = acc[blocks[j], :].astype(BF16)

    outs = launch(
        scan_forward,
        "scan_forward",
        device,
        [
            whole(map_a),
            whole(map_b),
            whole(mask),
            chunked(pre),
            chunked(y),
            chunked(cum),
            chunked(cum_t),
            chunked(skip_rows),
            columns(gate_gain, CH, chunk),
            chunked(z),
            rows(w_out, CH, chunk),
        ],
        [
            out_chunked((PARTS, R, CH), F32),
            out_whole((R, 128), F32),
            out_whole((T, D), F32),
        ]
        + [out_whole((T, D), BF16) for _ in range(1, S)],
        PARTS,
        scratch=[
            pltpu.VMEM((S, T, T), F32),
            pltpu.VMEM((R, D), F32),
            pltpu.VMEM((R, CH), BF16),
        ],
        us=4.0,
    )
    core, squares, out_own = outs[:3]
    out_sends = outs[3:]

    def mixed_backward(dev, core_r, z_r, gg, cols_r, squares_r, wo, n_r, *refs):
        cot, refs = refs[:S], refs[S:]
        group_r, refs = refs[0], refs[1:]
        dm_r, sums_r = refs[0], refs[1]
        sends, sums = refs[2 : 1 + S], refs[1 + S]
        c = pl.program_id(0)
        lane = iota((T, 128), 1)

        @pl.when(c == 0)
        def _():
            sums[...] = squares_r[...]
            group_r[:, 0:D] = n_r[...]
            for b in range(S):
                group_r[blocks[b], D : 2 * D] = cot[b][...]

        for b in range(S):
            d_mixed = mm_rt(cot[b][...], wo[...]) * cols_r[blocks[b], 0:1]
            dm_r[0, blocks[b], :] = d_mixed
            zed = z_r[0, blocks[b], :]
            gated = core_r[0, blocks[b], :] * (zed * jax.nn.sigmoid(zed))
            dots = jnp.sum(d_mixed * (gated * gg[...]), axis=1, keepdims=True)
            sums[blocks[b], :] += jnp.where(lane == 1, dots, 0.0)

        @pl.when(c == PARTS - 1)
        def _():
            for b in range(S):
                turned = sums[blocks[b], :].T[0:8]
                sums_r[:, blocks[b]] = turned
                for j in range(1, S):
                    sends[j - 1][:, blocks[b ^ j]] = turned

    outs = launch(
        mixed_backward,
        "mixed_backward",
        device,
        [
            chunked(core),
            chunked(z),
            columns(gate_gain, CH, chunk),
            whole(cols),
            whole(squares),
            rows(w_out, CH, chunk),
            whole(normed),
        ]
        + [whole(c) for c in cots],
        [out_whole((R, 2 * D), BF16), out_chunked((PARTS, R, CH), F32), out_whole((8, R), F32)]
        + [out_whole((8, R), F32) for _ in range(1, S)],
        PARTS,
        scratch=[pltpu.VMEM((R, 128), F32)],
        us=1.6,
    )
    group_rows, d_mixed, sums_own = outs[:3]
    sums_all = [sums_own] + [exchange(outs[2 + j], "shard", j) for j in range(1, S)]
    group_other = exchange(group_rows, "rep", 1)

    def gate_backward(dev, core_r, z_r, dm_r, gg, cols_r, far_in, *refs):
        parts, refs = refs[:S], refs[S:]
        mixed_r, cotz_r = refs[:PARTS], refs[PARTS : 2 * PARTS]
        cotz_c, dcore_r, gg_r, rows_r, far_out = refs[2 * PARTS :]
        c = pl.program_id(0)
        lane = iota((T, 128), 1)

        @pl.when(c == 0)
        def _():
            far_out[...] = far_in[...]
            for b in range(S):
                total = parts[0][:, blocks[b]]
                for j in range(1, S):
                    total = total + parts[j][:, blocks[b]]
                turned = jnp.concatenate([total, jnp.zeros((T - 8, 128), F32)], axis=0).T
                inverse = lax.rsqrt(turned[:, 0:1] / inner + epsilon)
                factor = inverse * inverse * inverse * turned[:, 1:2] / inner
                rows_r[blocks[b], :] = jnp.where(
                    lane == 0, inverse, jnp.where(lane == 1, factor, 0.0)
                )

        gate_sum = jnp.zeros((1, CH), F32)
        mixed_parts, cot_parts = [], []
        for b in range(S):
            inverse = rows_r[blocks[b], 0:1]
            factor = rows_r[blocks[b], 1:2]
            used = cols_r[blocks[b], 0:1]
            core = core_r[0, blocks[b], :]
            zed = z_r[0, blocks[b], :]
            sig = jax.nn.sigmoid(zed)
            gated = core * (zed * sig)
            d_mixed = dm_r[0, blocks[b], :]
            scaled = gated * inverse
            gate_sum = gate_sum + jnp.sum(d_mixed * scaled, axis=0, keepdims=True)
            d_gated = inverse * (d_mixed * gg[...]) - gated * factor
            dcore_r[0, blocks[b], :] = (d_gated * (zed * sig)).astype(BF16)
            d_z = d_gated * core * sig * (1.0 + zed * (1.0 - sig))
            mixed_parts.append((scaled * gg[...] * used).astype(BF16))
            cot_parts.append(d_z.astype(BF16))
            cotz_c[0, blocks[b], :] = cot_parts[b]
        gg_r[0] = jnp.broadcast_to(gate_sum, (8, CH))
        for r in range(PARTS):

            @pl.when(c == r)
            def _():
                for b in range(S):
                    mixed_r[r][blocks[b], :] = mixed_parts[b]
                    cotz_r[r][blocks[b], :] = cot_parts[b]

    outs = launch(
        gate_backward,
        "gate_backward",
        device,
        [chunked(core), chunked(z), chunked(d_mixed), columns(gate_gain, CH, chunk), whole(cols), whole(far_rows[0])]
        + [whole(s) for s in sums_all],
        [out_whole((R, CH), BF16) for _ in range(2 * PARTS)]
        + [
            out_chunked((PARTS, R, CH), BF16),
            out_chunked((PARTS, R, CH), BF16),
            out_chunked((PARTS, 8, CH), F32),
            out_whole((R, 128), F32),
            out_whole((T, 2 * D), BF16),
        ],
        PARTS,
        us=2.2,
    )
    cotz, d_core, gate_grads, row_scale, far_own = outs[2 * PARTS :]
    mixed_q = [outs[0]] + [exchange(outs[r], "rep", r) for r in range(1, PARTS)]
    cotz_q = [outs[PARTS]] + [exchange(outs[PARTS + r], "rep", r) for r in range(1, PARTS)]

    far_rows = [far_own] + [exchange(far_own, "shard", j) for j in range(1, S)]

    half_parts = PARTS // 2

    def scan_backward(
        last, dev, a_r, b_r, mask_r, pre_r, px_r, y_r, cum_r, cumt_r, hp, sk, tx, core_r, dcore_r,
        cols_r, *refs
    ):
        if last:
            d_before, refs = refs[0], refs[1:]
        cotx_r, refs = refs[:half_parts], refs[half_parts:]
        cotx_c, cdt_r, cg_r, hg_r = refs[:4]
        if last:
            own_r, sends = refs[4], refs[5 : 4 + S]
            scores, scores_t, d_scores = refs[4 + S :]
        else:
            d_scores, scores, scores_t = refs[4:]
        c = pl.program_id(0)

        @pl.when(c == 0)
        def _():
            fill_scores(dev, a_r, b_r, mask_r, scores)
            for b in range(S):
                scores_t[b] = scores[b].T
            d_scores[...] = d_before[...] if last else jnp.zeros_like(d_scores)

        row = iota((T, 128), 0)
        lane = iota((T, 128), 1)
        pattern = head_pattern()
        pattern_t = head_pattern_t()
        masks = [m.astype(BF16) for m in head_masks()]
        tap_grads = [jnp.zeros((1, CH), F32) for _ in range(6)]
        bias_grad = jnp.zeros((1, 128), F32)
        rate_grad = jnp.zeros((1, 128), F32)
        cot_parts = []
        rate = hp[0, 0:1, :]
        for b in range(S):
            before = pre_r[0, blocks[b], :]
            sig = jax.nn.sigmoid(before)
            values = before * sig
            raw = y_r[0, blocks[b], :]
            step = softplus(raw)
            step_full = spread(step, pattern)
            scaled = (values * step_full).astype(BF16)
            d_out = dcore_r[0, blocks[b], :]
            d_scaled = []
            for first in range(0, HC, group):
                at = slice(first * HS, first * HS + width)
                stacked = jnp.concatenate([d_out[:, at] * m for m in masks], axis=0)
                d_weights = mm_rt(stacked, scaled[:, at])
                turned, change = [], None
                for g in range(group):
                    h = first + g
                    gap = cum_r[0, blocks[b], h : h + 1] - cumt_r[0, b, h : h + 1, :]
                    turned.append((scores_t[b] * jnp.exp(jnp.minimum(-gap, 0.0))).astype(BF16))
                    term = d_weights[g * T : (g + 1) * T] * jnp.exp(jnp.minimum(gap, 0.0))
                    change = term if change is None else change + term
                d_scores[b] += change
                d_scaled.append(mm(jnp.concatenate(turned, axis=1), stacked))
            d_scaled = jnp.concatenate(d_scaled, axis=1)
            d_out = d_out.astype(F32)
            plain = core_r[0, blocks[b], :] - values * sk[0, 0:1]
            d_cum = spread(d_out * plain - d_scaled * scaled.astype(F32), pattern_t)
            d_step = spread(d_scaled * values, pattern_t)
            shift = 1
            while shift < T:
                d_cum = d_cum + jnp.where(row < T - shift, pltpu.roll(d_cum, T - shift, 0), 0.0)
                shift *= 2
            rate_grad = rate_grad - jnp.sum(d_cum * step, axis=0, keepdims=True) * rate
            d_raw = (d_step - d_cum * rate) * jax.nn.sigmoid(raw)
            d_raw = jnp.where(lane < HC, d_raw, 0.0)
            bias_grad = bias_grad + jnp.sum(d_raw, axis=0, keepdims=True)
            cdt_r[0, blocks[b], :] = d_raw
            d_val = d_scaled * step_full + d_out * sk[0, 0:1]
            d_pre = d_val * sig * (1.0 + before * (1.0 - sig))
            d_in, grads, total = conv_back(
                d_pre, px_r[0, blocks[b], :], tx[...], cols_r[blocks[b], :]
            )
            skip = jnp.sum(d_out * values, axis=0, keepdims=True)
            for i, grad in enumerate(grads + [total, skip]):
                tap_grads[i] = tap_grads[i] + grad
            cot_parts.append(d_in.astype(BF16))
            cotx_c[0, blocks[b], :] = cot_parts[b]
        cg_r[0] = jnp.concatenate(tap_grads + [jnp.zeros((2, CH), F32)], axis=0)
        high, low = split(jnp.broadcast_to(tap_grads[5], (8, CH)))
        skip_grad = mm(high, pattern_t) + mm(low, pattern_t)
        hg_r[0] = jnp.concatenate(
            [bias_grad, rate_grad, skip_grad[0:1], jnp.zeros((5, 128), F32)], axis=0
        )
        for r in range(half_parts):

            @pl.when(c == r)
            def _():
                for b in range(S):
                    cotx_r[r][blocks[b], :] = cot_parts[b]

        if last:

            @pl.when(c == half_parts - 1)
            def _():
                a_is_key = me_of(dev) < S // 2

                def finish(key_first):
                    for b in range(S):
                        d_s = (d_scores[b] * mask_r[blocks[b], :]).astype(BF16)
                        a, bb = a_r[blocks[b], :], b_r[blocks[b], :]
                        if key_first:
                            both = (mm_lt(d_s, bb), mm(d_s, a))
                        else:
                            both = (mm(d_s, bb), mm_lt(d_s, a))
                        for j in range(S):
                            half = both[0] if j < S // 2 else both[1]
                            at = (j % (S // 2)) * NB
                            piece = half[:, at : at + NB]
                            if j == 0:
                                own_r[blocks[b], :] = piece
                            else:
                                sends[j - 1][blocks[b ^ j], :] = piece.astype(BF16)

                @pl.when(a_is_key)
                def _():
                    finish(True)

                @pl.when(jnp.logical_not(a_is_key))
                def _():
                    finish(False)

    def half_backward(last, carried):
        start = 0 if last else half_parts
        ins = [whole(map_a), whole(map_b), whole(mask)]
        for array in (pre, px, y, cum, cum_t, head_rows, skip_rows):
            ins.append(chunked(array, start))
        ins.append(columns(conv_x, CH, lambda c, dev: chunk(c + start, dev)))
        ins += [chunked(core, start), chunked(d_core, start), whole(cols)]
        outs = [out_whole((R, CH), BF16) for _ in range(half_parts)] + [
            out_chunked((half_parts, R, CH), BF16),
            out_chunked((half_parts, R, 128), F32),
            out_chunked((half_parts, 8, CH), F32),
            out_chunked((half_parts, 8, 128), F32),
        ]
        square = pltpu.VMEM((S, T, T), F32)
        if last:
            ins.append(whole(carried))
            outs += [out_whole((R, NB), F32)]
            outs += [out_whole((R, NB), BF16) for _ in range(1, S)]
            scratch = [square, square, square]
        else:
            outs += [out_whole((S, T, T), F32)]
            scratch = [square, square]
        return launch(
            partial(scan_backward, last),
            "scan_backward_near" if last else "scan_backward_far",
            device,
            ins,
            outs,
            half_parts,
            scratch=scratch,
            us=5.0,
            after="plane_rows" if last else "gate_backward",
        )

    far = half_backward(False, None)
    cotx_far = [exchange(far[r], "rep", half_parts + r) for r in range(half_parts)]
    def plane_rows(dev, *refs):
        for b in range(S):
            refs[S][blocks[b], :] = refs[b][...]

    (far_group,) = launch(
        plane_rows,
        "plane_rows",
        device,
        [whole(a) for a in far_rows],
        [out_whole((R, 2 * D), BF16)],
        1,
        us=0.5,
        after="scan_backward_far",
    )
    planes = [group_rows, group_other, far_group, exchange(far_group, "rep", 1)]

    near = half_backward(True, far[half_parts + 4])
    cotx_q = [near[0], exchange(near[1], "rep", 1)] + cotx_far
    halves = [near[half_parts : half_parts + 4], far[half_parts : half_parts + 4]]
    d_map_own = near[half_parts + 4]
    d_map_other = [exchange(near[half_parts + 4 + j], "shard", j) for j in range(1, S)]

    def split_specs(shape):
        half = spans // 2
        send = pl.BlockSpec((1,) + shape, lambda i, dev: (jnp.minimum(i, half - 1), 0, 0, 0))
        keep = pl.BlockSpec((1,) + shape, lambda i, dev: (jnp.maximum(i - half, 0), 0, 0, 0))
        return [
            (jax.ShapeDtypeStruct((half,) + shape, BF16), send),
            (jax.ShapeDtypeStruct((half,) + shape, F32), keep),
        ]

    def relative(i):
        half = spans // 2
        return jnp.where(i < half, 2 * i + 1, 2 * (i - half))

    def by_span(array, side):
        def at(i, dev):
            return (0, side * spans + (span_of(dev) ^ relative(i)))

        return (array, pl.BlockSpec((array.shape[0], DCH), at))

    def store_split(value, slot, send_r, keep_r):
        i = pl.program_id(0)

        @pl.when(i < spans // 2)
        def _():
            send_r[0, slot] = value.astype(BF16)

        @pl.when(i >= spans // 2)
        def _():
            keep_r[0, slot] = value

    def weight_grad(dev, *refs):
        value = jnp.zeros((CH, DCH), F32)
        for r in range(PARTS):
            value = value + mm_lt(refs[r][...], refs[PARTS + r][...])
        store_split(value, 0, *refs[2 * PARTS :])

    def add_stage(dev, total, recv, *refs):
        count = total.shape[0]
        for i in range(count):
            value = total[i] + recv[i].astype(F32)
            if count == 1:
                refs[0][0] = value.astype(BF16)
            elif i % 2 == 0:
                refs[0][i // 2] = value
            else:
                refs[1][i // 2] = value.astype(BF16)

    def join_stage(dev, held, recv, out_r):
        count = held.shape[0]
        out_r[0:count] = held[...]
        out_r[count : 2 * count] = recv[...]

    def sum_spans(label, send, total):
        bit, stage, held = PARTS, 0, None
        while held is None:
            recv = exchange(send, "rep", bit)
            after = yield label, stage, None
            shape = (max(total.shape[0] // 2, 1),) + total.shape[1:]
            more = total.shape[0] > 1
            outs = launch(
                add_stage,
                f"{label}_{stage}",
                device,
                [whole(total), whole(recv)],
                [out_whole(shape, F32), out_whole(shape, BF16)] if more else [out_whole(shape, BF16)],
                1,
                us=0.5,
                after=after,
            )
            stage += 1
            if more:
                total, send = outs
                bit *= 2
            else:
                held = outs[0]
        while bit >= PARTS:
            recv = exchange(held, "rep", bit)
            after = yield label, stage, None
            shape = (2 * held.shape[0],) + held.shape[1:]
            (held,) = launch(
                join_stage,
                f"{label}_{stage}",
                device,
                [whole(held), whole(recv)],
                [out_whole(shape, BF16)],
                1,
                us=0.5,
                after=after,
            )
            stage += 1
            bit //= 2
        far = exchange(held, "rep", 2)
        yield label, stage, [held, exchange(held, "rep", 1), far, exchange(far, "rep", 1)]

    def reversed_bits(i):
        result = jnp.int32(0) * i
        count = spans.bit_length() - 1
        for b in range(count):
            result = result | (((i >> b) & 1) << (count - 1 - b))
        return result

    def in_spec(name=None):
        def at(i, dev):
            return (span_of(dev) ^ reversed_bits(i), 0)

        return (jax.ShapeDtypeStruct((D, C), F32), pl.BlockSpec((DCH, C), at))

    def out_spec():
        def at(i, dev):
            return (0, span_of(dev) ^ reversed_bits(i))

        return (jax.ShapeDtypeStruct((C, D), F32), pl.BlockSpec((C, DCH), at))

    def join_out(dev, *refs):
        mine = part_of(dev)
        for m in range(PARTS):

            @pl.when(mine == m)
            def _():
                for r in range(PARTS):
                    at = slice((m ^ r) * CH, ((m ^ r) + 1) * CH)
                    refs[PARTS][at, :] = refs[r][0, 0].astype(F32)

    def join_x(dev, *refs):
        mine = part_of(dev)
        for m in range(PARTS):

            @pl.when(mine == m)
            def _():
                for r in range(PARTS):
                    at = slice((m ^ r) * CH, ((m ^ r) + 1) * CH)
                    refs[PARTS][:, at] = refs[r][0, 0].astype(F32).T

    send_out, keep_out = launch(
        weight_grad,
        "out_weight_grad",
        device,
        [whole(c) for c in mixed_q] + [by_span(p, 1) for p in planes],
        split_specs((1, CH, DCH)),
        spans,
        us=2.0,
        after="scan_backward_near",
    )
    chains = {"out": sum_spans("out", send_out, keep_out)}
    next(chains["out"])

    def input_backward(dev, cz, near_x, far_x, near_dt, far_dt, wz, wx, wdt, dn_r, dt_r):
        c = pl.program_id(0)

        @pl.when(c == 0)
        def _():
            joined = jnp.zeros((R, 128), F32)
            for i in range(PARTS):
                held = (near_dt, far_dt)[i // half_parts]
                joined = joined + from_part(held[i % half_parts], i, dev)
            joined = joined.astype(BF16)
            dt_r[...] = joined
            dn_r[...] = mm(joined[:, 0:H], wdt[...])

        @pl.when(c < half_parts)
        def _():
            dn_r[...] += mm_rt(cz[0], wz[...]) + mm_rt(near_x[0], wx[...])

        @pl.when(c >= half_parts)
        def _():
            dn_r[...] += mm_rt(cz[0], wz[...]) + mm_rt(far_x[0], wx[...])

    def half_spec(array, first):
        def at(c, dev):
            if first:
                return (jnp.minimum(c, half_parts - 1), 0, 0)
            return (jnp.maximum(c - half_parts, 0), 0, 0)

        return (array, pl.BlockSpec((1,) + array.shape[1:], at))

    d_normed, cot_dt_all = launch(
        input_backward,
        "input_backward",
        device,
        [
            chunked(cotz),
            half_spec(halves[0][0], True),
            half_spec(halves[1][0], False),
            whole(halves[0][1]),
            whole(halves[1][1]),
            columns(w_z, CH, chunk),
            columns(w_x, CH, chunk),
            whole(wdt_t),
        ],
        [out_whole((R, D), F32), out_whole((R, 128), BF16)],
        PARTS,
        us=3.0,
        after="out_weight_grad",
    )

    send_z, keep_z = launch(
        weight_grad,
        "z_weight_grad",
        device,
        [whole(c) for c in cotz_q] + [by_span(p, 0) for p in planes],
        split_specs((1, CH, DCH)),
        spans,
        us=2.0,
        after="input_backward",
    )
    chains["z"] = sum_spans("z", send_z, keep_z)
    next(chains["z"])

    small_half = -(-(NB + H + 15) // 32) * 16

    def maps_backward(
        dev, own, pre_r, pbc_r, cols_r, tbc, n_r, wbc, dn_r, cdt, cg0, cg1, hg0, hg1, gg, *refs
    ):
        others, hid, refs = refs[: S - 1], refs[S - 1 : 2 * S - 1], refs[2 * S - 1 :]
        kept, refs = refs[: S - 1], refs[S - 1 :]
        dn_own, pack_keep, pack_send = refs[0], refs[1], refs[2]
        sends = refs[3 : 2 + S]
        cot_s, dn_s, pack_r = refs[2 + S :]
        pack_r[...] = jnp.zeros_like(pack_r)
        grads = [jnp.zeros((1, NB), F32) for _ in range(5)]
        for b in range(S):
            d_map = own[blocks[b], :]
            for other in others:
                d_map = d_map + other[blocks[b], :].astype(F32)
            before = pre_r[blocks[b], :]
            sig = jax.nn.sigmoid(before)
            d_pre = d_map * sig * (1.0 + before * (1.0 - sig))
            d_in, taps, total = conv_back(d_pre, pbc_r[blocks[b], :], tbc[...], cols_r[blocks[b], :])
            for i, grad in enumerate(taps + [total]):
                grads[i] = grads[i] + grad
            cot_s[blocks[b], :] = d_in.astype(BF16)
        dn_s[...] = dn_r[...] + mm_rt(cot_s[...], wbc[...])
        dn_own[...] = dn_s[blocks[0], :]
        gain_sum = jnp.zeros((1, D), F32)
        for b in range(S):
            x = hid[b][...].astype(F32)
            scale = lax.rsqrt(jnp.mean(x * x, axis=1, keepdims=True) + epsilon)
            part = dn_s[blocks[b], :]
            gain_sum = gain_sum + jnp.sum(part * (x * scale), axis=0, keepdims=True)
            if b > 0:
                sends[b - 1][:, 0:D] = part.astype(BF16)
                sends[b - 1][:, D : 2 * D] = kept[b - 1][...]
        pack_r[0:NB, :] = mm_lt(cot_s[...], n_r[...])
        pack_r[NB : NB + H, :] = mm_lt(cdt[...], n_r[...])[0:H]
        at = NB + H
        heads = jnp.zeros((8, 128), F32)
        for i in range(PARTS):
            heads = heads + from_part((hg0, hg1)[i // half_parts][i % half_parts], i, dev)
        pack_r[at + 6 : at + 9, 0:128] = heads[0:3]
        mine = part_of(dev)
        for m in range(PARTS):

            @pl.when(mine == m)
            def _():
                for i in range(PARTS):
                    cg = (cg0, cg1)[i // half_parts]
                    lanes = slice((m ^ i) * CH, ((m ^ i) + 1) * CH)
                    pack_r[at : at + 5, lanes] = cg[i % half_parts, 0:5]
                    pack_r[at + 5 : at + 6, lanes] = gg[i, 0:1]

        for i in range(5):
            pack_r[at + 9 + i : at + 10 + i, 0:NB] = grads[i]
        pack_r[at + 14 : at + 15, :] = gain_sum
        core_at = lax.rem(mine, 2)
        keep_at = pl.multiple_of(core_at * small_half, 16)
        send_at = pl.multiple_of((1 - core_at) * small_half, 16)
        pack_keep[...] = pack_r[pl.ds(keep_at, small_half), :]
        pack_send[...] = pack_r[pl.ds(send_at, small_half), :].astype(BF16)

    outs = launch(
        maps_backward,
        "maps_backward",
        device,
        [
            whole(a)
            for a in (
                d_map_own,
                pre_bc,
                proj_bc,
                cols,
                conv_bc,
                normed,
                w_bc,
                d_normed,
                cot_dt_all,
                halves[0][2],
                halves[1][2],
                halves[0][3],
                halves[1][3],
                gate_grads,
                *d_map_other,
                *hidden,
                *out_sends,
            )
        ],
        [
            out_whole((T, D), F32),
            out_whole((small_half, D), F32),
            out_whole((small_half, D), BF16),
        ]
        + [out_whole((T, 2 * D), BF16) for _ in range(1, S)],
        1,
        scratch=[
            pltpu.VMEM((R, NB), BF16),
            pltpu.VMEM((R, D), F32),
            pltpu.VMEM((2 * small_half, D), F32),
        ],
        us=3.0,
        after="z_weight_grad",
    )
    dn_own, pack, pack_send = outs[:3]
    dn_other = [exchange(outs[2 + j], "shard", j) for j in range(1, S)]

    chains["out"].send("maps_backward")
    send_x, keep_x = launch(
        weight_grad,
        "x_weight_grad",
        device,
        [whole(c) for c in cotx_q] + [by_span(p, 0) for p in planes],
        split_specs((1, CH, DCH)),
        spans,
        us=2.0,
        after="out_0",
    )
    chains["x"] = sum_spans("x", send_x, keep_x)
    next(chains["x"])
    stages = 2 * (spans.bit_length() - 1)
    turns = [(3 * k, "out") for k in range(1, stages)]
    turns += [(3 * k + 2, "z") for k in range(stages)]
    turns += [(3 * k + 4, "x") for k in range(stages)]
    pieces, last = {}, "x_weight_grad"
    for _, label in sorted(turns):
        _, stage, pieces[label] = chains[label].send(last)
        last = f"{label}_{stage - 1}"

    def own_rows(dev, hid, cot, cols_r, rows_r, gain_r, dn_r, out_r, *refs):
        others, refs = refs[: S - 1], refs[S - 1 :]
        hidden_r, grad_r = refs
        used = cols_r[:, 0:1]
        x = hid[...].astype(F32)
        added = out_r[...]
        for other in others:
            added = added + other[:, D : 2 * D].astype(F32)
        hidden_r[...] = used * (x + rows_r[:, 0:1] * added)
        d_n = dn_r[...]
        for other in others:
            d_n = d_n + other[:, 0:D].astype(F32)
        scale = lax.rsqrt(jnp.mean(x * x, axis=1, keepdims=True) + epsilon)
        u = d_n * gain_r[...]
        dot = jnp.mean(u * x, axis=1, keepdims=True)
        grad_r[...] = used * cot[...].astype(F32) + scale * u - x * (scale * scale * scale * dot)

    hidden_out, grad_hidden = launch(
        own_rows,
        "own_rows",
        device,
        [
            whole(hidden_in),
            whole(cotangent),
            (cols, pl.BlockSpec((T, 128), lambda *_: (0, 0))),
            (row_scale, pl.BlockSpec((T, 128), lambda *_: (0, 0))),
        ]
        + [whole(a) for a in (gain, dn_own, out_own, *dn_other)],
        [out_whole((T, D), F32), out_whole((T, D), F32)],
        1,
        after="maps_backward",
    )

    (grad_out,) = launch(
        join_out,
        "join_out",
        device,
        [chunked(p) for p in pieces["out"]],
        [out_spec()],
        spans,
        us=4.0,
        after=last,
    )
    (grad_z,) = launch(
        join_x,
        "join_z",
        device,
        [chunked(p) for p in pieces["z"]],
        [in_spec()],
        spans,
        us=4.0,
        after="join_out",
    )
    (grad_x,) = launch(
        join_x,
        "join_x",
        device,
        [chunked(p) for p in pieces["x"]],
        [in_spec()],
        spans,
        us=4.0,
        after="join_z",
    )

    pack = pack + exchange(pack_send, "rep", 1).astype(F32)
    bit = 2
    while bit < replicas:
        rounded = pack.astype(BF16)
        pack = rounded.astype(F32) + exchange(rounded, "rep", bit).astype(F32)
        bit *= 2

    pack = pack.astype(BF16)
    pack_other = exchange(pack, "rep", 1)

    def unpack(dev, own, other, *refs):
        pack_r = refs[-1]
        core_at = lax.rem(part_of(dev), 2)
        own_at = pl.multiple_of(core_at * small_half, 16)
        other_at = pl.multiple_of((1 - core_at) * small_half, 16)
        pack_r[pl.ds(own_at, small_half), :] = own[...].astype(F32)
        pack_r[pl.ds(other_at, small_half), :] = other[...].astype(F32)
        at = NB + H
        refs[0][...] = pack_r[0:NB, :].T
        refs[1][...] = pack_r[NB:at, :]
        refs[2][...] = pack_r[at : at + 4, 0:C]
        refs[3][...] = pack_r[at + 9 : at + 13, 0:NB]
        refs[4][...] = pack_r[at + 4 : at + 5, 0:C]
        refs[5][...] = pack_r[at + 13 : at + 14, 0:NB]
        for i in range(3):
            refs[6 + i][...] = pack_r[at + 6 + i : at + 7 + i, 0:H]
        refs[9][...] = pack_r[at + 5 : at + 6, 0:C]
        me = me_of(dev)
        for m in range(S):

            @pl.when(me == m)
            def _():
                for j in range(S):
                    lanes = slice((m ^ j) * (D // S), ((m ^ j) + 1) * (D // S))
                    refs[10 + j][...] = pack_r[at + 14 : at + 15, lanes]

    outs = launch(
        unpack,
        "unpack",
        device,
        [whole(pack), whole(pack_other)],
        [
            out_whole(shape, F32)
            for shape in [(D, NB), (H, D), (4, C), (4, NB), (1, C), (1, NB)]
            + [(1, H)] * 3
            + [(1, C)]
            + [(1, D // S)] * S
        ],
        1,
        scratch=[pltpu.VMEM((2 * small_half, D), F32)],
        us=1.5,
    )
    grad_bc, grad_dt, grad_conv_x, grad_conv_bc, grad_bias_x, grad_bias_bc = outs[:6]
    heads, grad_gate = outs[6:9], outs[9]
    grad_gain = outs[10]
    for j in range(1, S):
        grad_gain = grad_gain + exchange(outs[10 + j], "shard", j)
    return (
        hidden_out,
        grad_hidden,
        grad_gain,
        grad_z[None],
        grad_x[None],
        grad_bc[None],
        grad_dt.T[None],
        grad_conv_x[None],
        grad_conv_bc[None],
        grad_bias_x,
        grad_bias_bc,
        *heads,
        grad_gate,
        grad_out[None],
    )
```
